32 devices in a mesh: groups: 2 (over y), seq: 4 (over z), segment: 2 (over x), cfg: 2 (over core).
Axes of the slice: x: 2, y: 2, z: 4, core: 2. Of those that a mesh axis runs over, the one named last changes fastest.
Arguments:
- latent: float32 [2, 64, 64], P(None, ('groups', 'seq')), parts along dimension 1, may hold values from -0.1 to 0.1
- w_embed: bfloat16 [64, 3072], replicated, may hold values from -0.75 to 0.75
- w_qkv: bfloat16 [2, 9216, 3072], P('segment', 'seq'), may hold values from -0.109375 to 0.109375
- w_out: bfloat16 [2, 3072, 3072], P('segment', 'seq'), may hold values from -0.109375 to 0.109375
- mod_table: bfloat16 [50, 3, 3072], replicated, may hold values from -3 to 3
- cond_mod: float32 [2, 4, 3, 3072], P('cfg', ('groups', 'segment')), parts along dimension 1, may hold values from -3 to 3
- stale_kv: bfloat16 [2, 2, 4, 2, 64, 1536], P('segment', 'cfg', 'seq', None, 'groups'), parts along dimension 4, may hold values from -6 to 6
- w_final: bfloat16 [3072, 64], replicated, may hold values from -0.109375 to 0.109375
- w_conv: bfloat16 [27, 16, 512], P(None, None, ('segment', 'cfg')), may hold values from -0.3125 to 0.3125
- patch_order: int32 [4], P('groups'), parts along dimension 0, may hold values from 0 to 1, each once
- timestep: int32 [2], P('groups'), parts along dimension 0, may hold values from 0 to 49
- slab_rows: int32 [8], P('groups'), parts along dimension 0, may hold values from 1 to 4, 8 in all
Outputs:
- velocity: float32 [2, 64, 64], P(None, ('groups', 'seq')), parts along dimension 1
- decoded: bfloat16 [8, 4, 4, 8, 512], P(('groups', 'seq'), None, None, None, ('segment', 'cfg')), parts along dimension 0
The draws below stay inside these ranges and needn't reach their ends.
There are 2 independent parts, one for each index of `groups`. The reference program is written for one: setup_inputs(seed, part) draws one part's arguments, and reference() takes and returns one part's arrays. A program takes and returns all parts, laid end to end along the dimension named above; an argument that names none is the same for every part. Nothing has to cross between parts.
Inputs may be any that keep to these rules, and one draw needn't show every extreme that they name: `patch_order`: each patch once. `slab_rows`: the rows sum to 8; some slab has exactly 4 rows.
All inputs are finite; a program needn't handle non-finite values.
Results may differ from the reference program's by a relative error of at most 0.03.
Values may be sent and summed in bfloat16 or wider, within the bound.
A program may use at most 128 MiB of HBM per device.

```python
import math
import jax
import jax.numpy as jnp
import numpy as np
from jax import lax

HEADS = 24
HEAD_DIM = 128
D = 3072
LAT_CH = 16
DEC_CH = 512
SCHED_STEPS = 50
MICRO = 2
TOK_DEV = 8
FRAMES = 4
LAT_W = 8
LAYERS = 2
HGROUPS = 4
CYCLE = 1
GHEADS = 6
TOK_PATCH = 32
TOK_LANES = 64
LAT_H = 8
SLAB_MAX = 4
N_SEQ = 4


def steps_of(rng, extent, split, smallest, largest):
    def one(dim, blocks):
        steps = jax.random.uniform(jax.random.fold_in(jax.random.fold_in(rng, 6), dim), (blocks,), jnp.float32, smallest / len(split), largest / len(split))
        return jnp.repeat(jnp.exp(steps), extent[dim] // blocks).reshape((-1,) + (1,) * (len(extent) - dim - 1))

    loudness = one(*split[0])
    for cut in split[1:]:
        loudness = loudness * one(*cut)
    return loudness


def length_profile(number_of, total, limit, skew):
    portions = [(1 << 20) // math.isqrt(standing ** skew) + 1 for standing in range(2, number_of + 1)]
    rest, given = total - limit - (number_of - 1), [1] * (number_of - 1)
    while rest > 0:
        movable = [i for i in range(number_of - 1) if given[i] < limit]
        mass, remaining = sum([portions[i] for i in movable]), rest
        for i in movable:
            extra = min(limit - given[i], max(1, remaining * portions[i] // mass), rest)
            given[i] = given[i] + extra
            rest = rest - extra
    return np.array([limit] + given)


def ragged(own_key, number_of, total, reach, lean):
    if number_of == 2:
        one = jax.random.randint(own_key, (), max(1, total - reach), min(reach, total - 1) + 1)
        return jnp.stack([one, total - one])
    tallies = jnp.asarray(length_profile(number_of, total, reach, lean), jnp.int32)
    twos = (number_of - 1) // 2
    donor, taker = tallies[1:1 + 2 * twos:2], tallies[2:2 + 2 * twos:2]
    margin = jnp.minimum(donor - 1, reach - taker)
    passed = jax.random.randint(jax.random.fold_in(own_key, 1), (twos,), 0, 1 << 20) % (margin + 1)
    tallies = tallies.at[1:1 + 2 * twos:2].set(donor - passed).at[2:2 + 2 * twos:2].set(taker + passed)
    return tallies[jax.random.permutation(jax.random.fold_in(own_key, 2), number_of)]


def normal_values(rng, shape, scale, reach, cuts=(), kind=jnp.bfloat16):
    values = scale * jax.random.normal(rng, shape, jnp.float32)
    if cuts:
        values = values * steps_of(rng, shape, cuts, -0.22, 0.18)
    return jnp.clip(values, -reach, reach).astype(kind)


def setup_inputs(seed: int = 0, part: int = 0) -> dict:
    arg_keys = jax.random.split(jax.random.key(seed), 13)
    part_splits = jax.random.split(jax.random.fold_in(arg_keys[12], part), 13)
    latent = jnp.clip(jax.random.uniform(part_splits[0], (MICRO, TOK_PATCH, TOK_LANES), jnp.float32, -0.1, 0.1) * steps_of(part_splits[0], (MICRO, TOK_PATCH, TOK_LANES), ((1, 4),), -0.4, 0.0), -0.1, 0.1)
    w_embed = normal_values(arg_keys[1], (TOK_LANES, D), TOK_LANES ** -0.5, 0.75)
    w_qkv = normal_values(arg_keys[2], (LAYERS, 3 * D, D), D ** -0.5, 0.109375, ((0, 2), (1, 4)))
    w_out = normal_values(arg_keys[3], (LAYERS, D, D), D ** -0.5, 0.109375, ((0, 2), (1, 4)))
    mod_table = normal_values(arg_keys[4], (SCHED_STEPS, 3, D), 0.5, 3.0)
    cond_mod = normal_values(part_splits[5], (2, LAYERS, 3, D), 0.5, 3.0, ((0, 2), (1, 2)), jnp.float32)
    stale_kv = normal_values(part_splits[6], (LAYERS, 2, N_SEQ, MICRO, HGROUPS * TOK_DEV, 2 * GHEADS * HEAD_DIM), 1.0, 6.0, ((0, 2), (1, 2), (2, 4)))
    w_final = normal_values(arg_keys[7], (D, TOK_LANES), D ** -0.5, 0.109375)
    w_conv = normal_values(arg_keys[8], (27, LAT_CH, DEC_CH), (27 * LAT_CH) ** -0.5, 0.3125, ((2, 4),))
    patch_order = jax.random.permutation(part_splits[9], MICRO).astype(jnp.int32)
    timestep = jax.random.randint(part_splits[10], (1,), 0, SCHED_STEPS).astype(jnp.int32)
    slab_rows = ragged(part_splits[11], N_SEQ, LAT_H, SLAB_MAX, 2).astype(jnp.int32)
    return {"latent": latent, "w_embed": w_embed, "w_qkv": w_qkv, "w_out": w_out, "mod_table": mod_table, "cond_mod": cond_mod, "stale_kv": stale_kv, "w_final": w_final, "w_conv": w_conv, "patch_order": patch_order, "timestep": timestep, "slab_rows": slab_rows}


guide_scale = 5.0
norm_eps = 1e-06

def rms_scaled(values):
    wide = values.astype(jnp.float32)
    return wide * lax.rsqrt(lax.optimization_barrier(jnp.mean(wide * wide, axis=-1, keepdims=True)) + norm_eps)

def causal_conv(image, kernel):
    frames, rows, width = (image.shape[0], image.shape[1], image.shape[2])
    padded = jnp.concatenate([image[:1], image[:1], image], 0)
    padded = jnp.pad(padded, ((0, 0), (1, 1), (1, 1), (0, 0)))
    pieces = []
    for frame_shift in range(3):
        for row_shift in range(3):
            for col_shift in range(3):
                pieces.append(padded[frame_shift:frame_shift + frames, row_shift:row_shift + rows, col_shift:col_shift + width])
    columns = jnp.concatenate(pieces, -1)
    flat = columns.reshape(frames * rows * width, columns.shape[-1])
    result = jnp.dot(flat, kernel.reshape(-1, kernel.shape[-1]), preferred_element_type=jnp.float32)
    return result.reshape(frames, rows, width, kernel.shape[-1]).astype(jnp.bfloat16)

def reference(latent, w_embed, w_qkv, w_out, mod_table, cond_mod, stale_kv, w_final, w_conv, patch_order, timestep, slab_rows):
    stale = stale_kv.reshape(LAYERS, 2, HGROUPS, CYCLE, MICRO, N_SEQ, TOK_DEV // CYCLE, 2, GHEADS, HEAD_DIM)
    stale = jnp.transpose(stale, (0, 1, 4, 5, 3, 6, 7, 2, 8, 9)).reshape(LAYERS, 2, MICRO, TOK_PATCH, 2, HEADS, HEAD_DIM)
    table_row = lax.dynamic_index_in_dim(mod_table, timestep[0], 0, keepdims=False).astype(jnp.float32)
    flat_latent = latent.astype(jnp.bfloat16).reshape(MICRO * TOK_PATCH, TOK_LANES)
    embedded = jnp.dot(flat_latent, w_embed, preferred_element_type=jnp.float32).astype(jnp.bfloat16)
    embedded = embedded.reshape(MICRO, TOK_PATCH, D)
    predictions = []
    for branch in range(2):
        hidden = embedded
        for layer in range(LAYERS):
            modulation = table_row + cond_mod[branch, layer]
            cache = stale[layer, branch]
            for micro_index in range(MICRO):
                patch_id = patch_order[micro_index]
                current = lax.dynamic_index_in_dim(hidden, patch_id, 0, keepdims=False)
                normed = (rms_scaled(current) * (1.0 + modulation[1]) + modulation[0]).astype(jnp.bfloat16)
                projected = jnp.dot(normed, w_qkv[layer].T, preferred_element_type=jnp.float32).astype(jnp.bfloat16)
                projected = projected.reshape(TOK_PATCH, HEADS, 3, HEAD_DIM)
                fresh = jnp.transpose(projected[:, :, 1:], (0, 2, 1, 3))
                cache = lax.dynamic_update_index_in_dim(cache, fresh, patch_id, 0)
                keys = cache[:, :, 0].reshape(MICRO * TOK_PATCH, HEADS, HEAD_DIM)
                values = cache[:, :, 1].reshape(MICRO * TOK_PATCH, HEADS, HEAD_DIM)
                queries = projected[:, :, 0]
                scores = jnp.einsum('thd,khd->htk', queries.astype(jnp.float32), keys.astype(jnp.float32)) * HEAD_DIM ** (-0.5)
                probs = jax.nn.softmax(scores, axis=-1).astype(jnp.bfloat16)
                attended = jnp.einsum('htk,khd->thd', probs.astype(jnp.float32), values.astype(jnp.float32)).astype(jnp.bfloat16)
                mixed = jnp.dot(attended.reshape(TOK_PATCH, D), w_out[layer], preferred_element_type=jnp.float32)
                updated = (current.astype(jnp.float32) + modulation[2] * mixed).astype(jnp.bfloat16)
                hidden = lax.dynamic_update_index_in_dim(hidden, updated, patch_id, 0)
        final_normed = rms_scaled(hidden).astype(jnp.bfloat16).reshape(MICRO * TOK_PATCH, D)
        predicted = jnp.dot(final_normed, w_final, preferred_element_type=jnp.float32)
        predictions.append(predicted.reshape(MICRO, TOK_PATCH, TOK_LANES))
    velocity = (1.0 - guide_scale) * predictions[0] + guide_scale * predictions[1]
    stepped = latent - velocity / SCHED_STEPS
    image = stepped.reshape(FRAMES, LAT_H // 2, LAT_W // 2, 2, 2, LAT_CH)
    image = jnp.transpose(image, (0, 1, 3, 2, 4, 5)).reshape(FRAMES, LAT_H, LAT_W, LAT_CH).astype(jnp.bfloat16)
    features = causal_conv(image, w_conv)
    starts = jnp.cumsum(slab_rows) - slab_rows
    offsets = jnp.arange(SLAB_MAX).astype(jnp.int32)
    row_index = jnp.clip(starts[:, None] + offsets[None, :], 0, LAT_H - 1).astype(jnp.int32)
    valid = offsets[None, :] < slab_rows[:, None]
    picked = jnp.take(features, row_index.reshape(-1), axis=1).reshape(FRAMES, N_SEQ, SLAB_MAX, LAT_W, DEC_CH)
    picked = jnp.transpose(picked, (1, 0, 2, 3, 4))
    decoded = jnp.where(valid[:, None, :, None, None], picked, jnp.zeros_like(picked))
    return (velocity, decoded)
```

```python
import functools

import jax
import jax.numpy as jnp
from jax import lax
from jax.experimental import pallas as pl
from jax.experimental.pallas import tpu as pltpu
from jax.sharding import PartitionSpec as P

HEADS = 24
HEAD_DIM = 128
D = 3072
LAT_CH = 16
SCHED_STEPS = 50
MICRO = 2
TOK_DEV = 8
FRAMES = 4
LAT_W = 8


guide_scale = 5.0
norm_eps = 1e-06


def swapped(value, axis, bit):
    return lax.ppermute(value, axis, [(i, i ^ 1 << bit) for i in range(lax.axis_size(axis))])


def passed_along(value, axis, by):
    size = lax.axis_size(axis)
    pairs = [(i, i + by) for i in range(size) if 0 <= i + by < size]
    return lax.ppermute(value, axis, pairs)


def rms_scaled(values):
    wide = values.astype(jnp.float32)
    return wide * lax.rsqrt(jnp.mean(wide * wide, axis=-1, keepdims=True) + norm_eps)


def cycle_join(piece, seq_index, cycle_bits):
    joined = piece
    for bit_number in range(cycle_bits):
        partner = swapped(joined, "seq", bit_number)
        upper_half = (seq_index // 2**bit_number % 2).astype(jnp.int32)
        part_rows = joined.shape[0]
        combined = jnp.zeros((2 * part_rows,) + joined.shape[1:], joined.dtype)
        combined = lax.dynamic_update_slice_in_dim(combined, joined, upper_half * part_rows, 0)
        joined = lax.dynamic_update_slice_in_dim(combined, partner, (1 - upper_half) * part_rows, 0)
    return joined


def decode(stepped, w_conv, slab_rows):
    seq_count = lax.axis_size("seq")
    seq_index = lax.axis_index("seq")
    token_rows = MICRO * seq_count * TOK_DEV // (FRAMES * (LAT_W // 2))
    image_rows = 2 * token_rows
    slab_most = 2 * image_rows // seq_count
    image = stepped.reshape(FRAMES, token_rows, LAT_W // 2, 2, 2, LAT_CH)
    image = (
        jnp.transpose(image, (0, 1, 3, 2, 4, 5))
        .reshape(FRAMES, image_rows, LAT_W, LAT_CH)
        .astype(jnp.bfloat16)
    )
    padded = jnp.concatenate([image[:1], image[:1], image], 0)
    padded = jnp.pad(padded, ((0, 0), (1, 1 + slab_most), (1, 1), (0, 0)))
    positions = jnp.arange(seq_count)
    slab_count = jnp.sum(jnp.where(positions == seq_index, slab_rows, 0))
    slab_start = jnp.sum(jnp.where(positions < seq_index, slab_rows, 0))
    window = lax.dynamic_slice_in_dim(padded, slab_start, slab_most + 2, 1)
    pieces = []
    for frame_shift in range(3):
        for row_shift in range(3):
            for col_shift in range(3):
                pieces.append(
                    window[
                        frame_shift : frame_shift + FRAMES,
                        row_shift : row_shift + slab_most,
                        col_shift : col_shift + LAT_W,
                    ]
                )
    columns = jnp.concatenate(pieces, -1).reshape(FRAMES * slab_most * LAT_W, 27 * LAT_CH)
    kernel = w_conv.reshape(27 * LAT_CH, w_conv.shape[2])
    features = jnp.dot(columns, kernel, preferred_element_type=jnp.float32).astype(jnp.bfloat16)
    features = features.reshape(FRAMES, slab_most, LAT_W, w_conv.shape[2])
    row_valid = jnp.arange(slab_most)[None, :, None, None] < slab_count
    decoded = jnp.where(row_valid, features, jnp.zeros_like(features))
    return decoded[None]


def shards_general(
    latent,
    w_embed,
    w_qkv,
    w_out,
    mod_table,
    cond_mod,
    stale_kv,
    w_final,
    w_conv,
    patch_order,
    timestep,
    slab_rows,
):
    seq_count = lax.axis_size("seq")
    segment_count = lax.axis_size("segment")
    seq_index = lax.axis_index("seq")
    segment_index = lax.axis_index("segment")
    branch_index = lax.axis_index("cfg")
    group_count = min(seq_count, 8)
    cycle_size = seq_count // group_count
    cycle_bits = cycle_size.bit_length() - 1
    group_heads = HEADS // group_count
    sub_rows = TOK_DEV // cycle_size
    share_rows = seq_count * sub_rows
    kv_lanes = 2 * group_heads * HEAD_DIM
    table_row = lax.dynamic_index_in_dim(mod_table, timestep[0], 0, keepdims=False).astype(
        jnp.float32
    )
    modulation = table_row + cond_mod[0, 0]
    shift_row = modulation[0]
    scale_row = modulation[1]
    gate_row = modulation[2]
    joined_weights = (
        cycle_join(w_qkv[0], seq_index, cycle_bits),
        cycle_join(w_out[0], seq_index, cycle_bits),
    )
    stale_joined = cycle_join(stale_kv[0, 0], seq_index, cycle_bits)
    cache = jnp.transpose(stale_joined, (1, 0, 2, 3)).reshape(
        MICRO, cycle_size * share_rows, kv_lanes
    )
    received = jnp.zeros((TOK_DEV, D), jnp.bfloat16)
    finished = jnp.zeros((MICRO, TOK_DEV, D), jnp.bfloat16)
    slot_ids = jnp.arange(MICRO)
    tick_count = MICRO + segment_count - 1
    for tick_index in range(tick_count):
        qkv_rows, out_rows = joined_weights
        micro_index = tick_index - segment_index
        active = (micro_index >= 0) & (micro_index < MICRO)
        clipped = jnp.clip(micro_index, 0, MICRO - 1)
        patch_id = jnp.sum(jnp.where(slot_ids == clipped, patch_order, 0))
        own_latent = lax.dynamic_index_in_dim(latent, patch_id, 0, keepdims=False).astype(
            jnp.bfloat16
        )
        embedded = jnp.dot(own_latent, w_embed, preferred_element_type=jnp.float32).astype(
            jnp.bfloat16
        )
        layer_input = jnp.where(segment_index == 0, embedded, received)
        normed = (rms_scaled(layer_input) * (1.0 + scale_row) + shift_row).astype(jnp.bfloat16)
        outgoing = jnp.broadcast_to(
            normed.reshape(1, cycle_size, sub_rows, D), (group_count, cycle_size, sub_rows, D)
        )
        shared = lax.all_to_all(
            outgoing.reshape(share_rows, D), "seq", split_axis=0, concat_axis=0, tiled=True
        )
        projected = lax.dot_general(
            shared, qkv_rows, (((1,), (1,)), ((), ())), preferred_element_type=jnp.float32
        )
        projected = projected.astype(jnp.bfloat16).reshape(share_rows, group_heads, 3, HEAD_DIM)
        queries = projected[:, :, 0]
        fresh_local = jnp.transpose(projected[:, :, 1:], (0, 2, 1, 3)).reshape(
            1, share_rows, kv_lanes
        )
        fresh = cycle_join(fresh_local, seq_index, cycle_bits).reshape(
            cycle_size * share_rows, kv_lanes
        )
        previous = lax.dynamic_index_in_dim(cache, patch_id, 0, keepdims=False)
        cache = lax.dynamic_update_index_in_dim(
            cache, jnp.where(active, fresh, previous), patch_id, 0
        )
        keyvals = cache.reshape(MICRO * cycle_size * share_rows, 2, group_heads, HEAD_DIM)
        scores = jnp.einsum(
            "shd,khd->hsk", queries, keyvals[:, 0], preferred_element_type=jnp.float32
        ) * HEAD_DIM ** (-0.5)
        probs = jax.nn.softmax(scores, axis=-1).astype(jnp.bfloat16)
        attended = jnp.einsum(
            "hsk,khd->shd", probs, keyvals[:, 1], preferred_element_type=jnp.float32
        ).astype(jnp.bfloat16)
        partial_out = jnp.dot(
            attended.reshape(share_rows, group_heads * HEAD_DIM),
            out_rows,
            preferred_element_type=jnp.float32,
        )
        returned = lax.all_to_all(
            partial_out.astype(jnp.bfloat16), "seq", split_axis=0, concat_axis=0, tiled=True
        ).astype(partial_out.dtype)
        mixed = jnp.sum(returned.reshape(group_count, cycle_size, sub_rows, D), axis=0).reshape(
            TOK_DEV, D
        )
        layer_output = (layer_input.astype(jnp.float32) + gate_row * mixed).astype(jnp.bfloat16)
        keep_final = active & (segment_index == segment_count - 1)
        earlier = lax.dynamic_index_in_dim(finished, patch_id, 0, keepdims=False)
        finished = lax.dynamic_update_index_in_dim(
            finished, jnp.where(keep_final, layer_output, earlier), patch_id, 0
        )
        if tick_index + 1 < tick_count:
            received = passed_along(layer_output, "segment", 1)
    final_normed = rms_scaled(finished).astype(jnp.bfloat16)
    predicted = jnp.einsum("mtd,dc->mtc", final_normed, w_final, preferred_element_type=jnp.float32)
    is_last = segment_index == segment_count - 1
    branch_weight = jnp.where(branch_index == 0, 1.0 - guide_scale, guide_scale)
    velocity_term = jnp.where(is_last, branch_weight * predicted, 0.0)
    latent_term = jnp.where(is_last & (branch_index == 0), latent, 0.0)
    velocity_own, latent_own = lax.psum((velocity_term, latent_term), ("segment", "cfg"))
    velocity_full, latent_full = (
        lax.all_gather(velocity_own, "seq", axis=1, tiled=True),
        lax.all_gather(latent_own, "seq", axis=1, tiled=True),
    )
    stepped = latent_full - velocity_full / SCHED_STEPS
    return (velocity_own, decode(stepped, w_conv, slab_rows))


ROWS = MICRO * TOK_DEV
SHIFTS = [(u, dy, dz) for u in range(3) for dy in (-1, 0, 1) for dz in (-1, 0, 1)]
QUARTERS = [
    (a, e, row, col) for a in range(2) for e in range(2) for row in range(2) for col in range(2)
]
MESH = pl.DeviceIdType.MESH


def cuts(*widths):
    edges = [sum(widths[:i]) for i in range(len(widths) + 1)]
    return [slice(a, b) for a, b in zip(edges[:-1], edges[1:])]


LOADS = cuts(768, 768, 768, 768)
PASSES = cuts(512, 512, 512, 512, 512, 512)
RETURNS = cuts(512, 512, 512, 512, 512, 512)


def fused_kernel(
    seq_count,
    group_heads,
    lat_ref,
    order_ref,
    slab_ref,
    step_index,
    cond_ref,
    table_hbm,
    conv_hbm,
    emb_hbm,
    qkv_hbm,
    out_hbm,
    stale_hbm,
    fin_hbm,
    vel_ref,
    dec_ref,
    table,
    conv,
    spread,
    taps,
    feature,
    emb,
    w_qkv,
    w_out,
    stale,
    fin,
    mod_ref,
    bias_ref,
    lat_all,
    staged,
    sums,
    folded,
    attended,
    parts,
    got_first,
    got_second,
    x_own,
    x_second,
    pred_all,
    load_sem,
    qkv_sem,
    lat_send,
    lat_recv,
    first_send,
    first_recv,
    pass_send,
    pass_recv,
    second_send,
    second_recv,
    pred_send,
    pred_recv,
):
    me = lax.axis_index("seq")
    segment = lax.axis_index("segment")
    branch = lax.axis_index("cfg")
    head_rows = 3 * HEAD_DIM
    tokens = seq_count * ROWS
    lanes = lat_ref.shape[-1]
    first = segment == 0
    second = segment == 1
    bf16, f32 = jnp.bfloat16, jnp.float32

    def peer(step):
        return lax.rem(me + step, seq_count)

    def block(index):
        return pl.ds(pl.multiple_of(index * ROWS, ROWS), ROWS)

    barrier = pltpu.get_barrier_semaphore()
    others = [
        (k, a, b) for k in range(seq_count) for a in range(2) for b in range(2) if k + a + b
    ]
    for k, a, b in others:
        where = {
            "seq": peer(k),
            "segment": lax.rem(segment + a, 2),
            "cfg": lax.rem(branch + b, 2),
        }
        pl.semaphore_signal(barrier, inc=1, device_id=where, device_id_type=MESH)

    def load(i, source, target):
        return pltpu.make_async_copy(source, target, load_sem.at[i])

    emb_load = load(0, emb_hbm, emb)
    table_load = load(1, table_hbm, table)
    conv_load = load(2, conv_hbm, conv)
    stale_load = load(3, stale_hbm, stale)
    out_load = load(4, out_hbm, w_out)
    fin_load = load(5, fin_hbm, fin)
    qkv_loads = [
        pltpu.make_async_copy(qkv_hbm.at[:, part], w_qkv.at[:, part], qkv_sem.at[c])
        for c, part in enumerate(LOADS)
    ]
    emb_load.start()
    table_load.start()
    for copy in qkv_loads:
        copy.start()
    conv_load.start()
    stale_load.start()
    out_load.start()
    fin_load.start()

    row = lax.broadcasted_iota(jnp.int32, bias_ref.shape, 0)
    column = lax.broadcasted_iota(jnp.int32, bias_ref.shape, 1)
    query_patch = (row >> 3) & 1
    fresh = column < tokens
    key_patch = jnp.where(
        fresh, (column >> 3) & 1, jnp.where(column < tokens + tokens // MICRO, 0, 1)
    )
    early = query_patch == order_ref[0]
    same = query_patch == key_patch
    bias_fresh = jnp.where(same, 0.0, jnp.where(early, -1e30, 0.0))
    bias_stale = jnp.where(same, -1e30, jnp.where(early, 0.0, -1e30))
    bias_ref[...] = jnp.where(fresh, bias_fresh, bias_stale)

    emb_load.wait()
    own_latent = lat_ref[...].reshape(ROWS, lanes)
    square = jnp.zeros((ROWS, 1), f32)
    for part in LOADS:
        embedded = jnp.dot(
            own_latent.astype(bf16), emb[:, part], preferred_element_type=f32
        ).astype(bf16)
        x_own[:, part] = embedded
        wide = embedded.astype(f32)
        square = square + jnp.sum(wide * wide, axis=-1, keepdims=True)
    lat_all[me] = jnp.concatenate(
        [own_latent, jnp.broadcast_to(square, (ROWS, lanes))], 1
    ).reshape(MICRO, TOK_DEV, 2 * lanes)

    table_load.wait()
    plan_row = lax.broadcasted_iota(jnp.int32, table.shape[1:], 0) == step_index[0]
    for i in range(3):
        chosen = jnp.where(plan_row, table[i].astype(f32), 0.0)
        mod_ref[i : i + 1] = jnp.sum(chosen, axis=0, keepdims=True)
    pieces = D // 128
    for i in range(3):
        for j in range(pieces):
            at = slice(j * 128, (j + 1) * 128)
            mod_ref[i : i + 1, at] += cond_ref[i * pieces + j : i * pieces + j + 1]
    staged[tokens:] = jnp.broadcast_to(mod_ref[0:1], (16, D)).astype(bf16)

    def project(c, part):
        for head in range(group_heads):
            rows = slice(head * head_rows, (head + 1) * head_rows)
            piece = lax.dot_general(
                staged[:, part],
                w_qkv[rows, part],
                (((1,), (1,)), ((), ())),
                preferred_element_type=f32,
            )
            if c == 0:
                sums[head] = piece
            else:
                sums[head] += piece

    def build_spread():
        conv_load.wait()
        spread[...] = jnp.zeros_like(spread)
        for n, (u, dy, dz) in enumerate(SHIFTS):
            for a, e, row_out, col_out in QUARTERS:
                v, w = 2 * dy + a - row_out + 1, 2 * dz + e - col_out + 1
                if 0 <= v < 3 and 0 <= w < 3:
                    at = n * lanes + (2 * a + e) * LAT_CH
                    to = (2 * row_out + col_out) * conv.shape[2]
                    spread[at : at + LAT_CH, to : to + conv.shape[2]] = conv[9 * u + 3 * v + w]

    @pl.when(first)
    def _():
        for c, part in enumerate(LOADS):
            scaled = emb[:, part].astype(f32) * (1.0 + mod_ref[1:2, part])
            staged[0:tokens, part] = scaled.astype(bf16)
            qkv_loads[c].wait()
            project(c, part)
        for head in range(group_heads):
            whole = sums[head, 0:lanes]
            upper = whole.astype(bf16)
            folded[head, 0:lanes] = upper
            folded[head, lanes : 2 * lanes] = (whole - upper.astype(f32)).astype(bf16)

    @pl.when(second)
    def _():
        build_spread()
        for c in range(len(LOADS)):
            qkv_loads[c].wait()

    stale_load.wait()
    pl.semaphore_wait(barrier, len(others))

    def remote(source, target, send, recv, where):
        return pltpu.make_async_remote_copy(
            src_ref=source,
            dst_ref=target,
            send_sem=send,
            recv_sem=recv,
            device_id=where,
            device_id_type=MESH,
        )

    def lat_copy(k, slot):
        return remote(
            lat_all.at[slot], lat_all.at[slot], lat_send.at[k], lat_recv.at[slot], {"seq": peer(k)}
        )

    def first_copy(k, c, sender):
        part = PASSES[c]
        return remote(
            parts.at[block(peer(k)), part],
            got_first.at[sender, :, part],
            first_send.at[k, c],
            first_recv.at[sender, c],
            {"seq": peer(k), "segment": 1},
        )

    def pass_copy(k, c, sender):
        rows = block(sender)
        return remote(
            x_second.at[rows, PASSES[c]],
            x_second.at[rows, PASSES[c]],
            pass_send.at[k, c],
            pass_recv.at[sender, c],
            {"seq": peer(k)},
        )

    def second_copy(k, c, sender):
        part = RETURNS[c]
        return remote(
            parts.at[block(peer(k)), part],
            got_second.at[sender, :, part],
            second_send.at[k, c],
            second_recv.at[sender, c],
            {"seq": peer(k)},
        )

    def pred_copy(index, k, a, b, slot, sender_branch):
        return remote(
            pred_all.at[slot, sender_branch],
            pred_all.at[slot, sender_branch],
            pred_send.at[index],
            pred_recv.at[slot, sender_branch],
            {"seq": peer(k), "segment": 1 - a, "cfg": lax.rem(branch + b, 2)},
        )

    for k in range(1, seq_count):
        lat_copy(k, me).start()

    def attend(projected):
        scores = []
        for head in range(group_heads):
            key_lanes = slice(head * HEAD_DIM, (head + 1) * HEAD_DIM)
            keys = jnp.concatenate(
                [projected[head][:, HEAD_DIM : 2 * HEAD_DIM], stale[:, key_lanes]], 0
            )
            scores.append(
                lax.dot_general(
                    projected[head][:, :HEAD_DIM],
                    keys,
                    (((1,), (1,)), ((), ())),
                    preferred_element_type=f32,
                )
            )
        scores = jnp.stack(scores) * HEAD_DIM ** (-0.5) + bias_ref[...][None]
        weights = jnp.exp(scores - jnp.max(scores, axis=-1, keepdims=True))
        probs = (weights / jnp.sum(weights, axis=-1, keepdims=True)).astype(bf16)
        for head in range(group_heads):
            key_lanes = slice(head * HEAD_DIM, (head + 1) * HEAD_DIM)
            value_lanes = slice(
                (group_heads + head) * HEAD_DIM, (group_heads + head + 1) * HEAD_DIM
            )
            values = jnp.concatenate(
                [projected[head][:, 2 * HEAD_DIM :], stale[:, value_lanes]], 0
            )
            attended[:, key_lanes] = jnp.dot(
                probs[head], values, preferred_element_type=f32
            ).astype(bf16)

    def mix(part):
        mixed = jnp.dot(attended[...], w_out[:, part], preferred_element_type=f32)
        parts[:, part] = (mixed * mod_ref[2:3, part]).astype(bf16)

    @pl.when(first)
    def _():
        for k in range(1, seq_count):
            lat_copy(k, peer(k)).wait_recv()
        whole = lat_all[...].reshape(tokens, 2 * lanes)
        lane = lax.broadcasted_iota(jnp.int32, whole.shape, 1)
        twice = jnp.where(lane < lanes, whole, pltpu.roll(whole, lanes, 1)).astype(bf16)
        inverse = lax.rsqrt(whole[:, lanes : lanes + 1] / D + norm_eps)
        projected = []
        for head in range(group_heads):
            product = jnp.dot(twice, folded[head], preferred_element_type=f32)
            product = product * inverse + sums[head, tokens : tokens + 1]
            projected.append(product.astype(bf16))
        attend(projected)
        out_load.wait()
        for c, part in enumerate(PASSES):
            mix(part)
            for k in range(seq_count):
                first_copy(k, c, me).start()
        fin_load.wait()
        build_spread()
        for c in range(len(PASSES)):
            for k in range(seq_count):
                first_copy(k, c, me).wait_send()
        for k in range(seq_count):
            for b in range(2):
                slot, sender_branch = peer(k), lax.rem(branch + b, 2)
                pred_copy(0, 0, 0, 0, slot, sender_branch).wait_recv()

    @pl.when(second)
    def _():
        for k in range(1, seq_count):
            lat_copy(k, peer(k)).wait_recv()
        fin_load.wait()
        out_load.wait()
        for c, part in enumerate(PASSES):
            total = x_own[:, part].astype(f32)
            for s in range(seq_count):
                first_copy(0, c, s).wait_recv()
                total = total + got_first[s, :, part].astype(f32)
            x_second[block(me), part] = total.astype(bf16)
            for k in range(1, seq_count):
                pass_copy(k, c, me).start()
        square = jnp.zeros((tokens, 1), f32)
        for c, part in enumerate(PASSES):
            for k in range(1, seq_count):
                pass_copy(k, c, peer(k)).wait_recv()
            wide = x_second[:, part].astype(f32)
            square = square + jnp.sum(wide * wide, axis=-1, keepdims=True)
            staged[0:tokens, part] = (wide * (1.0 + mod_ref[1:2, part])).astype(bf16)
            project(c, part)
        inverse = lax.rsqrt(square / D + norm_eps)
        projected = [
            (sums[head, 0:tokens] * inverse + sums[head, tokens : tokens + 1]).astype(bf16)
            for head in range(group_heads)
        ]
        attend(projected)
        for c, part in enumerate(RETURNS):
            mix(part)
            for k in range(1, seq_count):
                second_copy(k, c, me).start()
        predicted = jnp.zeros((ROWS, lanes), f32)
        square = jnp.zeros((ROWS, 1), f32)
        for c, part in enumerate(RETURNS):
            total = x_second[block(me), part].astype(f32) + parts[block(me), part].astype(f32)
            for k in range(1, seq_count):
                second_copy(k, c, peer(k)).wait_recv()
                total = total + got_second[peer(k), :, part].astype(f32)
            rounded = total.astype(bf16)
            wide = rounded.astype(f32)
            square = square + jnp.sum(wide * wide, axis=-1, keepdims=True)
            predicted = predicted + lax.dot_general(
                rounded, fin[:, part], (((1,), (1,)), ((), ())), preferred_element_type=f32
            )
        predicted = predicted * lax.rsqrt(square / D + norm_eps)
        pred_all[me, branch] = jnp.concatenate([predicted[:TOK_DEV], predicted[TOK_DEV:]], 1)
        targets = [(k, a, b) for k, a, b in others]
        for index, (k, a, b) in enumerate(targets):
            pred_copy(index, k, a, b, me, branch).start()
        for c in range(len(PASSES)):
            for k in range(1, seq_count):
                pass_copy(k, c, me).wait_send()
        for c in range(len(RETURNS)):
            for k in range(1, seq_count):
                second_copy(k, c, me).wait_send()
        for k in range(seq_count):
            for b in range(2):
                if k + b:
                    slot, sender_branch = peer(k), lax.rem(branch + b, 2)
                    pred_copy(0, 0, 0, 0, slot, sender_branch).wait_recv()
        for index, (k, a, b) in enumerate(targets):
            pred_copy(index, k, a, b, me, branch).wait_send()

    def guided(slot):
        return (1.0 - guide_scale) * pred_all[slot, 0] + guide_scale * pred_all[slot, 1]

    velocity = guided(me)
    for p in range(MICRO):
        vel_ref[p] = velocity[:, p * lanes : (p + 1) * lanes]
    image = []
    for s in range(seq_count):
        velocity = guided(s) / SCHED_STEPS
        image.append(lat_all[s, 0] - velocity)
    for s in range(seq_count):
        velocity = pltpu.roll(guided(s), lanes, 1) / SCHED_STEPS
        image.append(lat_all[s, 1] - velocity)
    image = jnp.concatenate(image, 0)[:, :lanes]
    image = image.astype(bf16).astype(f32)
    rows_deep = tokens // (FRAMES * (LAT_W // 2))
    frame = tokens // FRAMES
    place = lax.broadcasted_iota(jnp.int32, image.shape, 0)
    across = place & (LAT_W // 2 - 1)
    down = (place >> 2) & (rows_deep - 1)
    moved = {}
    for dy in (-1, 0, 1):
        for dz in (-1, 0, 1):
            by = dy * (LAT_W // 2) + dz
            shifted = pltpu.roll(image, (-by) % tokens, 0) if by else image
            if dz == 1:
                shifted = jnp.where(across < LAT_W // 2 - 1, shifted, 0.0)
            if dz == -1:
                shifted = jnp.where(across > 0, shifted, 0.0)
            if dy == 1:
                shifted = jnp.where(down < rows_deep - 1, shifted, 0.0)
            if dy == -1:
                shifted = jnp.where(down > 0, shifted, 0.0)
            moved[dy, dz] = shifted

    def tap(n):
        if n == len(SHIFTS):
            return jnp.zeros_like(image)
        u, dy, dz = SHIFTS[n]
        order = [max(f + u - 2, 0) for f in range(FRAMES)]
        return jnp.concatenate(
            [moved[dy, dz][f * frame : (f + 1) * frame] for f in order], 0
        )

    for pair in range((len(SHIFTS) + 1) // 2):
        both = jnp.concatenate([tap(2 * pair), tap(2 * pair + 1)], 1)
        taps[:, pair * 2 * lanes : (pair + 1) * 2 * lanes] = both.astype(bf16)
    channels = conv.shape[2]
    features = jnp.dot(taps[...], spread[...], preferred_element_type=f32)
    for a in range(2):
        for e in range(2):
            at = (2 * a + e) * channels
            feature[a, pl.ds(e, tokens, stride=2), :] = features[:, at : at + channels]
    start = jnp.int32(0)
    count = jnp.int32(0)
    for s in range(seq_count):
        start = start + jnp.where(s < me, slab_ref[s], 0)
        count = count + jnp.where(s == me, slab_ref[s], 0)
    for k in range(dec_ref.shape[2]):
        keep = [
            jnp.where((start + k == y) & (k < count), 1.0, 0.0) for y in range(2 * rows_deep)
        ]
        for f in range(FRAMES):
            total = jnp.zeros((LAT_W, channels), f32)
            for y in range(2 * rows_deep):
                at = (f * rows_deep + y // 2) * LAT_W
                total = total + keep[y] * feature[y % 2, at : at + LAT_W]
            dec_ref[0, f, k] = total.astype(bf16)

    for k in range(1, seq_count):
        lat_copy(k, me).wait_send()


def shards_fused(
    latent,
    w_embed,
    w_qkv,
    w_out,
    mod_table,
    cond_mod,
    stale_kv,
    w_final,
    w_conv,
    patch_order,
    timestep,
    slab_rows,
):
    seq_count = lax.axis_size("seq")
    group_heads = HEADS // seq_count
    tokens = seq_count * ROWS
    lanes = latent.shape[-1]
    spreads = (len(SHIFTS) + 1) * lanes
    slab_most = 2 * 2 * tokens // (FRAMES * (LAT_W // 2)) // seq_count
    channels = w_conv.shape[2]
    bf16, f32, dma = jnp.bfloat16, jnp.float32, pltpu.SemaphoreType.DMA
    here = pl.BlockSpec(memory_space=pltpu.VMEM)
    small = pl.BlockSpec(memory_space=pltpu.SMEM)
    away = pl.BlockSpec(memory_space=pl.ANY)
    return pl.pallas_call(
        functools.partial(fused_kernel, seq_count, group_heads),
        out_shape=(
            jax.ShapeDtypeStruct(latent.shape, f32),
            jax.ShapeDtypeStruct((1, FRAMES, slab_most, LAT_W, channels), bf16),
        ),
        in_specs=[here, small, small, small, here] + [away] * 7,
        out_specs=(here, here),
        scratch_shapes=[
            pltpu.VMEM((3, SCHED_STEPS, D), bf16),
            pltpu.VMEM(w_conv.shape, bf16),
            pltpu.VMEM((spreads, 4 * channels), bf16),
            pltpu.VMEM((tokens, spreads), bf16),
            pltpu.VMEM((2, 2 * tokens, channels), f32),
            pltpu.VMEM((lanes, D), bf16),
            pltpu.VMEM((3 * group_heads * HEAD_DIM, D), bf16),
            pltpu.VMEM((group_heads * HEAD_DIM, D), bf16),
            pltpu.VMEM((tokens, 2 * group_heads * HEAD_DIM), bf16),
            pltpu.VMEM((lanes, D), bf16),
            pltpu.VMEM((8, D), f32),
            pltpu.VMEM((tokens, 2 * tokens), f32),
            pltpu.VMEM((seq_count, MICRO, TOK_DEV, 2 * lanes), f32),
            pltpu.VMEM((tokens + 16, D), bf16),
            pltpu.VMEM((group_heads, tokens + 16, 3 * HEAD_DIM), f32),
            pltpu.VMEM((group_heads, 2 * lanes, 3 * HEAD_DIM), bf16),
            pltpu.VMEM((tokens, group_heads * HEAD_DIM), bf16),
            pltpu.VMEM((tokens, D), bf16),
            pltpu.VMEM((seq_count, ROWS, D), bf16),
            pltpu.VMEM((seq_count, ROWS, D), bf16),
            pltpu.VMEM((ROWS, D), bf16),
            pltpu.VMEM((tokens, D), bf16),
            pltpu.VMEM((seq_count, 2, TOK_DEV, 2 * lanes), f32),
            dma((6,)),
            dma((len(LOADS),)),
            dma((seq_count,)),
            dma((seq_count,)),
            dma((seq_count, len(PASSES))),
            dma((seq_count, len(PASSES))),
            dma((seq_count, len(PASSES))),
            dma((seq_count, len(PASSES))),
            dma((seq_count, len(RETURNS))),
            dma((seq_count, len(RETURNS))),
            dma((4 * seq_count - 1,)),
            dma((seq_count, 2)),
        ],
        compiler_params=pltpu.CompilerParams(
            collective_id=0, has_side_effects=True, vmem_limit_bytes=60 * 2**20
        ),
        name="denoise",
    )(
        latent,
        patch_order,
        slab_rows,
        timestep,
        cond_mod.reshape(3 * D // 128, 128),
        jnp.transpose(mod_table, (1, 0, 2)),
        w_conv,
        w_embed,
        w_qkv[0],
        w_out[0],
        stale_kv.reshape(tokens, 2 * group_heads * HEAD_DIM),
        w_final.T,
    )


def solution(mesh):
    in_specs = (
        P(None, ("groups", "seq"), None),
        P(),
        P("segment", "seq", None),
        P("segment", "seq", None),
        P(),
        P("cfg", ("groups", "segment"), None, None),
        P("segment", "cfg", "seq", None, "groups", None),
        P(),
        P(None, None, ("segment", "cfg")),
        P("groups"),
        P("groups"),
        P("groups"),
    )
    out_specs = (
        P(None, ("groups", "seq"), None),
        P(("groups", "seq"), None, None, None, ("segment", "cfg")),
    )
    small = mesh.shape["seq"] == 4 and mesh.shape["segment"] == 2 and mesh.shape["cfg"] == 2
    shards = shards_fused if small else shards_general
    return jax.shard_map(shards, mesh=mesh, in_specs=in_specs, out_specs=out_specs, check_vma=False)
```

```python
import functools

import jax
import jax.numpy as jnp
from jax import lax
from jax.experimental import pallas as pl
from jax.experimental.pallas import tpu as pltpu
from jax.sharding import PartitionSpec as P

HEADS = 24
HEAD_DIM = 128
D = 3072
LAT_CH = 16
SCHED_STEPS = 50
MICRO = 2
TOK_DEV = 8
FRAMES = 4
LAT_W = 8


guide_scale = 5.0
norm_eps = 1e-06


def swapped(value, axis, bit):
    return lax.ppermute(value, axis, [(i, i ^ 1 << bit) for i in range(lax.axis_size(axis))])


def passed_along(value, axis, by):
    size = lax.axis_size(axis)
    pairs = [(i, i + by) for i in range(size) if 0 <= i + by < size]
    return lax.ppermute(value, axis, pairs)


def rms_scaled(values):
    wide = values.astype(jnp.float32)
    return wide * lax.rsqrt(jnp.mean(wide * wide, axis=-1, keepdims=True) + norm_eps)


def cycle_join(piece, seq_index, cycle_bits):
    joined = piece
    for bit_number in range(cycle_bits):
        partner = swapped(joined, "seq", bit_number)
        upper_half = (seq_index // 2**bit_number % 2).astype(jnp.int32)
        part_rows = joined.shape[0]
        combined = jnp.zeros((2 * part_rows,) + joined.shape[1:], joined.dtype)
        combined = lax.dynamic_update_slice_in_dim(combined, joined, upper_half * part_rows, 0)
        joined = lax.dynamic_update_slice_in_dim(combined, partner, (1 - upper_half) * part_rows, 0)
    return joined


def decode(stepped, w_conv, slab_rows):
    seq_count = lax.axis_size("seq")
    seq_index = lax.axis_index("seq")
    token_rows = MICRO * seq_count * TOK_DEV // (FRAMES * (LAT_W // 2))
    image_rows = 2 * token_rows
    slab_most = 2 * image_rows // seq_count
    image = stepped.reshape(FRAMES, token_rows, LAT_W // 2, 2, 2, LAT_CH)
    image = (
        jnp.transpose(image, (0, 1, 3, 2, 4, 5))
        .reshape(FRAMES, image_rows, LAT_W, LAT_CH)
        .astype(jnp.bfloat16)
    )
    padded = jnp.concatenate([image[:1], image[:1], image], 0)
    padded = jnp.pad(padded, ((0, 0), (1, 1 + slab_most), (1, 1), (0, 0)))
    positions = jnp.arange(seq_count)
    slab_count = jnp.sum(jnp.where(positions == seq_index, slab_rows, 0))
    slab_start = jnp.sum(jnp.where(positions < seq_index, slab_rows, 0))
    window = lax.dynamic_slice_in_dim(padded, slab_start, slab_most + 2, 1)
    pieces = []
    for frame_shift in range(3):
        for row_shift in range(3):
            for col_shift in range(3):
                pieces.append(
                    window[
                        frame_shift : frame_shift + FRAMES,
                        row_shift : row_shift + slab_most,
                        col_shift : col_shift + LAT_W,
                    ]
                )
    columns = jnp.concatenate(pieces, -1).reshape(FRAMES * slab_most * LAT_W, 27 * LAT_CH)
    kernel = w_conv.reshape(27 * LAT_CH, w_conv.shape[2])
    features = jnp.dot(columns, kernel, preferred_element_type=jnp.float32).astype(jnp.bfloat16)
    features = features.reshape(FRAMES, slab_most, LAT_W, w_conv.shape[2])
    row_valid = jnp.arange(slab_most)[None, :, None, None] < slab_count
    decoded = jnp.where(row_valid, features, jnp.zeros_like(features))
    return decoded[None]


def shards_general(
    latent,
    w_embed,
    w_qkv,
    w_out,
    mod_table,
    cond_mod,
    stale_kv,
    w_final,
    w_conv,
    patch_order,
    timestep,
    slab_rows,
):
    seq_count = lax.axis_size("seq")
    segment_count = lax.axis_size("segment")
    seq_index = lax.axis_index("seq")
    segment_index = lax.axis_index("segment")
    branch_index = lax.axis_index("cfg")
    group_count = min(seq_count, 8)
    cycle_size = seq_count // group_count
    cycle_bits = cycle_size.bit_length() - 1
    group_heads = HEADS // group_count
    sub_rows = TOK_DEV // cycle_size
    share_rows = seq_count * sub_rows
    kv_lanes = 2 * group_heads * HEAD_DIM
    table_row = lax.dynamic_index_in_dim(mod_table, timestep[0], 0, keepdims=False).astype(
        jnp.float32
    )
    modulation = table_row + cond_mod[0, 0]
    shift_row = modulation[0]
    scale_row = modulation[1]
    gate_row = modulation[2]
    joined_weights = (
        cycle_join(w_qkv[0], seq_index, cycle_bits),
        cycle_join(w_out[0], seq_index, cycle_bits),
    )
    stale_joined = cycle_join(stale_kv[0, 0], seq_index, cycle_bits)
    cache = jnp.transpose(stale_joined, (1, 0, 2, 3)).reshape(
        MICRO, cycle_size * share_rows, kv_lanes
    )
    received = jnp.zeros((TOK_DEV, D), jnp.bfloat16)
    finished = jnp.zeros((MICRO, TOK_DEV, D), jnp.bfloat16)
    slot_ids = jnp.arange(MICRO)
    tick_count = MICRO + segment_count - 1
    for tick_index in range(tick_count):
        qkv_rows, out_rows = joined_weights
        micro_index = tick_index - segment_index
        active = (micro_index >= 0) & (micro_index < MICRO)
        clipped = jnp.clip(micro_index, 0, MICRO - 1)
        patch_id = jnp.sum(jnp.where(slot_ids == clipped, patch_order, 0))
        own_latent = lax.dynamic_index_in_dim(latent, patch_id, 0, keepdims=False).astype(
            jnp.bfloat16
        )
        embedded = jnp.dot(own_latent, w_embed, preferred_element_type=jnp.float32).astype(
            jnp.bfloat16
        )
        layer_input = jnp.where(segment_index == 0, embedded, received)
        normed = (rms_scaled(layer_input) * (1.0 + scale_row) + shift_row).astype(jnp.bfloat16)
        outgoing = jnp.broadcast_to(
            normed.reshape(1, cycle_size, sub_rows, D), (group_count, cycle_size, sub_rows, D)
        )
        shared = lax.all_to_all(
            outgoing.reshape(share_rows, D), "seq", split_axis=0, concat_axis=0, tiled=True
        )
        projected = lax.dot_general(
            shared, qkv_rows, (((1,), (1,)), ((), ())), preferred_element_type=jnp.float32
        )
        projected = projected.astype(jnp.bfloat16).reshape(share_rows, group_heads, 3, HEAD_DIM)
        queries = projected[:, :, 0]
        fresh_local = jnp.transpose(projected[:, :, 1:], (0, 2, 1, 3)).reshape(
            1, share_rows, kv_lanes
        )
        fresh = cycle_join(fresh_local, seq_index, cycle_bits).reshape(
            cycle_size * share_rows, kv_lanes
        )
        previous = lax.dynamic_index_in_dim(cache, patch_id, 0, keepdims=False)
        cache = lax.dynamic_update_index_in_dim(
            cache, jnp.where(active, fresh, previous), patch_id, 0
        )
        keyvals = cache.reshape(MICRO * cycle_size * share_rows, 2, group_heads, HEAD_DIM)
        scores = jnp.einsum(
            "shd,khd->hsk", queries, keyvals[:, 0], preferred_element_type=jnp.float32
        ) * HEAD_DIM ** (-0.5)
        probs = jax.nn.softmax(scores, axis=-1).astype(jnp.bfloat16)
        attended = jnp.einsum(
            "hsk,khd->shd", probs, keyvals[:, 1], preferred_element_type=jnp.float32
        ).astype(jnp.bfloat16)
        partial_out = jnp.dot(
            attended.reshape(share_rows, group_heads * HEAD_DIM),
            out_rows,
            preferred_element_type=jnp.float32,
        )
        returned = lax.all_to_all(
            partial_out.astype(jnp.bfloat16), "seq", split_axis=0, concat_axis=0, tiled=True
        ).astype(partial_out.dtype)
        mixed = jnp.sum(returned.reshape(group_count, cycle_size, sub_rows, D), axis=0).reshape(
            TOK_DEV, D
        )
        layer_output = (layer_input.astype(jnp.float32) + gate_row * mixed).astype(jnp.bfloat16)
        keep_final = active & (segment_index == segment_count - 1)
        earlier = lax.dynamic_index_in_dim(finished, patch_id, 0, keepdims=False)
        finished = lax.dynamic_update_index_in_dim(
            finished, jnp.where(keep_final, layer_output, earlier), patch_id, 0
        )
        if tick_index + 1 < tick_count:
            received = passed_along(layer_output, "segment", 1)
    final_normed = rms_scaled(finished).astype(jnp.bfloat16)
    predicted = jnp.einsum("mtd,dc->mtc", final_normed, w_final, preferred_element_type=jnp.float32)
    is_last = segment_index == segment_count - 1
    branch_weight = jnp.where(branch_index == 0, 1.0 - guide_scale, guide_scale)
    velocity_term = jnp.where(is_last, branch_weight * predicted, 0.0)
    latent_term = jnp.where(is_last & (branch_index == 0), latent, 0.0)
    velocity_own, latent_own = lax.psum((velocity_term, latent_term), ("segment", "cfg"))
    velocity_full, latent_full = (
        lax.all_gather(velocity_own, "seq", axis=1, tiled=True),
        lax.all_gather(latent_own, "seq", axis=1, tiled=True),
    )
    stepped = latent_full - velocity_full / SCHED_STEPS
    return (velocity_own, decode(stepped, w_conv, slab_rows))


ROWS = MICRO * TOK_DEV
SHIFTS = [(u, dy, dz) for u in range(3) for dy in (-1, 0, 1) for dz in (-1, 0, 1)]
QUARTERS = [
    (a, e, row, col) for a in range(2) for e in range(2) for row in range(2) for col in range(2)
]
MESH = pl.DeviceIdType.MESH


def cuts(*widths):
    edges = [sum(widths[:i]) for i in range(len(widths) + 1)]
    return [slice(a, b) for a, b in zip(edges[:-1], edges[1:])]


LOADS = cuts(768, 768, 768, 768)
PASSES = cuts(512, 512, 512, 512, 512, 512)
RETURNS = cuts(512, 512, 512, 512, 512, 512)
EARLY = 3


def fused_kernel(
    seq_count,
    group_heads,
    lat_hbm,
    order_hbm,
    slab_hbm,
    step_hbm,
    cond_hbm,
    table_hbm,
    conv_hbm,
    emb_hbm,
    qkv_hbm,
    out_hbm,
    stale_hbm,
    fin_hbm,
    vel_ref,
    dec_ref,
    lat_ref,
    order_ref,
    slab_ref,
    step_index,
    cond_ref,
    table,
    conv,
    spread,
    taps,
    feature,
    emb,
    w_qkv,
    w_out,
    stale,
    fin,
    mod_ref,
    bias_ref,
    lat_all,
    staged,
    sums,
    folded,
    attended,
    parts,
    got_first,
    got_second,
    x_own,
    x_second,
    pred_all,
    load_sem,
    qkv_sem,
    lat_send,
    lat_recv,
    first_send,
    first_recv,
    pass_send,
    pass_recv,
    second_send,
    second_recv,
    pred_send,
    pred_recv,
):
    me = lax.axis_index("seq")
    segment = lax.axis_index("segment")
    branch = lax.axis_index("cfg")
    head_rows = 3 * HEAD_DIM
    tokens = seq_count * ROWS
    lanes = lat_ref.shape[-1]
    first = segment == 0
    second = segment == 1
    bf16, f32 = jnp.bfloat16, jnp.float32

    def peer(step):
        return lax.rem(me + step, seq_count)

    def block(index):
        return pl.ds(pl.multiple_of(index * ROWS, ROWS), ROWS)

    barrier = pltpu.get_barrier_semaphore()
    others = [
        (k, a, b) for k in range(seq_count) for a in range(2) for b in range(2) if k + a + b
    ]
    for k, a, b in others:
        where = {
            "seq": peer(k),
            "segment": lax.rem(segment + a, 2),
            "cfg": lax.rem(branch + b, 2),
        }
        pl.semaphore_signal(barrier, inc=1, device_id=where, device_id_type=MESH)

    def load(i, source, target):
        return pltpu.make_async_copy(source, target, load_sem.at[i])

    emb_load = load(0, emb_hbm, emb)
    table_load = load(1, table_hbm, table)
    conv_load = load(2, conv_hbm, conv)
    stale_load = load(3, stale_hbm, stale)
    out_load = load(4, out_hbm, w_out)
    fin_load = load(5, fin_hbm, fin)
    qkv_loads = [
        pltpu.make_async_copy(qkv_hbm.at[:, part], w_qkv.at[:, part], qkv_sem.at[c])
        for c, part in enumerate(LOADS)
    ]
    lat_load = load(6, lat_hbm, lat_ref)
    order_load = load(7, order_hbm, order_ref)
    slab_load = load(8, slab_hbm, slab_ref)
    step_load = load(9, step_hbm, step_index)
    cond_load = load(10, cond_hbm, cond_ref)
    lat_load.start()
    step_load.start()
    cond_load.start()
    table_load.start()
    emb_load.start()
    order_load.start()
    slab_load.start()
    for copy in qkv_loads:
        copy.start()
    conv_load.start()
    stale_load.start()
    out_load.start()
    fin_load.start()

    step_load.wait()
    cond_load.wait()
    table_load.wait()
    plan_row = lax.broadcasted_iota(jnp.int32, table.shape[1:], 0) == step_index[0]
    for i in range(3):
        chosen = jnp.where(plan_row, table[i].astype(f32), 0.0)
        mod_ref[i : i + 1] = jnp.sum(chosen, axis=0, keepdims=True)
    pieces = D // 128
    for i in range(3):
        for j in range(pieces):
            at = slice(j * 128, (j + 1) * 128)
            mod_ref[i : i + 1, at] += cond_ref[i * pieces + j : i * pieces + j + 1]
    staged[tokens:] = jnp.broadcast_to(mod_ref[0:1], (16, D)).astype(bf16)
    lat_load.wait()
    lat_all[me] = lat_ref[...]
    emb_load.wait()

    def project(c, part):
        for head in range(group_heads):
            rows = slice(head * head_rows, (head + 1) * head_rows)
            piece = lax.dot_general(
                staged[:, part],
                w_qkv[rows, part],
                (((1,), (1,)), ((), ())),
                preferred_element_type=f32,
            )
            if c == 0:
                sums[head] = piece
            else:
                sums[head] += piece

    def build_spread():
        conv_load.wait()
        spread[...] = jnp.zeros_like(spread)
        for n, (u, dy, dz) in enumerate(SHIFTS):
            for a, e, row_out, col_out in QUARTERS:
                v, w = 2 * dy + a - row_out + 1, 2 * dz + e - col_out + 1
                if 0 <= v < 3 and 0 <= w < 3:
                    at = n * lanes + (2 * a + e) * LAT_CH
                    to = (2 * row_out + col_out) * conv.shape[2]
                    spread[at : at + LAT_CH, to : to + conv.shape[2]] = conv[9 * u + 3 * v + w]

    def fold(c):
        part = LOADS[c]
        scaled = emb[:, part].astype(f32) * (1.0 + mod_ref[1:2, part])
        staged[0:tokens, part] = scaled.astype(bf16)
        qkv_loads[c].wait()
        project(c, part)

    @pl.when(first)
    def _():
        for c in range(EARLY):
            fold(c)

    pl.semaphore_wait(barrier, len(others))

    def remote(source, target, send, recv, where):
        return pltpu.make_async_remote_copy(
            src_ref=source,
            dst_ref=target,
            send_sem=send,
            recv_sem=recv,
            device_id=where,
            device_id_type=MESH,
        )

    def lat_copy(k, slot):
        return remote(
            lat_ref, lat_all.at[slot], lat_send.at[k], lat_recv.at[slot], {"seq": peer(k)}
        )

    def first_copy(k, c, sender):
        part = PASSES[c]
        return remote(
            parts.at[block(peer(k)), part],
            got_first.at[sender, :, part],
            first_send.at[k, c],
            first_recv.at[sender, c],
            {"seq": peer(k), "segment": 1},
        )

    def pass_copy(k, c, sender):
        rows = block(sender)
        return remote(
            x_second.at[rows, PASSES[c]],
            x_second.at[rows, PASSES[c]],
            pass_send.at[k, c],
            pass_recv.at[sender, c],
            {"seq": peer(k)},
        )

    def second_copy(k, c, sender):
        part = RETURNS[c]
        return remote(
            parts.at[block(peer(k)), part],
            got_second.at[sender, :, part],
            second_send.at[k, c],
            second_recv.at[sender, c],
            {"seq": peer(k)},
        )

    def pred_copy(index, k, a, b, slot, sender_branch):
        return remote(
            pred_all.at[slot, sender_branch],
            pred_all.at[slot, sender_branch],
            pred_send.at[index],
            pred_recv.at[slot, sender_branch],
            {"seq": peer(k), "segment": 1 - a, "cfg": lax.rem(branch + b, 2)},
        )

    for k in range(1, seq_count):
        lat_copy(k, me).start()
    order_load.wait()
    slab_load.wait()
    stale_load.wait()
    row = lax.broadcasted_iota(jnp.int32, bias_ref.shape, 0)
    column = lax.broadcasted_iota(jnp.int32, bias_ref.shape, 1)
    query_patch = (row >> 3) & 1
    fresh = column < tokens
    key_patch = jnp.where(
        fresh, (column >> 3) & 1, jnp.where(column < tokens + tokens // MICRO, 0, 1)
    )
    early = query_patch == order_ref[0]
    same = query_patch == key_patch
    bias_fresh = jnp.where(same, 0.0, jnp.where(early, -1e30, 0.0))
    bias_stale = jnp.where(same, -1e30, jnp.where(early, 0.0, -1e30))
    bias_ref[...] = jnp.where(fresh, bias_fresh, bias_stale)

    def attend(projected):
        scores = []
        for head in range(group_heads):
            key_lanes = slice(head * HEAD_DIM, (head + 1) * HEAD_DIM)
            keys = jnp.concatenate(
                [projected[head][:, HEAD_DIM : 2 * HEAD_DIM], stale[:, key_lanes]], 0
            )
            scores.append(
                lax.dot_general(
                    projected[head][:, :HEAD_DIM],
                    keys,
                    (((1,), (1,)), ((), ())),
                    preferred_element_type=f32,
                )
            )
        scores = jnp.stack(scores) * HEAD_DIM ** (-0.5) + bias_ref[...][None]
        weights = jnp.exp(scores - jnp.max(scores, axis=-1, keepdims=True))
        probs = (weights / jnp.sum(weights, axis=-1, keepdims=True)).astype(bf16)
        for head in range(group_heads):
            key_lanes = slice(head * HEAD_DIM, (head + 1) * HEAD_DIM)
            value_lanes = slice(
                (group_heads + head) * HEAD_DIM, (group_heads + head + 1) * HEAD_DIM
            )
            values = jnp.concatenate(
                [projected[head][:, 2 * HEAD_DIM :], stale[:, value_lanes]], 0
            )
            attended[:, key_lanes] = jnp.dot(
                probs[head], values, preferred_element_type=f32
            ).astype(bf16)

    def mix(part):
        mixed = jnp.dot(attended[...], w_out[:, part], preferred_element_type=f32)
        parts[:, part] = (mixed * mod_ref[2:3, part]).astype(bf16)

    @pl.when(first)
    def _():
        for c in range(EARLY, len(LOADS)):
            fold(c)
        for head in range(group_heads):
            whole = sums[head, 0:lanes]
            upper = whole.astype(bf16)
            folded[head, 0:lanes] = upper
            folded[head, lanes : 2 * lanes] = (whole - upper.astype(f32)).astype(bf16)
        for k in range(1, seq_count):
            lat_copy(k, peer(k)).wait_recv()
        once = lat_all[...].reshape(tokens, lanes).astype(bf16)
        square = jnp.zeros((tokens, 1), f32)
        for part in LOADS:
            wide = jnp.dot(once, emb[:, part], preferred_element_type=f32)
            wide = wide.astype(bf16).astype(f32)
            square = square + jnp.sum(wide * wide, axis=-1, keepdims=True)
        inverse = lax.rsqrt(square / D + norm_eps)
        twice = jnp.concatenate([once, once], 1)
        projected = []
        for head in range(group_heads):
            product = jnp.dot(twice, folded[head], preferred_element_type=f32)
            product = product * inverse + sums[head, tokens : tokens + 1]
            projected.append(product.astype(bf16))
        attend(projected)
        out_load.wait()
        for c, part in enumerate(PASSES):
            mix(part)
            for k in range(seq_count):
                first_copy(k, c, me).start()
        fin_load.wait()
        build_spread()
        for c in range(len(PASSES)):
            for k in range(seq_count):
                first_copy(k, c, me).wait_send()
        for k in range(seq_count):
            for b in range(2):
                slot, sender_branch = peer(k), lax.rem(branch + b, 2)
                pred_copy(0, 0, 0, 0, slot, sender_branch).wait_recv()

    @pl.when(second)
    def _():
        own_latent = lat_ref[...].reshape(ROWS, lanes).astype(bf16)
        for part in LOADS:
            x_own[:, part] = jnp.dot(
                own_latent, emb[:, part], preferred_element_type=f32
            ).astype(bf16)
        for copy in qkv_loads:
            copy.wait()
        build_spread()
        for k in range(1, seq_count):
            lat_copy(k, peer(k)).wait_recv()
        fin_load.wait()
        out_load.wait()
        for c, part in enumerate(PASSES):
            total = x_own[:, part].astype(f32)
            for s in range(seq_count):
                first_copy(0, c, s).wait_recv()
                total = total + got_first[s, :, part].astype(f32)
            x_second[block(me), part] = total.astype(bf16)
            for k in range(1, seq_count):
                pass_copy(k, c, me).start()
        square = jnp.zeros((tokens, 1), f32)
        for c, part in enumerate(PASSES):
            for k in range(1, seq_count):
                pass_copy(k, c, peer(k)).wait_recv()
            wide = x_second[:, part].astype(f32)
            square = square + jnp.sum(wide * wide, axis=-1, keepdims=True)
            staged[0:tokens, part] = (wide * (1.0 + mod_ref[1:2, part])).astype(bf16)
            project(c, part)
        inverse = lax.rsqrt(square / D + norm_eps)
        projected = [
            (sums[head, 0:tokens] * inverse + sums[head, tokens : tokens + 1]).astype(bf16)
            for head in range(group_heads)
        ]
        attend(projected)
        for c, part in enumerate(RETURNS):
            mix(part)
            for k in range(1, seq_count):
                second_copy(k, c, me).start()
        predicted = jnp.zeros((ROWS, lanes), f32)
        square = jnp.zeros((ROWS, 1), f32)
        for c, part in enumerate(RETURNS):
            total = x_second[block(me), part].astype(f32) + parts[block(me), part].astype(f32)
            for k in range(1, seq_count):
                second_copy(k, c, peer(k)).wait_recv()
                total = total + got_second[peer(k), :, part].astype(f32)
            rounded = total.astype(bf16)
            wide = rounded.astype(f32)
            square = square + jnp.sum(wide * wide, axis=-1, keepdims=True)
            predicted = predicted + lax.dot_general(
                rounded, fin[:, part], (((1,), (1,)), ((), ())), preferred_element_type=f32
            )
        predicted = predicted * lax.rsqrt(square / D + norm_eps)
        pred_all[me, branch] = jnp.concatenate([predicted[:TOK_DEV], predicted[TOK_DEV:]], 1)
        targets = [(k, a, b) for k, a, b in others]
        for index, (k, a, b) in enumerate(targets):
            pred_copy(index, k, a, b, me, branch).start()
        for c in range(len(PASSES)):
            for k in range(1, seq_count):
                pass_copy(k, c, me).wait_send()
        for c in range(len(RETURNS)):
            for k in range(1, seq_count):
                second_copy(k, c, me).wait_send()
        for k in range(seq_count):
            for b in range(2):
                if k + b:
                    slot, sender_branch = peer(k), lax.rem(branch + b, 2)
                    pred_copy(0, 0, 0, 0, slot, sender_branch).wait_recv()
        for index, (k, a, b) in enumerate(targets):
            pred_copy(index, k, a, b, me, branch).wait_send()

    def guided(slot):
        return (1.0 - guide_scale) * pred_all[slot, 0] + guide_scale * pred_all[slot, 1]

    velocity = guided(me)
    for p in range(MICRO):
        vel_ref[p] = velocity[:, p * lanes : (p + 1) * lanes]
    steps = [guided(s) / SCHED_STEPS for s in range(seq_count)]
    image = [
        lat_all[s, p] - steps[s][:, p * lanes : (p + 1) * lanes]
        for p in range(MICRO)
        for s in range(seq_count)
    ]
    image = jnp.concatenate(image, 0)
    image = image.astype(bf16).astype(f32)
    rows_deep = tokens // (FRAMES * (LAT_W // 2))
    frame = tokens // FRAMES
    place = lax.broadcasted_iota(jnp.int32, image.shape, 0)
    across = place & (LAT_W // 2 - 1)
    down = (place >> 2) & (rows_deep - 1)
    moved = {}
    for dy in (-1, 0, 1):
        for dz in (-1, 0, 1):
            by = dy * (LAT_W // 2) + dz
            shifted = pltpu.roll(image, (-by) % tokens, 0) if by else image
            if dz == 1:
                shifted = jnp.where(across < LAT_W // 2 - 1, shifted, 0.0)
            if dz == -1:
                shifted = jnp.where(across > 0, shifted, 0.0)
            if dy == 1:
                shifted = jnp.where(down < rows_deep - 1, shifted, 0.0)
            if dy == -1:
                shifted = jnp.where(down > 0, shifted, 0.0)
            moved[dy, dz] = shifted

    def tap(n):
        if n == len(SHIFTS):
            return jnp.zeros_like(image)
        u, dy, dz = SHIFTS[n]
        order = [max(f + u - 2, 0) for f in range(FRAMES)]
        return jnp.concatenate(
            [moved[dy, dz][f * frame : (f + 1) * frame] for f in order], 0
        )

    for pair in range((len(SHIFTS) + 1) // 2):
        both = jnp.concatenate([tap(2 * pair), tap(2 * pair + 1)], 1)
        taps[:, pair * 2 * lanes : (pair + 1) * 2 * lanes] = both.astype(bf16)
    channels = conv.shape[2]
    features = jnp.dot(taps[...], spread[...], preferred_element_type=f32)
    for a in range(2):
        for e in range(2):
            at = (2 * a + e) * channels
            feature[a, pl.ds(e, tokens, stride=2), :] = features[:, at : at + channels]
    start = jnp.int32(0)
    count = jnp.int32(0)
    for s in range(seq_count):
        start = start + jnp.where(s < me, slab_ref[s], 0)
        count = count + jnp.where(s == me, slab_ref[s], 0)
    for k in range(dec_ref.shape[2]):
        keep = [
            jnp.where((start + k == y) & (k < count), 1.0, 0.0) for y in range(2 * rows_deep)
        ]
        for f in range(FRAMES):
            total = jnp.zeros((LAT_W, channels), f32)
            for y in range(2 * rows_deep):
                at = (f * rows_deep + y // 2) * LAT_W
                total = total + keep[y] * feature[y % 2, at : at + LAT_W]
            dec_ref[0, f, k] = total.astype(bf16)

    for k in range(1, seq_count):
        lat_copy(k, me).wait_send()


def handed_over(velocity_in, decoded_in, velocity_out, decoded_out):
    velocity_out[...] = velocity_in[...]
    decoded_out[...] = decoded_in[...]


def shards_fused(
    latent,
    w_embed,
    w_qkv,
    w_out,
    mod_table,
    cond_mod,
    stale_kv,
    w_final,
    w_conv,
    patch_order,
    timestep,
    slab_rows,
):
    seq_count = lax.axis_size("seq")
    group_heads = HEADS // seq_count
    tokens = seq_count * ROWS
    lanes = latent.shape[-1]
    spreads = (len(SHIFTS) + 1) * lanes
    slab_most = 2 * 2 * tokens // (FRAMES * (LAT_W // 2)) // seq_count
    channels = w_conv.shape[2]
    bf16, f32, dma = jnp.bfloat16, jnp.float32, pltpu.SemaphoreType.DMA
    here = pl.BlockSpec(memory_space=pltpu.VMEM)
    away = pl.BlockSpec(memory_space=pl.ANY)
    velocity, decoded = pl.pallas_call(
        functools.partial(fused_kernel, seq_count, group_heads),
        out_shape=(
            jax.ShapeDtypeStruct(latent.shape, f32),
            jax.ShapeDtypeStruct((1, FRAMES, slab_most, LAT_W, channels), bf16),
        ),
        in_specs=[away] * 12,
        out_specs=(here, here),
        scratch_shapes=[
            pltpu.VMEM(latent.shape, f32),
            pltpu.SMEM(patch_order.shape, jnp.int32),
            pltpu.SMEM(slab_rows.shape, jnp.int32),
            pltpu.SMEM(timestep.shape, jnp.int32),
            pltpu.VMEM((3 * D // 128, 128), f32),
            pltpu.VMEM((3, SCHED_STEPS, D), bf16),
            pltpu.VMEM(w_conv.shape, bf16),
            pltpu.VMEM((spreads, 4 * channels), bf16),
            pltpu.VMEM((tokens, spreads), bf16),
            pltpu.VMEM((2, 2 * tokens, channels), f32),
            pltpu.VMEM((lanes, D), bf16),
            pltpu.VMEM((3 * group_heads * HEAD_DIM, D), bf16),
            pltpu.VMEM((group_heads * HEAD_DIM, D), bf16),
            pltpu.VMEM((tokens, 2 * group_heads * HEAD_DIM), bf16),
            pltpu.VMEM((lanes, D), bf16),
            pltpu.VMEM((8, D), f32),
            pltpu.VMEM((tokens, 2 * tokens), f32),
            pltpu.VMEM((seq_count,) + latent.shape, f32),
            pltpu.VMEM((tokens + 16, D), bf16),
            pltpu.VMEM((group_heads, tokens + 16, 3 * HEAD_DIM), f32),
            pltpu.VMEM((group_heads, 2 * lanes, 3 * HEAD_DIM), bf16),
            pltpu.VMEM((tokens, group_heads * HEAD_DIM), bf16),
            pltpu.VMEM((tokens, D), bf16),
            pltpu.VMEM((seq_count, ROWS, D), bf16),
            pltpu.VMEM((seq_count, ROWS, D), bf16),
            pltpu.VMEM((ROWS, D), bf16),
            pltpu.VMEM((tokens, D), bf16),
            pltpu.VMEM((seq_count, 2, TOK_DEV, 2 * lanes), f32),
            dma((11,)),
            dma((len(LOADS),)),
            dma((seq_count,)),
            dma((seq_count,)),
            dma((seq_count, len(PASSES))),
            dma((seq_count, len(PASSES))),
            dma((seq_count, len(PASSES))),
            dma((seq_count, len(PASSES))),
            dma((seq_count, len(RETURNS))),
            dma((seq_count, len(RETURNS))),
            dma((4 * seq_count - 1,)),
            dma((seq_count, 2)),
        ],
        compiler_params=pltpu.CompilerParams(
            collective_id=0, has_side_effects=True, vmem_limit_bytes=60 * 2**20
        ),
        name="denoise",
    )(
        latent,
        patch_order,
        slab_rows,
        timestep,
        cond_mod.reshape(3 * D // 128, 128),
        jnp.transpose(mod_table, (1, 0, 2)),
        w_conv,
        w_embed,
        w_qkv[0],
        w_out[0],
        stale_kv.reshape(tokens, 2 * group_heads * HEAD_DIM),
        w_final.T,
    )
    return pl.pallas_call(
        handed_over,
        out_shape=(
            jax.ShapeDtypeStruct(velocity.shape, f32),
            jax.ShapeDtypeStruct(decoded.shape, bf16),
        ),
        in_specs=[here, here],
        out_specs=(here, here),
        name="results",
    )(velocity, decoded)


def solution(mesh):
    in_specs = (
        P(None, ("groups", "seq"), None),
        P(),
        P("segment", "seq", None),
        P("segment", "seq", None),
        P(),
        P("cfg", ("groups", "segment"), None, None),
        P("segment", "cfg", "seq", None, "groups", None),
        P(),
        P(None, None, ("segment", "cfg")),
        P("groups"),
        P("groups"),
        P("groups"),
    )
    out_specs = (
        P(None, ("groups", "seq"), None),
        P(("groups", "seq"), None, None, None, ("segment", "cfg")),
    )
    small = mesh.shape["seq"] == 4 and mesh.shape["segment"] == 2 and mesh.shape["cfg"] == 2
    shards = shards_fused if small else shards_general
    return jax.shard_map(shards, mesh=mesh, in_specs=in_specs, out_specs=out_specs, check_vma=False)
```

```python
import functools

import jax
import jax.numpy as jnp
from jax import lax
from jax.experimental import pallas as pl
from jax.experimental.pallas import tpu as pltpu
from jax.sharding import PartitionSpec as P

HEADS = 24
HEAD_DIM = 128
D = 3072
LAT_CH = 16
SCHED_STEPS = 50
MICRO = 2
TOK_DEV = 8
FRAMES = 4
LAT_W = 8


guide_scale = 5.0
norm_eps = 1e-06


def swapped(value, axis, bit):
    return lax.ppermute(value, axis, [(i, i ^ 1 << bit) for i in range(lax.axis_size(axis))])


def passed_along(value, axis, by):
    size = lax.axis_size(axis)
    pairs = [(i, i + by) for i in range(size) if 0 <= i + by < size]
    return lax.ppermute(value, axis, pairs)


def rms_scaled(values):
    wide = values.astype(jnp.float32)
    return wide * lax.rsqrt(jnp.mean(wide * wide, axis=-1, keepdims=True) + norm_eps)


def cycle_join(piece, seq_index, cycle_bits):
    joined = piece
    for bit_number in range(cycle_bits):
        partner = swapped(joined, "seq", bit_number)
        upper_half = (seq_index // 2**bit_number % 2).astype(jnp.int32)
        part_rows = joined.shape[0]
        combined = jnp.zeros((2 * part_rows,) + joined.shape[1:], joined.dtype)
        combined = lax.dynamic_update_slice_in_dim(combined, joined, upper_half * part_rows, 0)
        joined = lax.dynamic_update_slice_in_dim(combined, partner, (1 - upper_half) * part_rows, 0)
    return joined


def decode(stepped, w_conv, slab_rows):
    seq_count = lax.axis_size("seq")
    seq_index = lax.axis_index("seq")
    token_rows = MICRO * seq_count * TOK_DEV // (FRAMES * (LAT_W // 2))
    image_rows = 2 * token_rows
    slab_most = 2 * image_rows // seq_count
    image = stepped.reshape(FRAMES, token_rows, LAT_W // 2, 2, 2, LAT_CH)
    image = (
        jnp.transpose(image, (0, 1, 3, 2, 4, 5))
        .reshape(FRAMES, image_rows, LAT_W, LAT_CH)
        .astype(jnp.bfloat16)
    )
    padded = jnp.concatenate([image[:1], image[:1], image], 0)
    padded = jnp.pad(padded, ((0, 0), (1, 1 + slab_most), (1, 1), (0, 0)))
    positions = jnp.arange(seq_count)
    slab_count = jnp.sum(jnp.where(positions == seq_index, slab_rows, 0))
    slab_start = jnp.sum(jnp.where(positions < seq_index, slab_rows, 0))
    window = lax.dynamic_slice_in_dim(padded, slab_start, slab_most + 2, 1)
    pieces = []
    for frame_shift in range(3):
        for row_shift in range(3):
            for col_shift in range(3):
                pieces.append(
                    window[
                        frame_shift : frame_shift + FRAMES,
                        row_shift : row_shift + slab_most,
                        col_shift : col_shift + LAT_W,
                    ]
                )
    columns = jnp.concatenate(pieces, -1).reshape(FRAMES * slab_most * LAT_W, 27 * LAT_CH)
    kernel = w_conv.reshape(27 * LAT_CH, w_conv.shape[2])
    features = jnp.dot(columns, kernel, preferred_element_type=jnp.float32).astype(jnp.bfloat16)
    features = features.reshape(FRAMES, slab_most, LAT_W, w_conv.shape[2])
    row_valid = jnp.arange(slab_most)[None, :, None, None] < slab_count
    decoded = jnp.where(row_valid, features, jnp.zeros_like(features))
    return decoded[None]


def shards_general(
    latent,
    w_embed,
    w_qkv,
    w_out,
    mod_table,
    cond_mod,
    stale_kv,
    w_final,
    w_conv,
    patch_order,
    timestep,
    slab_rows,
):
    seq_count = lax.axis_size("seq")
    segment_count = lax.axis_size("segment")
    seq_index = lax.axis_index("seq")
    segment_index = lax.axis_index("segment")
    branch_index = lax.axis_index("cfg")
    group_count = min(seq_count, 8)
    cycle_size = seq_count // group_count
    cycle_bits = cycle_size.bit_length() - 1
    group_heads = HEADS // group_count
    sub_rows = TOK_DEV // cycle_size
    share_rows = seq_count * sub_rows
    kv_lanes = 2 * group_heads * HEAD_DIM
    table_row = lax.dynamic_index_in_dim(mod_table, timestep[0], 0, keepdims=False).astype(
        jnp.float32
    )
    modulation = table_row + cond_mod[0, 0]
    shift_row = modulation[0]
    scale_row = modulation[1]
    gate_row = modulation[2]
    joined_weights = (
        cycle_join(w_qkv[0], seq_index, cycle_bits),
        cycle_join(w_out[0], seq_index, cycle_bits),
    )
    stale_joined = cycle_join(stale_kv[0, 0], seq_index, cycle_bits)
    cache = jnp.transpose(stale_joined, (1, 0, 2, 3)).reshape(
        MICRO, cycle_size * share_rows, kv_lanes
    )
    received = jnp.zeros((TOK_DEV, D), jnp.bfloat16)
    finished = jnp.zeros((MICRO, TOK_DEV, D), jnp.bfloat16)
    slot_ids = jnp.arange(MICRO)
    tick_count = MICRO + segment_count - 1
    for tick_index in range(tick_count):
        qkv_rows, out_rows = joined_weights
        micro_index = tick_index - segment_index
        active = (micro_index >= 0) & (micro_index < MICRO)
        clipped = jnp.clip(micro_index, 0, MICRO - 1)
        patch_id = jnp.sum(jnp.where(slot_ids == clipped, patch_order, 0))
        own_latent = lax.dynamic_index_in_dim(latent, patch_id, 0, keepdims=False).astype(
            jnp.bfloat16
        )
        embedded = jnp.dot(own_latent, w_embed, preferred_element_type=jnp.float32).astype(
            jnp.bfloat16
        )
        layer_input = jnp.where(segment_index == 0, embedded, received)
        normed = (rms_scaled(layer_input) * (1.0 + scale_row) + shift_row).astype(jnp.bfloat16)
        outgoing = jnp.broadcast_to(
            normed.reshape(1, cycle_size, sub_rows, D), (group_count, cycle_size, sub_rows, D)
        )
        shared = lax.all_to_all(
            outgoing.reshape(share_rows, D), "seq", split_axis=0, concat_axis=0, tiled=True
        )
        projected = lax.dot_general(
            shared, qkv_rows, (((1,), (1,)), ((), ())), preferred_element_type=jnp.float32
        )
        projected = projected.astype(jnp.bfloat16).reshape(share_rows, group_heads, 3, HEAD_DIM)
        queries = projected[:, :, 0]
        fresh_local = jnp.transpose(projected[:, :, 1:], (0, 2, 1, 3)).reshape(
            1, share_rows, kv_lanes
        )
        fresh = cycle_join(fresh_local, seq_index, cycle_bits).reshape(
            cycle_size * share_rows, kv_lanes
        )
        previous = lax.dynamic_index_in_dim(cache, patch_id, 0, keepdims=False)
        cache = lax.dynamic_update_index_in_dim(
            cache, jnp.where(active, fresh, previous), patch_id, 0
        )
        keyvals = cache.reshape(MICRO * cycle_size * share_rows, 2, group_heads, HEAD_DIM)
        scores = jnp.einsum(
            "shd,khd->hsk", queries, keyvals[:, 0], preferred_element_type=jnp.float32
        ) * HEAD_DIM ** (-0.5)
        probs = jax.nn.softmax(scores, axis=-1).astype(jnp.bfloat16)
        attended = jnp.einsum(
            "hsk,khd->shd", probs, keyvals[:, 1], preferred_element_type=jnp.float32
        ).astype(jnp.bfloat16)
        partial_out = jnp.dot(
            attended.reshape(share_rows, group_heads * HEAD_DIM),
            out_rows,
            preferred_element_type=jnp.float32,
        )
        returned = lax.all_to_all(
            partial_out.astype(jnp.bfloat16), "seq", split_axis=0, concat_axis=0, tiled=True
        ).astype(partial_out.dtype)
        mixed = jnp.sum(returned.reshape(group_count, cycle_size, sub_rows, D), axis=0).reshape(
            TOK_DEV, D
        )
        layer_output = (layer_input.astype(jnp.float32) + gate_row * mixed).astype(jnp.bfloat16)
        keep_final = active & (segment_index == segment_count - 1)
        earlier = lax.dynamic_index_in_dim(finished, patch_id, 0, keepdims=False)
        finished = lax.dynamic_update_index_in_dim(
            finished, jnp.where(keep_final, layer_output, earlier), patch_id, 0
        )
        if tick_index + 1 < tick_count:
            received = passed_along(layer_output, "segment", 1)
    final_normed = rms_scaled(finished).astype(jnp.bfloat16)
    predicted = jnp.einsum("mtd,dc->mtc", final_normed, w_final, preferred_element_type=jnp.float32)
    is_last = segment_index == segment_count - 1
    branch_weight = jnp.where(branch_index == 0, 1.0 - guide_scale, guide_scale)
    velocity_term = jnp.where(is_last, branch_weight * predicted, 0.0)
    latent_term = jnp.where(is_last & (branch_index == 0), latent, 0.0)
    velocity_own, latent_own = lax.psum((velocity_term, latent_term), ("segment", "cfg"))
    velocity_full, latent_full = (
        lax.all_gather(velocity_own, "seq", axis=1, tiled=True),
        lax.all_gather(latent_own, "seq", axis=1, tiled=True),
    )
    stepped = latent_full - velocity_full / SCHED_STEPS
    return (velocity_own, decode(stepped, w_conv, slab_rows))


ROWS = MICRO * TOK_DEV
SHIFTS = [(u, dy, dz) for u in range(3) for dy in (-1, 0, 1) for dz in (-1, 0, 1)]
QUARTERS = [
    (a, e, row, col) for a in range(2) for e in range(2) for row in range(2) for col in range(2)
]
MESH = pl.DeviceIdType.MESH


def cuts(*widths):
    edges = [sum(widths[:i]) for i in range(len(widths) + 1)]
    return [slice(a, b) for a, b in zip(edges[:-1], edges[1:])]


LOADS = cuts(512, 512, 512, 512, 512, 512)
PASSES = cuts(512, 512, 512, 512, 512, 512)
RETURNS = cuts(512, 512, 512, 512, 512, 512)
EARLY = 4
RELAYED = 1


def fused_kernel(
    seq_count,
    group_heads,
    lat_hbm,
    order_hbm,
    slab_hbm,
    step_hbm,
    cond_hbm,
    table_hbm,
    conv_hbm,
    emb_hbm,
    qkv_hbm,
    out_hbm,
    stale_hbm,
    fin_hbm,
    vel_ref,
    dec_ref,
    lat_ref,
    order_ref,
    slab_ref,
    step_index,
    cond_ref,
    table,
    conv,
    spread,
    taps,
    feature,
    emb,
    w_qkv,
    w_out,
    stale,
    fin,
    mod_ref,
    bias_ref,
    lat_all,
    staged,
    sums,
    folded,
    attended,
    parts,
    got_first,
    got_second,
    relay,
    x_own,
    x_second,
    pred_all,
    load_sem,
    qkv_sem,
    lat_send,
    lat_recv,
    first_send,
    first_recv,
    pass_send,
    pass_recv,
    second_send,
    second_recv,
    relay_send,
    relay_recv,
    onward_send,
    pred_send,
    pred_recv,
):
    me = lax.axis_index("seq")
    segment = lax.axis_index("segment")
    branch = lax.axis_index("cfg")
    head_rows = 3 * HEAD_DIM
    tokens = seq_count * ROWS
    lanes = lat_ref.shape[-1]
    first = segment == 0
    second = segment == 1
    bf16, f32 = jnp.bfloat16, jnp.float32

    def peer(step):
        return lax.rem(me + step, seq_count)

    def block(index):
        return pl.ds(pl.multiple_of(index * ROWS, ROWS), ROWS)

    barrier = pltpu.get_barrier_semaphore()
    others = [
        (k, a, b) for k in range(seq_count) for a in range(2) for b in range(2) if k + a + b
    ]
    for k, a, b in others:
        where = {
            "seq": peer(k),
            "segment": lax.rem(segment + a, 2),
            "cfg": lax.rem(branch + b, 2),
        }
        pl.semaphore_signal(barrier, inc=1, device_id=where, device_id_type=MESH)

    def load(i, source, target):
        return pltpu.make_async_copy(source, target, load_sem.at[i])

    emb_load = load(0, emb_hbm, emb)
    table_load = load(1, table_hbm, table)
    conv_load = load(2, conv_hbm, conv)
    stale_load = load(3, stale_hbm, stale)
    out_load = load(4, out_hbm, w_out)
    fin_load = load(5, fin_hbm, fin)
    qkv_loads = [
        pltpu.make_async_copy(qkv_hbm.at[:, part], w_qkv.at[:, part], qkv_sem.at[c])
        for c, part in enumerate(LOADS)
    ]
    lat_load = load(6, lat_hbm, lat_ref)
    order_load = load(7, order_hbm, order_ref)
    slab_load = load(8, slab_hbm, slab_ref)
    step_load = load(9, step_hbm, step_index)
    cond_load = load(10, cond_hbm, cond_ref)
    lat_load.start()
    step_load.start()
    cond_load.start()
    table_load.start()
    emb_load.start()
    order_load.start()
    slab_load.start()
    for copy in qkv_loads:
        copy.start()
    conv_load.start()
    stale_load.start()
    out_load.start()
    fin_load.start()

    step_load.wait()
    cond_load.wait()
    table_load.wait()
    plan_row = lax.broadcasted_iota(jnp.int32, table.shape[1:], 0) == step_index[0]
    for i in range(3):
        chosen = jnp.where(plan_row, table[i].astype(f32), 0.0)
        mod_ref[i : i + 1] = jnp.sum(chosen, axis=0, keepdims=True)
    pieces = D // 128
    for i in range(3):
        for j in range(pieces):
            at = slice(j * 128, (j + 1) * 128)
            mod_ref[i : i + 1, at] += cond_ref[i * pieces + j : i * pieces + j + 1]
    staged[tokens:] = jnp.broadcast_to(mod_ref[0:1], (16, D)).astype(bf16)
    lat_load.wait()
    lat_all[me] = lat_ref[...]
    emb_load.wait()

    def project(c, part):
        for head in range(group_heads):
            rows = slice(head * head_rows, (head + 1) * head_rows)
            piece = lax.dot_general(
                staged[:, part],
                w_qkv[rows, part],
                (((1,), (1,)), ((), ())),
                preferred_element_type=f32,
            )
            if c == 0:
                sums[head] = piece
            else:
                sums[head] += piece

    def build_spread():
        conv_load.wait()
        spread[...] = jnp.zeros_like(spread)
        for n, (u, dy, dz) in enumerate(SHIFTS):
            for a, e, row_out, col_out in QUARTERS:
                v, w = 2 * dy + a - row_out + 1, 2 * dz + e - col_out + 1
                if 0 <= v < 3 and 0 <= w < 3:
                    at = n * lanes + (2 * a + e) * LAT_CH
                    to = (2 * row_out + col_out) * conv.shape[2]
                    spread[at : at + LAT_CH, to : to + conv.shape[2]] = conv[9 * u + 3 * v + w]

    def fold(c):
        part = LOADS[c]
        scaled = emb[:, part].astype(f32) * (1.0 + mod_ref[1:2, part])
        staged[0:tokens, part] = scaled.astype(bf16)
        qkv_loads[c].wait()
        project(c, part)

    @pl.when(first)
    def _():
        for c in range(EARLY):
            fold(c)

    pl.semaphore_wait(barrier, len(others))

    def remote(source, target, send, recv, where):
        return pltpu.make_async_remote_copy(
            src_ref=source,
            dst_ref=target,
            send_sem=send,
            recv_sem=recv,
            device_id=where,
            device_id_type=MESH,
        )

    def lat_copy(k, slot):
        return remote(
            lat_ref, lat_all.at[slot], lat_send.at[k], lat_recv.at[slot], {"seq": peer(k)}
        )

    def first_copy(k, c, sender):
        part = PASSES[c]
        return remote(
            parts.at[block(peer(k)), part],
            got_first.at[sender, :, part],
            first_send.at[k, c],
            first_recv.at[sender, c],
            {"seq": peer(k), "segment": 1},
        )

    def pass_copy(k, c, sender):
        rows = block(sender)
        return remote(
            x_second.at[rows, PASSES[c]],
            x_second.at[rows, PASSES[c]],
            pass_send.at[k, c],
            pass_recv.at[sender, c],
            {"seq": peer(k)},
        )

    def second_copy(k, c, sender):
        part = RETURNS[c]
        return remote(
            parts.at[block(peer(k)), part],
            got_second.at[sender, :, part],
            second_send.at[k, c],
            second_recv.at[sender, c],
            {"seq": peer(k)},
        )

    def relay_copy(k, c):
        rows = block(peer(k))
        return remote(
            parts.at[rows, RETURNS[c]],
            relay.at[rows, RETURNS[c]],
            relay_send.at[k, c],
            relay_recv.at[k, c],
            {"segment": 1 - segment},
        )

    def onward_copy(k, c):
        part = RETURNS[c]
        return remote(
            relay.at[block(peer(k)), part],
            got_second.at[me, :, part],
            onward_send.at[k, c],
            second_recv.at[me, c],
            {"seq": peer(k), "segment": 1},
        )

    def pred_copy(index, k, a, b, slot, sender_branch):
        return remote(
            pred_all.at[slot, sender_branch],
            pred_all.at[slot, sender_branch],
            pred_send.at[index],
            pred_recv.at[slot, sender_branch],
            {"seq": peer(k), "segment": 1 - a, "cfg": lax.rem(branch + b, 2)},
        )

    for k in range(1, seq_count):
        lat_copy(k, me).start()
    order_load.wait()
    slab_load.wait()
    stale_load.wait()
    row = lax.broadcasted_iota(jnp.int32, bias_ref.shape, 0)
    column = lax.broadcasted_iota(jnp.int32, bias_ref.shape, 1)
    query_patch = (row >> 3) & 1
    fresh = column < tokens
    key_patch = jnp.where(
        fresh, (column >> 3) & 1, jnp.where(column < tokens + tokens // MICRO, 0, 1)
    )
    early = query_patch == order_ref[0]
    same = query_patch == key_patch
    bias_fresh = jnp.where(same, 0.0, jnp.where(early, -1e30, 0.0))
    bias_stale = jnp.where(same, -1e30, jnp.where(early, 0.0, -1e30))
    bias_ref[...] = jnp.where(fresh, bias_fresh, bias_stale)

    def attend(projected):
        scores = []
        for head in range(group_heads):
            key_lanes = slice(head * HEAD_DIM, (head + 1) * HEAD_DIM)
            keys = jnp.concatenate(
                [projected[head][:, HEAD_DIM : 2 * HEAD_DIM], stale[:, key_lanes]], 0
            )
            scores.append(
                lax.dot_general(
                    projected[head][:, :HEAD_DIM],
                    keys,
                    (((1,), (1,)), ((), ())),
                    preferred_element_type=f32,
                )
            )
        scores = jnp.stack(scores) * HEAD_DIM ** (-0.5) + bias_ref[...][None]
        weights = jnp.exp(scores - jnp.max(scores, axis=-1, keepdims=True))
        probs = (weights / jnp.sum(weights, axis=-1, keepdims=True)).astype(bf16)
        for head in range(group_heads):
            key_lanes = slice(head * HEAD_DIM, (head + 1) * HEAD_DIM)
            value_lanes = slice(
                (group_heads + head) * HEAD_DIM, (group_heads + head + 1) * HEAD_DIM
            )
            values = jnp.concatenate(
                [projected[head][:, 2 * HEAD_DIM :], stale[:, value_lanes]], 0
            )
            attended[:, key_lanes] = jnp.dot(
                probs[head], values, preferred_element_type=f32
            ).astype(bf16)

    def mix(part):
        mixed = jnp.dot(attended[...], w_out[:, part], preferred_element_type=f32)
        parts[:, part] = (mixed * mod_ref[2:3, part]).astype(bf16)

    @pl.when(first)
    def _():
        for c in range(EARLY, len(LOADS)):
            fold(c)
        for head in range(group_heads):
            whole = sums[head, 0:lanes]
            upper = whole.astype(bf16)
            folded[head, 0:lanes] = upper
            folded[head, lanes : 2 * lanes] = (whole - upper.astype(f32)).astype(bf16)
        for k in range(1, seq_count):
            lat_copy(k, peer(k)).wait_recv()
        once = lat_all[...].reshape(tokens, lanes).astype(bf16)
        square = jnp.zeros((tokens, 1), f32)
        for part in LOADS:
            wide = jnp.dot(once, emb[:, part], preferred_element_type=f32)
            wide = wide.astype(bf16).astype(f32)
            square = square + jnp.sum(wide * wide, axis=-1, keepdims=True)
        inverse = lax.rsqrt(square / D + norm_eps)
        twice = jnp.concatenate([once, once], 1)
        projected = []
        for head in range(group_heads):
            product = jnp.dot(twice, folded[head], preferred_element_type=f32)
            product = product * inverse + sums[head, tokens : tokens + 1]
            projected.append(product.astype(bf16))
        attend(projected)
        out_load.wait()
        for c, part in enumerate(PASSES):
            mix(part)
            for k in range(seq_count):
                first_copy(k, c, me).start()
        fin_load.wait()
        build_spread()
        for c in range(len(PASSES)):
            for k in range(seq_count):
                first_copy(k, c, me).wait_send()
        for c in range(RELAYED):
            for k in range(1, seq_count):
                relay_copy(k, c).wait_recv()
                onward_copy(k, c).start()
        for k in range(seq_count):
            for b in range(2):
                slot, sender_branch = peer(k), lax.rem(branch + b, 2)
                pred_copy(0, 0, 0, 0, slot, sender_branch).wait_recv()
        for c in range(RELAYED):
            for k in range(1, seq_count):
                onward_copy(k, c).wait_send()

    @pl.when(second)
    def _():
        own_latent = lat_ref[...].reshape(ROWS, lanes).astype(bf16)
        for part in LOADS:
            x_own[:, part] = jnp.dot(
                own_latent, emb[:, part], preferred_element_type=f32
            ).astype(bf16)
        for copy in qkv_loads:
            copy.wait()
        build_spread()
        for k in range(1, seq_count):
            lat_copy(k, peer(k)).wait_recv()
        fin_load.wait()
        out_load.wait()
        for c, part in enumerate(PASSES):
            total = x_own[:, part].astype(f32)
            for s in range(seq_count):
                first_copy(0, c, s).wait_recv()
                total = total + got_first[s, :, part].astype(f32)
            x_second[block(me), part] = total.astype(bf16)
            for k in range(1, seq_count):
                pass_copy(k, c, me).start()
        square = jnp.zeros((tokens, 1), f32)
        for c, part in enumerate(PASSES):
            for k in range(1, seq_count):
                pass_copy(k, c, peer(k)).wait_recv()
            wide = x_second[:, part].astype(f32)
            square = square + jnp.sum(wide * wide, axis=-1, keepdims=True)
            staged[0:tokens, part] = (wide * (1.0 + mod_ref[1:2, part])).astype(bf16)
            project(c, part)
        inverse = lax.rsqrt(square / D + norm_eps)
        projected = [
            (sums[head, 0:tokens] * inverse + sums[head, tokens : tokens + 1]).astype(bf16)
            for head in range(group_heads)
        ]
        attend(projected)
        for c, part in enumerate(RETURNS):
            mix(part)
            for k in range(1, seq_count):
                (relay_copy(k, c) if c < RELAYED else second_copy(k, c, me)).start()
        predicted = jnp.zeros((ROWS, lanes), f32)
        square = jnp.zeros((ROWS, 1), f32)
        for c in [*range(RELAYED, len(RETURNS)), *range(RELAYED)]:
            part = RETURNS[c]
            total = x_second[block(me), part].astype(f32) + parts[block(me), part].astype(f32)
            for k in range(1, seq_count):
                second_copy(k, c, peer(k)).wait_recv()
                total = total + got_second[peer(k), :, part].astype(f32)
            rounded = total.astype(bf16)
            wide = rounded.astype(f32)
            square = square + jnp.sum(wide * wide, axis=-1, keepdims=True)
            predicted = predicted + lax.dot_general(
                rounded, fin[:, part], (((1,), (1,)), ((), ())), preferred_element_type=f32
            )
        predicted = predicted * lax.rsqrt(square / D + norm_eps)
        pred_all[me, branch] = jnp.concatenate([predicted[:TOK_DEV], predicted[TOK_DEV:]], 1)
        targets = [(k, a, b) for k, a, b in others]
        for index, (k, a, b) in enumerate(targets):
            pred_copy(index, k, a, b, me, branch).start()
        for c in range(len(PASSES)):
            for k in range(1, seq_count):
                pass_copy(k, c, me).wait_send()
        for c in range(len(RETURNS)):
            for k in range(1, seq_count):
                (relay_copy(k, c) if c < RELAYED else second_copy(k, c, me)).wait_send()
        for k in range(seq_count):
            for b in range(2):
                if k + b:
                    slot, sender_branch = peer(k), lax.rem(branch + b, 2)
                    pred_copy(0, 0, 0, 0, slot, sender_branch).wait_recv()
        for index, (k, a, b) in enumerate(targets):
            pred_copy(index, k, a, b, me, branch).wait_send()

    def guided(slot):
        return (1.0 - guide_scale) * pred_all[slot, 0] + guide_scale * pred_all[slot, 1]

    velocity = guided(me)
    for p in range(MICRO):
        vel_ref[p] = velocity[:, p * lanes : (p + 1) * lanes]
    steps = [guided(s) / SCHED_STEPS for s in range(seq_count)]
    image = [
        lat_all[s, p] - steps[s][:, p * lanes : (p + 1) * lanes]
        for p in range(MICRO)
        for s in range(seq_count)
    ]
    image = jnp.concatenate(image, 0)
    image = image.astype(bf16).astype(f32)
    rows_deep = tokens // (FRAMES * (LAT_W // 2))
    frame = tokens // FRAMES
    place = lax.broadcasted_iota(jnp.int32, image.shape, 0)
    across = place & (LAT_W // 2 - 1)
    down = (place >> 2) & (rows_deep - 1)
    moved = {}
    for dy in (-1, 0, 1):
        for dz in (-1, 0, 1):
            by = dy * (LAT_W // 2) + dz
            shifted = pltpu.roll(image, (-by) % tokens, 0) if by else image
            if dz == 1:
                shifted = jnp.where(across < LAT_W // 2 - 1, shifted, 0.0)
            if dz == -1:
                shifted = jnp.where(across > 0, shifted, 0.0)
            if dy == 1:
                shifted = jnp.where(down < rows_deep - 1, shifted, 0.0)
            if dy == -1:
                shifted = jnp.where(down > 0, shifted, 0.0)
            moved[dy, dz] = shifted

    def tap(n):
        if n == len(SHIFTS):
            return jnp.zeros_like(image)
        u, dy, dz = SHIFTS[n]
        order = [max(f + u - 2, 0) for f in range(FRAMES)]
        return jnp.concatenate(
            [moved[dy, dz][f * frame : (f + 1) * frame] for f in order], 0
        )

    for pair in range((len(SHIFTS) + 1) // 2):
        both = jnp.concatenate([tap(2 * pair), tap(2 * pair + 1)], 1)
        taps[:, pair * 2 * lanes : (pair + 1) * 2 * lanes] = both.astype(bf16)
    channels = conv.shape[2]
    features = jnp.dot(taps[...], spread[...], preferred_element_type=f32)
    for a in range(2):
        for e in range(2):
            at = (2 * a + e) * channels
            feature[a, pl.ds(e, tokens, stride=2), :] = features[:, at : at + channels]
    start = jnp.int32(0)
    count = jnp.int32(0)
    for s in range(seq_count):
        start = start + jnp.where(s < me, slab_ref[s], 0)
        count = count + jnp.where(s == me, slab_ref[s], 0)
    for k in range(dec_ref.shape[2]):
        keep = [
            jnp.where((start + k == y) & (k < count), 1.0, 0.0) for y in range(2 * rows_deep)
        ]
        for f in range(FRAMES):
            total = jnp.zeros((LAT_W, channels), f32)
            for y in range(2 * rows_deep):
                at = (f * rows_deep + y // 2) * LAT_W
                total = total + keep[y] * feature[y % 2, at : at + LAT_W]
            dec_ref[0, f, k] = total.astype(bf16)

    for k in range(1, seq_count):
        lat_copy(k, me).wait_send()


def handed_over(velocity_in, decoded_in, velocity_out, decoded_out):
    velocity_out[...] = velocity_in[...]
    decoded_out[...] = decoded_in[...]


def shards_fused(
    latent,
    w_embed,
    w_qkv,
    w_out,
    mod_table,
    cond_mod,
    stale_kv,
    w_final,
    w_conv,
    patch_order,
    timestep,
    slab_rows,
):
    seq_count = lax.axis_size("seq")
    group_heads = HEADS // seq_count
    tokens = seq_count * ROWS
    lanes = latent.shape[-1]
    spreads = (len(SHIFTS) + 1) * lanes
    slab_most = 2 * 2 * tokens // (FRAMES * (LAT_W // 2)) // seq_count
    channels = w_conv.shape[2]
    bf16, f32, dma = jnp.bfloat16, jnp.float32, pltpu.SemaphoreType.DMA
    here = pl.BlockSpec(memory_space=pltpu.VMEM)
    away = pl.BlockSpec(memory_space=pl.ANY)
    velocity, decoded = pl.pallas_call(
        functools.partial(fused_kernel, seq_count, group_heads),
        out_shape=(
            jax.ShapeDtypeStruct(latent.shape, f32),
            jax.ShapeDtypeStruct((1, FRAMES, slab_most, LAT_W, channels), bf16),
        ),
        in_specs=[away] * 12,
        out_specs=(here, here),
        scratch_shapes=[
            pltpu.VMEM(latent.shape, f32),
            pltpu.SMEM(patch_order.shape, jnp.int32),
            pltpu.SMEM(slab_rows.shape, jnp.int32),
            pltpu.SMEM(timestep.shape, jnp.int32),
            pltpu.VMEM((3 * D // 128, 128), f32),
            pltpu.VMEM((3, SCHED_STEPS, D), bf16),
            pltpu.VMEM(w_conv.shape, bf16),
            pltpu.VMEM((spreads, 4 * channels), bf16),
            pltpu.VMEM((tokens, spreads), bf16),
            pltpu.VMEM((2, 2 * tokens, channels), f32),
            pltpu.VMEM((lanes, D), bf16),
            pltpu.VMEM((3 * group_heads * HEAD_DIM, D), bf16),
            pltpu.VMEM((group_heads * HEAD_DIM, D), bf16),
            pltpu.VMEM((tokens, 2 * group_heads * HEAD_DIM), bf16),
            pltpu.VMEM((lanes, D), bf16),
            pltpu.VMEM((8, D), f32),
            pltpu.VMEM((tokens, 2 * tokens), f32),
            pltpu.VMEM((seq_count,) + latent.shape, f32),
            pltpu.VMEM((tokens + 16, D), bf16),
            pltpu.VMEM((group_heads, tokens + 16, 3 * HEAD_DIM), f32),
            pltpu.VMEM((group_heads, 2 * lanes, 3 * HEAD_DIM), bf16),
            pltpu.VMEM((tokens, group_heads * HEAD_DIM), bf16),
            pltpu.VMEM((tokens, D), bf16),
            pltpu.VMEM((seq_count, ROWS, D), bf16),
            pltpu.VMEM((seq_count, ROWS, D), bf16),
            pltpu.VMEM((tokens, RETURNS[RELAYED].start), bf16),
            pltpu.VMEM((ROWS, D), bf16),
            pltpu.VMEM((tokens, D), bf16),
            pltpu.VMEM((seq_count, 2, TOK_DEV, 2 * lanes), f32),
            dma((11,)),
            dma((len(LOADS),)),
            dma((seq_count,)),
            dma((seq_count,)),
            dma((seq_count, len(PASSES))),
            dma((seq_count, len(PASSES))),
            dma((seq_count, len(PASSES))),
            dma((seq_count, len(PASSES))),
            dma((seq_count, len(RETURNS))),
            dma((seq_count, len(RETURNS))),
            dma((seq_count, RELAYED)),
            dma((seq_count, RELAYED)),
            dma((seq_count, RELAYED)),
            dma((4 * seq_count - 1,)),
            dma((seq_count, 2)),
        ],
        compiler_params=pltpu.CompilerParams(
            collective_id=0, has_side_effects=True, vmem_limit_bytes=60 * 2**20
        ),
        name="denoise",
    )(
        latent,
        patch_order,
        slab_rows,
        timestep,
        cond_mod.reshape(3 * D // 128, 128),
        jnp.transpose(mod_table, (1, 0, 2)),
        w_conv,
        w_embed,
        w_qkv[0],
        w_out[0],
        stale_kv.reshape(tokens, 2 * group_heads * HEAD_DIM),
        w_final.T,
    )
    return pl.pallas_call(
        handed_over,
        out_shape=(
            jax.ShapeDtypeStruct(velocity.shape, f32),
            jax.ShapeDtypeStruct(decoded.shape, bf16),
        ),
        in_specs=[here, here],
        out_specs=(here, here),
        name="results",
    )(velocity, decoded)


def solution(mesh):
    in_specs = (
        P(None, ("groups", "seq"), None),
        P(),
        P("segment", "seq", None),
        P("segment", "seq", None),
        P(),
        P("cfg", ("groups", "segment"), None, None),
        P("segment", "cfg", "seq", None, "groups", None),
        P(),
        P(None, None, ("segment", "cfg")),
        P("groups"),
        P("groups"),
        P("groups"),
    )
    out_specs = (
        P(None, ("groups", "seq"), None),
        P(("groups", "seq"), None, None, None, ("segment", "cfg")),
    )
    small = mesh.shape["seq"] == 4 and mesh.shape["segment"] == 2 and mesh.shape["cfg"] == 2
    shards = shards_fused if small else shards_general
    return jax.shard_map(shards, mesh=mesh, in_specs=in_specs, out_specs=out_specs, check_vma=False)
```

```python
import functools

import jax
import jax.numpy as jnp
from jax import lax
from jax.experimental import pallas as pl
from jax.experimental.pallas import tpu as pltpu
from jax.sharding import PartitionSpec as P

HEADS = 24
HEAD_DIM = 128
D = 3072
LAT_CH = 16
SCHED_STEPS = 50
MICRO = 2
TOK_DEV = 8
FRAMES = 4
LAT_W = 8


guide_scale = 5.0
norm_eps = 1e-06


def swapped(value, axis, bit):
    return lax.ppermute(value, axis, [(i, i ^ 1 << bit) for i in range(lax.axis_size(axis))])


def passed_along(value, axis, by):
    size = lax.axis_size(axis)
    pairs = [(i, i + by) for i in range(size) if 0 <= i + by < size]
    return lax.ppermute(value, axis, pairs)


def rms_scaled(values):
    wide = values.astype(jnp.float32)
    return wide * lax.rsqrt(jnp.mean(wide * wide, axis=-1, keepdims=True) + norm_eps)


def cycle_join(piece, seq_index, cycle_bits):
    joined = piece
    for bit_number in range(cycle_bits):
        partner = swapped(joined, "seq", bit_number)
        upper_half = (seq_index // 2**bit_number % 2).astype(jnp.int32)
        part_rows = joined.shape[0]
        combined = jnp.zeros((2 * part_rows,) + joined.shape[1:], joined.dtype)
        combined = lax.dynamic_update_slice_in_dim(combined, joined, upper_half * part_rows, 0)
        joined = lax.dynamic_update_slice_in_dim(combined, partner, (1 - upper_half) * part_rows, 0)
    return joined


def decode(stepped, w_conv, slab_rows):
    seq_count = lax.axis_size("seq")
    seq_index = lax.axis_index("seq")
    token_rows = MICRO * seq_count * TOK_DEV // (FRAMES * (LAT_W // 2))
    image_rows = 2 * token_rows
    slab_most = 2 * image_rows // seq_count
    image = stepped.reshape(FRAMES, token_rows, LAT_W // 2, 2, 2, LAT_CH)
    image = (
        jnp.transpose(image, (0, 1, 3, 2, 4, 5))
        .reshape(FRAMES, image_rows, LAT_W, LAT_CH)
        .astype(jnp.bfloat16)
    )
    padded = jnp.concatenate([image[:1], image[:1], image], 0)
    padded = jnp.pad(padded, ((0, 0), (1, 1 + slab_most), (1, 1), (0, 0)))
    positions = jnp.arange(seq_count)
    slab_count = jnp.sum(jnp.where(positions == seq_index, slab_rows, 0))
    slab_start = jnp.sum(jnp.where(positions < seq_index, slab_rows, 0))
    window = lax.dynamic_slice_in_dim(padded, slab_start, slab_most + 2, 1)
    pieces = []
    for frame_shift in range(3):
        for row_shift in range(3):
            for col_shift in range(3):
                pieces.append(
                    window[
                        frame_shift : frame_shift + FRAMES,
                        row_shift : row_shift + slab_most,
                        col_shift : col_shift + LAT_W,
                    ]
                )
    columns = jnp.concatenate(pieces, -1).reshape(FRAMES * slab_most * LAT_W, 27 * LAT_CH)
    kernel = w_conv.reshape(27 * LAT_CH, w_conv.shape[2])
    features = jnp.dot(columns, kernel, preferred_element_type=jnp.float32).astype(jnp.bfloat16)
    features = features.reshape(FRAMES, slab_most, LAT_W, w_conv.shape[2])
    row_valid = jnp.arange(slab_most)[None, :, None, None] < slab_count
    decoded = jnp.where(row_valid, features, jnp.zeros_like(features))
    return decoded[None]


def shards_general(
    latent,
    w_embed,
    w_qkv,
    w_out,
    mod_table,
    cond_mod,
    stale_kv,
    w_final,
    w_conv,
    patch_order,
    timestep,
    slab_rows,
):
    seq_count = lax.axis_size("seq")
    segment_count = lax.axis_size("segment")
    seq_index = lax.axis_index("seq")
    segment_index = lax.axis_index("segment")
    branch_index = lax.axis_index("cfg")
    group_count = min(seq_count, 8)
    cycle_size = seq_count // group_count
    cycle_bits = cycle_size.bit_length() - 1
    group_heads = HEADS // group_count
    sub_rows = TOK_DEV // cycle_size
    share_rows = seq_count * sub_rows
    kv_lanes = 2 * group_heads * HEAD_DIM
    table_row = lax.dynamic_index_in_dim(mod_table, timestep[0], 0, keepdims=False).astype(
        jnp.float32
    )
    modulation = table_row + cond_mod[0, 0]
    shift_row = modulation[0]
    scale_row = modulation[1]
    gate_row = modulation[2]
    joined_weights = (
        cycle_join(w_qkv[0], seq_index, cycle_bits),
        cycle_join(w_out[0], seq_index, cycle_bits),
    )
    stale_joined = cycle_join(stale_kv[0, 0], seq_index, cycle_bits)
    cache = jnp.transpose(stale_joined, (1, 0, 2, 3)).reshape(
        MICRO, cycle_size * share_rows, kv_lanes
    )
    received = jnp.zeros((TOK_DEV, D), jnp.bfloat16)
    finished = jnp.zeros((MICRO, TOK_DEV, D), jnp.bfloat16)
    slot_ids = jnp.arange(MICRO)
    tick_count = MICRO + segment_count - 1
    for tick_index in range(tick_count):
        qkv_rows, out_rows = joined_weights
        micro_index = tick_index - segment_index
        active = (micro_index >= 0) & (micro_index < MICRO)
        clipped = jnp.clip(micro_index, 0, MICRO - 1)
        patch_id = jnp.sum(jnp.where(slot_ids == clipped, patch_order, 0))
        own_latent = lax.dynamic_index_in_dim(latent, patch_id, 0, keepdims=False).astype(
            jnp.bfloat16
        )
        embedded = jnp.dot(own_latent, w_embed, preferred_element_type=jnp.float32).astype(
            jnp.bfloat16
        )
        layer_input = jnp.where(segment_index == 0, embedded, received)
        normed = (rms_scaled(layer_input) * (1.0 + scale_row) + shift_row).astype(jnp.bfloat16)
        outgoing = jnp.broadcast_to(
            normed.reshape(1, cycle_size, sub_rows, D), (group_count, cycle_size, sub_rows, D)
        )
        shared = lax.all_to_all(
            outgoing.reshape(share_rows, D), "seq", split_axis=0, concat_axis=0, tiled=True
        )
        projected = lax.dot_general(
            shared, qkv_rows, (((1,), (1,)), ((), ())), preferred_element_type=jnp.float32
        )
        projected = projected.astype(jnp.bfloat16).reshape(share_rows, group_heads, 3, HEAD_DIM)
        queries = projected[:, :, 0]
        fresh_local = jnp.transpose(projected[:, :, 1:], (0, 2, 1, 3)).reshape(
            1, share_rows, kv_lanes
        )
        fresh = cycle_join(fresh_local, seq_index, cycle_bits).reshape(
            cycle_size * share_rows, kv_lanes
        )
        previous = lax.dynamic_index_in_dim(cache, patch_id, 0, keepdims=False)
        cache = lax.dynamic_update_index_in_dim(
            cache, jnp.where(active, fresh, previous), patch_id, 0
        )
        keyvals = cache.reshape(MICRO * cycle_size * share_rows, 2, group_heads, HEAD_DIM)
        scores = jnp.einsum(
            "shd,khd->hsk", queries, keyvals[:, 0], preferred_element_type=jnp.float32
        ) * HEAD_DIM ** (-0.5)
        probs = jax.nn.softmax(scores, axis=-1).astype(jnp.bfloat16)
        attended = jnp.einsum(
            "hsk,khd->shd", probs, keyvals[:, 1], preferred_element_type=jnp.float32
        ).astype(jnp.bfloat16)
        partial_out = jnp.dot(
            attended.reshape(share_rows, group_heads * HEAD_DIM),
            out_rows,
            preferred_element_type=jnp.float32,
        )
        returned = lax.all_to_all(
            partial_out.astype(jnp.bfloat16), "seq", split_axis=0, concat_axis=0, tiled=True
        ).astype(partial_out.dtype)
        mixed = jnp.sum(returned.reshape(group_count, cycle_size, sub_rows, D), axis=0).reshape(
            TOK_DEV, D
        )
        layer_output = (layer_input.astype(jnp.float32) + gate_row * mixed).astype(jnp.bfloat16)
        keep_final = active & (segment_index == segment_count - 1)
        earlier = lax.dynamic_index_in_dim(finished, patch_id, 0, keepdims=False)
        finished = lax.dynamic_update_index_in_dim(
            finished, jnp.where(keep_final, layer_output, earlier), patch_id, 0
        )
        if tick_index + 1 < tick_count:
            received = passed_along(layer_output, "segment", 1)
    final_normed = rms_scaled(finished).astype(jnp.bfloat16)
    predicted = jnp.einsum("mtd,dc->mtc", final_normed, w_final, preferred_element_type=jnp.float32)
    is_last = segment_index == segment_count - 1
    branch_weight = jnp.where(branch_index == 0, 1.0 - guide_scale, guide_scale)
    velocity_term = jnp.where(is_last, branch_weight * predicted, 0.0)
    latent_term = jnp.where(is_last & (branch_index == 0), latent, 0.0)
    velocity_own, latent_own = lax.psum((velocity_term, latent_term), ("segment", "cfg"))
    velocity_full, latent_full = (
        lax.all_gather(velocity_own, "seq", axis=1, tiled=True),
        lax.all_gather(latent_own, "seq", axis=1, tiled=True),
    )
    stepped = latent_full - velocity_full / SCHED_STEPS
    return (velocity_own, decode(stepped, w_conv, slab_rows))


ROWS = MICRO * TOK_DEV
SHIFTS = [(u, dy, dz) for u in range(3) for dy in (-1, 0, 1) for dz in (-1, 0, 1)]
QUARTERS = [
    (a, e, row, col) for a in range(2) for e in range(2) for row in range(2) for col in range(2)
]
MESH = pl.DeviceIdType.MESH


def cuts(*widths):
    edges = [sum(widths[:i]) for i in range(len(widths) + 1)]
    return [slice(a, b) for a, b in zip(edges[:-1], edges[1:])]


LOADS = cuts(512, 512, 512, 512, 512, 512)
PASSES = cuts(512, 512, 512, 512, 512, 512)
RETURNS = cuts(512, 512, 512, 512, 512, 512)
EARLY = 4
RELAYED = 1


def fused_kernel(
    seq_count,
    group_heads,
    lat_hbm,
    order_hbm,
    slab_hbm,
    step_hbm,
    cond_hbm,
    table_hbm,
    conv_hbm,
    emb_hbm,
    qkv_hbm,
    out_hbm,
    stale_hbm,
    fin_hbm,
    vel_ref,
    dec_ref,
    lat_ref,
    order_ref,
    slab_ref,
    step_index,
    cond_ref,
    table,
    conv,
    spread,
    taps,
    feature,
    emb,
    w_qkv,
    w_out,
    stale,
    fin,
    mod_ref,
    bias_ref,
    lat_all,
    staged,
    sums,
    folded,
    attended,
    parts,
    got_first,
    got_second,
    relay,
    owned,
    x_own,
    x_second,
    pred_all,
    load_sem,
    qkv_sem,
    lat_send,
    lat_recv,
    first_send,
    first_recv,
    pass_send,
    pass_recv,
    second_send,
    second_recv,
    relay_send,
    relay_recv,
    onward_send,
    pred_send,
    pred_recv,
):
    me = lax.axis_index("seq")
    segment = lax.axis_index("segment")
    branch = lax.axis_index("cfg")
    head_rows = 3 * HEAD_DIM
    tokens = seq_count * ROWS
    lanes = lat_ref.shape[-1]
    first = segment == 0
    second = segment == 1
    bf16, f32 = jnp.bfloat16, jnp.float32

    def peer(step):
        return lax.rem(me + step, seq_count)

    def block(index):
        return pl.ds(pl.multiple_of(index * ROWS, ROWS), ROWS)

    barrier = pltpu.get_barrier_semaphore()
    others = [
        (k, a, b) for k in range(seq_count) for a in range(2) for b in range(2) if k + a + b
    ]
    for k, a, b in others:
        where = {
            "seq": peer(k),
            "segment": lax.rem(segment + a, 2),
            "cfg": lax.rem(branch + b, 2),
        }
        pl.semaphore_signal(barrier, inc=1, device_id=where, device_id_type=MESH)

    def load(i, source, target):
        return pltpu.make_async_copy(source, target, load_sem.at[i])

    emb_load = load(0, emb_hbm, emb)
    table_load = load(1, table_hbm, table)
    conv_load = load(2, conv_hbm, conv)
    stale_load = load(3, stale_hbm, stale)
    out_load = load(4, out_hbm, w_out)
    fin_load = load(5, fin_hbm, fin)
    qkv_loads = [
        pltpu.make_async_copy(qkv_hbm.at[:, part], w_qkv.at[:, part], qkv_sem.at[c])
        for c, part in enumerate(LOADS)
    ]
    lat_load = load(6, lat_hbm, lat_ref)
    order_load = load(7, order_hbm, order_ref)
    slab_load = load(8, slab_hbm, slab_ref)
    step_load = load(9, step_hbm, step_index)
    cond_load = load(10, cond_hbm, cond_ref)
    lat_load.start()
    step_load.start()
    cond_load.start()
    table_load.start()
    emb_load.start()
    order_load.start()
    slab_load.start()
    for copy in qkv_loads:
        copy.start()
    conv_load.start()
    stale_load.start()
    out_load.start()
    fin_load.start()

    step_load.wait()
    cond_load.wait()
    table_load.wait()
    plan_row = lax.broadcasted_iota(jnp.int32, table.shape[1:], 0) == step_index[0]
    pieces = D // 128

    def plan(i):
        chosen = jnp.where(plan_row, table[i].astype(f32), 0.0)
        mod_ref[i : i + 1] = jnp.sum(chosen, axis=0, keepdims=True)
        for j in range(pieces):
            at = slice(j * 128, (j + 1) * 128)
            mod_ref[i : i + 1, at] += cond_ref[i * pieces + j : i * pieces + j + 1]

    plan(0)
    plan(1)
    staged[tokens:] = jnp.broadcast_to(mod_ref[0:1], (16, D)).astype(bf16)
    lat_load.wait()
    lat_all[me] = lat_ref[...]
    emb_load.wait()

    def project(c, part):
        for head in range(group_heads):
            rows = slice(head * head_rows, (head + 1) * head_rows)
            piece = lax.dot_general(
                staged[:, part],
                w_qkv[rows, part],
                (((1,), (1,)), ((), ())),
                preferred_element_type=f32,
            )
            if c == 0:
                sums[head] = piece
            else:
                sums[head] += piece

    def build_spread():
        conv_load.wait()
        spread[...] = jnp.zeros_like(spread)
        for n, (u, dy, dz) in enumerate(SHIFTS):
            for a, e, row_out, col_out in QUARTERS:
                v, w = 2 * dy + a - row_out + 1, 2 * dz + e - col_out + 1
                if 0 <= v < 3 and 0 <= w < 3:
                    at = n * lanes + (2 * a + e) * LAT_CH
                    to = (2 * row_out + col_out) * conv.shape[2]
                    spread[at : at + LAT_CH, to : to + conv.shape[2]] = conv[9 * u + 3 * v + w]

    def fold(c):
        part = LOADS[c]
        scaled = emb[:, part].astype(f32) * (1.0 + mod_ref[1:2, part])
        staged[0:tokens, part] = scaled.astype(bf16)
        qkv_loads[c].wait()
        project(c, part)

    @pl.when(first)
    def _():
        for c in range(EARLY):
            fold(c)

    pl.semaphore_wait(barrier, len(others))

    def remote(source, target, send, recv, where):
        return pltpu.make_async_remote_copy(
            src_ref=source,
            dst_ref=target,
            send_sem=send,
            recv_sem=recv,
            device_id=where,
            device_id_type=MESH,
        )

    def lat_copy(k, slot):
        return remote(
            lat_ref, lat_all.at[slot], lat_send.at[k], lat_recv.at[slot], {"seq": peer(k)}
        )

    def first_copy(k, c, sender):
        part = PASSES[c]
        return remote(
            parts.at[block(peer(k)), part],
            got_first.at[sender, :, part],
            first_send.at[k, c],
            first_recv.at[sender, c],
            {"seq": peer(k), "segment": 1, "cfg": 1 - branch},
        )

    def pass_copy(k, c, sender):
        return remote(
            owned.at[:, PASSES[c]],
            x_second.at[block(sender), PASSES[c]],
            pass_send.at[k, c],
            pass_recv.at[sender, c],
            {"seq": peer(k), "cfg": 1 - branch},
        )

    def second_copy(k, c, sender):
        part = RETURNS[c]
        return remote(
            parts.at[block(peer(k)), part],
            got_second.at[sender, :, part],
            second_send.at[k, c],
            second_recv.at[sender, c],
            {"seq": peer(k), "cfg": 1 - branch},
        )

    def relay_copy(k, c):
        rows = block(peer(k))
        return remote(
            parts.at[rows, RETURNS[c]],
            relay.at[rows, RETURNS[c]],
            relay_send.at[k, c],
            relay_recv.at[k, c],
            {"segment": 1 - segment, "cfg": 1 - branch},
        )

    def onward_copy(k, c):
        part = RETURNS[c]
        return remote(
            relay.at[block(peer(k)), part],
            got_second.at[me, :, part],
            onward_send.at[k, c],
            second_recv.at[me, c],
            {"seq": peer(k), "segment": 1},
        )

    def pred_copy(index, k, a, b, slot, sender_branch):
        return remote(
            pred_all.at[slot, sender_branch],
            pred_all.at[slot, sender_branch],
            pred_send.at[index],
            pred_recv.at[slot, sender_branch],
            {"seq": peer(k), "segment": 1 - a, "cfg": lax.rem(branch + b, 2)},
        )

    for k in range(1, seq_count):
        lat_copy(k, me).start()
    plan(2)
    order_load.wait()
    slab_load.wait()
    stale_load.wait()
    row = lax.broadcasted_iota(jnp.int32, bias_ref.shape, 0)
    column = lax.broadcasted_iota(jnp.int32, bias_ref.shape, 1)
    query_patch = (row >> 3) & 1
    fresh = column < tokens
    key_patch = jnp.where(
        fresh, (column >> 3) & 1, jnp.where(column < tokens + tokens // MICRO, 0, 1)
    )
    early = query_patch == order_ref[0]
    same = query_patch == key_patch
    bias_fresh = jnp.where(same, 0.0, jnp.where(early, -1e30, 0.0))
    bias_stale = jnp.where(same, -1e30, jnp.where(early, 0.0, -1e30))
    bias_ref[...] = jnp.where(fresh, bias_fresh, bias_stale)

    def attend(projected):
        scores = []
        for head in range(group_heads):
            key_lanes = slice(head * HEAD_DIM, (head + 1) * HEAD_DIM)
            keys = jnp.concatenate(
                [projected[head][:, HEAD_DIM : 2 * HEAD_DIM], stale[:, key_lanes]], 0
            )
            scores.append(
                lax.dot_general(
                    projected[head][:, :HEAD_DIM],
                    keys,
                    (((1,), (1,)), ((), ())),
                    preferred_element_type=f32,
                )
            )
        scores = jnp.stack(scores) * HEAD_DIM ** (-0.5) + bias_ref[...][None]
        weights = jnp.exp(scores - jnp.max(scores, axis=-1, keepdims=True))
        probs = (weights / jnp.sum(weights, axis=-1, keepdims=True)).astype(bf16)
        for head in range(group_heads):
            key_lanes = slice(head * HEAD_DIM, (head + 1) * HEAD_DIM)
            value_lanes = slice(
                (group_heads + head) * HEAD_DIM, (group_heads + head + 1) * HEAD_DIM
            )
            values = jnp.concatenate(
                [projected[head][:, 2 * HEAD_DIM :], stale[:, value_lanes]], 0
            )
            attended[:, key_lanes] = jnp.dot(
                probs[head], values, preferred_element_type=f32
            ).astype(bf16)

    def mix(part):
        mixed = jnp.dot(attended[...], w_out[:, part], preferred_element_type=f32)
        parts[:, part] = (mixed * mod_ref[2:3, part]).astype(bf16)

    @pl.when(first)
    def _():
        for c in range(EARLY, len(LOADS)):
            fold(c)
        for head in range(group_heads):
            whole = sums[head, 0:lanes]
            upper = whole.astype(bf16)
            folded[head, 0:lanes] = upper
            folded[head, lanes : 2 * lanes] = (whole - upper.astype(f32)).astype(bf16)
        for k in range(1, seq_count):
            lat_copy(k, peer(k)).wait_recv()
        once = lat_all[...].reshape(tokens, lanes).astype(bf16)
        square = jnp.zeros((tokens, 1), f32)
        for part in LOADS:
            wide = jnp.dot(once, emb[:, part], preferred_element_type=f32)
            wide = wide.astype(bf16).astype(f32)
            square = square + jnp.sum(wide * wide, axis=-1, keepdims=True)
        inverse = lax.rsqrt(square / D + norm_eps)
        twice = jnp.concatenate([once, once], 1)
        projected = []
        for head in range(group_heads):
            product = jnp.dot(twice, folded[head], preferred_element_type=f32)
            product = product * inverse + sums[head, tokens : tokens + 1]
            projected.append(product.astype(bf16))
        attend(projected)
        out_load.wait()
        for c, part in enumerate(PASSES):
            mix(part)
            for k in range(seq_count):
                first_copy(k, c, me).start()
        fin_load.wait()
        build_spread()
        for c in range(len(PASSES)):
            for k in range(seq_count):
                first_copy(k, c, me).wait_send()
        for c in range(RELAYED):
            for k in range(1, seq_count):
                relay_copy(k, c).wait_recv()
                onward_copy(k, c).start()
        for k in range(seq_count):
            for b in range(2):
                slot, sender_branch = peer(k), lax.rem(branch + b, 2)
                pred_copy(0, 0, 0, 0, slot, sender_branch).wait_recv()
        for c in range(RELAYED):
            for k in range(1, seq_count):
                onward_copy(k, c).wait_send()

    @pl.when(second)
    def _():
        own_latent = lat_ref[...].reshape(ROWS, lanes).astype(bf16)
        for part in LOADS:
            x_own[:, part] = jnp.dot(
                own_latent, emb[:, part], preferred_element_type=f32
            ).astype(bf16)
        for copy in qkv_loads:
            copy.wait()
        build_spread()
        for k in range(1, seq_count):
            lat_copy(k, peer(k)).wait_recv()
        fin_load.wait()
        out_load.wait()
        for c, part in enumerate(PASSES):
            total = x_own[:, part].astype(f32)
            for s in range(seq_count):
                first_copy(0, c, s).wait_recv()
                total = total + got_first[s, :, part].astype(f32)
            owned[:, part] = total.astype(bf16)
            for k in (2, 1, 3, 0):
                pass_copy(k, c, me).start()
        square = jnp.zeros((tokens, 1), f32)
        for c, part in enumerate(PASSES):
            for k in range(seq_count):
                pass_copy(k, c, peer(k)).wait_recv()
            wide = x_second[:, part].astype(f32)
            square = square + jnp.sum(wide * wide, axis=-1, keepdims=True)
            staged[0:tokens, part] = (wide * (1.0 + mod_ref[1:2, part])).astype(bf16)
            project(c, part)
        inverse = lax.rsqrt(square / D + norm_eps)
        projected = [
            (sums[head, 0:tokens] * inverse + sums[head, tokens : tokens + 1]).astype(bf16)
            for head in range(group_heads)
        ]
        attend(projected)
        for c, part in enumerate(RETURNS):
            mix(part)
            for k in (2, 1, 3, 0):
                (relay_copy(k, c) if k and c < RELAYED else second_copy(k, c, me)).start()
        predicted = jnp.zeros((ROWS, lanes), f32)
        square = jnp.zeros((ROWS, 1), f32)
        for c in [*range(RELAYED, len(RETURNS)), *range(RELAYED)]:
            part = RETURNS[c]
            total = owned[:, part].astype(f32)
            for k in range(seq_count):
                second_copy(k, c, peer(k)).wait_recv()
                total = total + got_second[peer(k), :, part].astype(f32)
            rounded = total.astype(bf16)
            wide = rounded.astype(f32)
            square = square + jnp.sum(wide * wide, axis=-1, keepdims=True)
            predicted = predicted + lax.dot_general(
                rounded, fin[:, part], (((1,), (1,)), ((), ())), preferred_element_type=f32
            )
        predicted = predicted * lax.rsqrt(square / D + norm_eps)
        pred_all[me, 1 - branch] = jnp.concatenate([predicted[:TOK_DEV], predicted[TOK_DEV:]], 1)
        targets = sorted(others, key=lambda t: (t[0] == 0, t[1] == 0, t[0] != 2))
        for index, (k, a, b) in enumerate(targets):
            pred_copy(index, k, a, b, me, 1 - branch).start()
        for c in range(len(PASSES)):
            for k in range(seq_count):
                pass_copy(k, c, me).wait_send()
        for c in range(len(RETURNS)):
            for k in range(seq_count):
                (relay_copy(k, c) if k and c < RELAYED else second_copy(k, c, me)).wait_send()
        for k in range(seq_count):
            for b in range(2):
                if k + b:
                    slot, sender_branch = peer(k), lax.rem(1 - branch + b, 2)
                    pred_copy(0, 0, 0, 0, slot, sender_branch).wait_recv()
        for index, (k, a, b) in enumerate(targets):
            pred_copy(index, k, a, b, me, 1 - branch).wait_send()

    def guided(slot):
        return (1.0 - guide_scale) * pred_all[slot, 0] + guide_scale * pred_all[slot, 1]

    velocity = guided(me)
    for p in range(MICRO):
        vel_ref[p] = velocity[:, p * lanes : (p + 1) * lanes]
    steps = [guided(s) / SCHED_STEPS for s in range(seq_count)]
    image = [
        lat_all[s, p] - steps[s][:, p * lanes : (p + 1) * lanes]
        for p in range(MICRO)
        for s in range(seq_count)
    ]
    image = jnp.concatenate(image, 0)
    image = image.astype(bf16).astype(f32)
    rows_deep = tokens // (FRAMES * (LAT_W // 2))
    frame = tokens // FRAMES
    place = lax.broadcasted_iota(jnp.int32, image.shape, 0)
    across = place & (LAT_W // 2 - 1)
    down = (place >> 2) & (rows_deep - 1)
    moved = {}
    for dy in (-1, 0, 1):
        for dz in (-1, 0, 1):
            by = dy * (LAT_W // 2) + dz
            shifted = pltpu.roll(image, (-by) % tokens, 0) if by else image
            if dz == 1:
                shifted = jnp.where(across < LAT_W // 2 - 1, shifted, 0.0)
            if dz == -1:
                shifted = jnp.where(across > 0, shifted, 0.0)
            if dy == 1:
                shifted = jnp.where(down < rows_deep - 1, shifted, 0.0)
            if dy == -1:
                shifted = jnp.where(down > 0, shifted, 0.0)
            moved[dy, dz] = shifted

    def tap(n):
        if n == len(SHIFTS):
            return jnp.zeros_like(image)
        u, dy, dz = SHIFTS[n]
        order = [max(f + u - 2, 0) for f in range(FRAMES)]
        return jnp.concatenate(
            [moved[dy, dz][f * frame : (f + 1) * frame] for f in order], 0
        )

    for pair in range((len(SHIFTS) + 1) // 2):
        both = jnp.concatenate([tap(2 * pair), tap(2 * pair + 1)], 1)
        taps[:, pair * 2 * lanes : (pair + 1) * 2 * lanes] = both.astype(bf16)
    channels = conv.shape[2]
    features = jnp.dot(taps[...], spread[...], preferred_element_type=f32)
    for a in range(2):
        for e in range(2):
            at = (2 * a + e) * channels
            feature[a, pl.ds(e, tokens, stride=2), :] = features[:, at : at + channels]
    start = jnp.int32(0)
    count = jnp.int32(0)
    for s in range(seq_count):
        start = start + jnp.where(s < me, slab_ref[s], 0)
        count = count + jnp.where(s == me, slab_ref[s], 0)
    for k in range(dec_ref.shape[2]):
        keep = [
            jnp.where((start + k == y) & (k < count), 1.0, 0.0) for y in range(2 * rows_deep)
        ]
        for f in range(FRAMES):
            total = jnp.zeros((LAT_W, channels), f32)
            for y in range(2 * rows_deep):
                at = (f * rows_deep + y // 2) * LAT_W
                total = total + keep[y] * feature[y % 2, at : at + LAT_W]
            dec_ref[0, f, k] = total.astype(bf16)

    for k in range(1, seq_count):
        lat_copy(k, me).wait_send()


def handed_over(velocity_in, decoded_in, velocity_out, decoded_out):
    velocity_out[...] = velocity_in[...]
    decoded_out[...] = decoded_in[...]


def shards_fused(
    latent,
    w_embed,
    w_qkv,
    w_out,
    mod_table,
    cond_mod,
    stale_kv,
    w_final,
    w_conv,
    patch_order,
    timestep,
    slab_rows,
):
    seq_count = lax.axis_size("seq")
    group_heads = HEADS // seq_count
    tokens = seq_count * ROWS
    lanes = latent.shape[-1]
    spreads = (len(SHIFTS) + 1) * lanes
    slab_most = 2 * 2 * tokens // (FRAMES * (LAT_W // 2)) // seq_count
    channels = w_conv.shape[2]
    bf16, f32, dma = jnp.bfloat16, jnp.float32, pltpu.SemaphoreType.DMA
    here = pl.BlockSpec(memory_space=pltpu.VMEM)
    away = pl.BlockSpec(memory_space=pl.ANY)
    velocity, decoded = pl.pallas_call(
        functools.partial(fused_kernel, seq_count, group_heads),
        out_shape=(
            jax.ShapeDtypeStruct(latent.shape, f32),
            jax.ShapeDtypeStruct((1, FRAMES, slab_most, LAT_W, channels), bf16),
        ),
        in_specs=[away] * 12,
        out_specs=(here, here),
        scratch_shapes=[
            pltpu.VMEM(latent.shape, f32),
            pltpu.SMEM(patch_order.shape, jnp.int32),
            pltpu.SMEM(slab_rows.shape, jnp.int32),
            pltpu.SMEM(timestep.shape, jnp.int32),
            pltpu.VMEM((3 * D // 128, 128), f32),
            pltpu.VMEM((3, SCHED_STEPS, D), bf16),
            pltpu.VMEM(w_conv.shape, bf16),
            pltpu.VMEM((spreads, 4 * channels), bf16),
            pltpu.VMEM((tokens, spreads), bf16),
            pltpu.VMEM((2, 2 * tokens, channels), f32),
            pltpu.VMEM((lanes, D), bf16),
            pltpu.VMEM((3 * group_heads * HEAD_DIM, D), bf16),
            pltpu.VMEM((group_heads * HEAD_DIM, D), bf16),
            pltpu.VMEM((tokens, 2 * group_heads * HEAD_DIM), bf16),
            pltpu.VMEM((lanes, D), bf16),
            pltpu.VMEM((8, D), f32),
            pltpu.VMEM((tokens, 2 * tokens), f32),
            pltpu.VMEM((seq_count,) + latent.shape, f32),
            pltpu.VMEM((tokens + 16, D), bf16),
            pltpu.VMEM((group_heads, tokens + 16, 3 * HEAD_DIM), f32),
            pltpu.VMEM((group_heads, 2 * lanes, 3 * HEAD_DIM), bf16),
            pltpu.VMEM((tokens, group_heads * HEAD_DIM), bf16),
            pltpu.VMEM((tokens, D), bf16),
            pltpu.VMEM((seq_count, ROWS, D), bf16),
            pltpu.VMEM((seq_count, ROWS, D), bf16),
            pltpu.VMEM((tokens, RETURNS[RELAYED].start), bf16),
            pltpu.VMEM((ROWS, D), bf16),
            pltpu.VMEM((ROWS, D), bf16),
            pltpu.VMEM((tokens, D), bf16),
            pltpu.VMEM((seq_count, 2, TOK_DEV, 2 * lanes), f32),
            dma((11,)),
            dma((len(LOADS),)),
            dma((seq_count,)),
            dma((seq_count,)),
            dma((seq_count, len(PASSES))),
            dma((seq_count, len(PASSES))),
            dma((seq_count, len(PASSES))),
            dma((seq_count, len(PASSES))),
            dma((seq_count, len(RETURNS))),
            dma((seq_count, len(RETURNS))),
            dma((seq_count, RELAYED)),
            dma((seq_count, RELAYED)),
            dma((seq_count, RELAYED)),
            dma((4 * seq_count - 1,)),
            dma((seq_count, 2)),
        ],
        compiler_params=pltpu.CompilerParams(
            collective_id=0, has_side_effects=True, vmem_limit_bytes=60 * 2**20
        ),
        name="denoise",
    )(
        latent,
        patch_order,
        slab_rows,
        timestep,
        cond_mod.reshape(3 * D // 128, 128),
        jnp.transpose(mod_table, (1, 0, 2)),
        w_conv,
        w_embed,
        w_qkv[0],
        w_out[0],
        stale_kv.reshape(tokens, 2 * group_heads * HEAD_DIM),
        w_final.T,
    )
    return pl.pallas_call(
        handed_over,
        out_shape=(
            jax.ShapeDtypeStruct(velocity.shape, f32),
            jax.ShapeDtypeStruct(decoded.shape, bf16),
        ),
        in_specs=[here, here],
        out_specs=(here, here),
        name="results",
    )(velocity, decoded)


def solution(mesh):
    in_specs = (
        P(None, ("groups", "seq"), None),
        P(),
        P("segment", "seq", None),
        P("segment", "seq", None),
        P(),
        P("cfg", ("groups", "segment"), None, None),
        P("segment", "cfg", "seq", None, "groups", None),
        P(),
        P(None, None, ("segment", "cfg")),
        P("groups"),
        P("groups"),
        P("groups"),
    )
    out_specs = (
        P(None, ("groups", "seq"), None),
        P(("groups", "seq"), None, None, None, ("segment", "cfg")),
    )
    small = mesh.shape["seq"] == 4 and mesh.shape["segment"] == 2 and mesh.shape["cfg"] == 2
    shards = shards_fused if small else shards_general
    return jax.shard_map(shards, mesh=mesh, in_specs=in_specs, out_specs=out_specs, check_vma=False)
```

```python
import functools

import jax
import jax.numpy as jnp
from jax import lax
from jax.experimental import pallas as pl
from jax.experimental.pallas import tpu as pltpu
from jax.sharding import PartitionSpec as P

HEADS = 24
HEAD_DIM = 128
D = 3072
LAT_CH = 16
SCHED_STEPS = 50
MICRO = 2
TOK_DEV = 8
FRAMES = 4
LAT_W = 8


guide_scale = 5.0
norm_eps = 1e-06


def swapped(value, axis, bit):
    return lax.ppermute(value, axis, [(i, i ^ 1 << bit) for i in range(lax.axis_size(axis))])


def passed_along(value, axis, by):
    size = lax.axis_size(axis)
    pairs = [(i, i + by) for i in range(size) if 0 <= i + by < size]
    return lax.ppermute(value, axis, pairs)


def rms_scaled(values):
    wide = values.astype(jnp.float32)
    return wide * lax.rsqrt(jnp.mean(wide * wide, axis=-1, keepdims=True) + norm_eps)


def cycle_join(piece, seq_index, cycle_bits):
    joined = piece
    for bit_number in range(cycle_bits):
        partner = swapped(joined, "seq", bit_number)
        upper_half = (seq_index // 2**bit_number % 2).astype(jnp.int32)
        part_rows = joined.shape[0]
        combined = jnp.zeros((2 * part_rows,) + joined.shape[1:], joined.dtype)
        combined = lax.dynamic_update_slice_in_dim(combined, joined, upper_half * part_rows, 0)
        joined = lax.dynamic_update_slice_in_dim(combined, partner, (1 - upper_half) * part_rows, 0)
    return joined


def decode(stepped, w_conv, slab_rows):
    seq_count = lax.axis_size("seq")
    seq_index = lax.axis_index("seq")
    token_rows = MICRO * seq_count * TOK_DEV // (FRAMES * (LAT_W // 2))
    image_rows = 2 * token_rows
    slab_most = 2 * image_rows // seq_count
    image = stepped.reshape(FRAMES, token_rows, LAT_W // 2, 2, 2, LAT_CH)
    image = (
        jnp.transpose(image, (0, 1, 3, 2, 4, 5))
        .reshape(FRAMES, image_rows, LAT_W, LAT_CH)
        .astype(jnp.bfloat16)
    )
    padded = jnp.concatenate([image[:1], image[:1], image], 0)
    padded = jnp.pad(padded, ((0, 0), (1, 1 + slab_most), (1, 1), (0, 0)))
    positions = jnp.arange(seq_count)
    slab_count = jnp.sum(jnp.where(positions == seq_index, slab_rows, 0))
    slab_start = jnp.sum(jnp.where(positions < seq_index, slab_rows, 0))
    window = lax.dynamic_slice_in_dim(padded, slab_start, slab_most + 2, 1)
    pieces = []
    for frame_shift in range(3):
        for row_shift in range(3):
            for col_shift in range(3):
                pieces.append(
                    window[
                        frame_shift : frame_shift + FRAMES,
                        row_shift : row_shift + slab_most,
                        col_shift : col_shift + LAT_W,
                    ]
                )
    columns = jnp.concatenate(pieces, -1).reshape(FRAMES * slab_most * LAT_W, 27 * LAT_CH)
    kernel = w_conv.reshape(27 * LAT_CH, w_conv.shape[2])
    features = jnp.dot(columns, kernel, preferred_element_type=jnp.float32).astype(jnp.bfloat16)
    features = features.reshape(FRAMES, slab_most, LAT_W, w_conv.shape[2])
    row_valid = jnp.arange(slab_most)[None, :, None, None] < slab_count
    decoded = jnp.where(row_valid, features, jnp.zeros_like(features))
    return decoded[None]


def shards_general(
    latent,
    w_embed,
    w_qkv,
    w_out,
    mod_table,
    cond_mod,
    stale_kv,
    w_final,
    w_conv,
    patch_order,
    timestep,
    slab_rows,
):
    seq_count = lax.axis_size("seq")
    segment_count = lax.axis_size("segment")
    seq_index = lax.axis_index("seq")
    segment_index = lax.axis_index("segment")
    branch_index = lax.axis_index("cfg")
    group_count = min(seq_count, 8)
    cycle_size = seq_count // group_count
    cycle_bits = cycle_size.bit_length() - 1
    group_heads = HEADS // group_count
    sub_rows = TOK_DEV // cycle_size
    share_rows = seq_count * sub_rows
    kv_lanes = 2 * group_heads * HEAD_DIM
    table_row = lax.dynamic_index_in_dim(mod_table, timestep[0], 0, keepdims=False).astype(
        jnp.float32
    )
    modulation = table_row + cond_mod[0, 0]
    shift_row = modulation[0]
    scale_row = modulation[1]
    gate_row = modulation[2]
    joined_weights = (
        cycle_join(w_qkv[0], seq_index, cycle_bits),
        cycle_join(w_out[0], seq_index, cycle_bits),
    )
    stale_joined = cycle_join(stale_kv[0, 0], seq_index, cycle_bits)
    cache = jnp.transpose(stale_joined, (1, 0, 2, 3)).reshape(
        MICRO, cycle_size * share_rows, kv_lanes
    )
    received = jnp.zeros((TOK_DEV, D), jnp.bfloat16)
    finished = jnp.zeros((MICRO, TOK_DEV, D), jnp.bfloat16)
    slot_ids = jnp.arange(MICRO)
    tick_count = MICRO + segment_count - 1
    for tick_index in range(tick_count):
        qkv_rows, out_rows = joined_weights
        micro_index = tick_index - segment_index
        active = (micro_index >= 0) & (micro_index < MICRO)
        clipped = jnp.clip(micro_index, 0, MICRO - 1)
        patch_id = jnp.sum(jnp.where(slot_ids == clipped, patch_order, 0))
        own_latent = lax.dynamic_index_in_dim(latent, patch_id, 0, keepdims=False).astype(
            jnp.bfloat16
        )
        embedded = jnp.dot(own_latent, w_embed, preferred_element_type=jnp.float32).astype(
            jnp.bfloat16
        )
        layer_input = jnp.where(segment_index == 0, embedded, received)
        normed = (rms_scaled(layer_input) * (1.0 + scale_row) + shift_row).astype(jnp.bfloat16)
        outgoing = jnp.broadcast_to(
            normed.reshape(1, cycle_size, sub_rows, D), (group_count, cycle_size, sub_rows, D)
        )
        shared = lax.all_to_all(
            outgoing.reshape(share_rows, D), "seq", split_axis=0, concat_axis=0, tiled=True
        )
        projected = lax.dot_general(
            shared, qkv_rows, (((1,), (1,)), ((), ())), preferred_element_type=jnp.float32
        )
        projected = projected.astype(jnp.bfloat16).reshape(share_rows, group_heads, 3, HEAD_DIM)
        queries = projected[:, :, 0]
        fresh_local = jnp.transpose(projected[:, :, 1:], (0, 2, 1, 3)).reshape(
            1, share_rows, kv_lanes
        )
        fresh = cycle_join(fresh_local, seq_index, cycle_bits).reshape(
            cycle_size * share_rows, kv_lanes
        )
        previous = lax.dynamic_index_in_dim(cache, patch_id, 0, keepdims=False)
        cache = lax.dynamic_update_index_in_dim(
            cache, jnp.where(active, fresh, previous), patch_id, 0
        )
        keyvals = cache.reshape(MICRO * cycle_size * share_rows, 2, group_heads, HEAD_DIM)
        scores = jnp.einsum(
            "shd,khd->hsk", queries, keyvals[:, 0], preferred_element_type=jnp.float32
        ) * HEAD_DIM ** (-0.5)
        probs = jax.nn.softmax(scores, axis=-1).astype(jnp.bfloat16)
        attended = jnp.einsum(
            "hsk,khd->shd", probs, keyvals[:, 1], preferred_element_type=jnp.float32
        ).astype(jnp.bfloat16)
        partial_out = jnp.dot(
            attended.reshape(share_rows, group_heads * HEAD_DIM),
            out_rows,
            preferred_element_type=jnp.float32,
        )
        returned = lax.all_to_all(
            partial_out.astype(jnp.bfloat16), "seq", split_axis=0, concat_axis=0, tiled=True
        ).astype(partial_out.dtype)
        mixed = jnp.sum(returned.reshape(group_count, cycle_size, sub_rows, D), axis=0).reshape(
            TOK_DEV, D
        )
        layer_output = (layer_input.astype(jnp.float32) + gate_row * mixed).astype(jnp.bfloat16)
        keep_final = active & (segment_index == segment_count - 1)
        earlier = lax.dynamic_index_in_dim(finished, patch_id, 0, keepdims=False)
        finished = lax.dynamic_update_index_in_dim(
            finished, jnp.where(keep_final, layer_output, earlier), patch_id, 0
        )
        if tick_index + 1 < tick_count:
            received = passed_along(layer_output, "segment", 1)
    final_normed = rms_scaled(finished).astype(jnp.bfloat16)
    predicted = jnp.einsum("mtd,dc->mtc", final_normed, w_final, preferred_element_type=jnp.float32)
    is_last = segment_index == segment_count - 1
    branch_weight = jnp.where(branch_index == 0, 1.0 - guide_scale, guide_scale)
    velocity_term = jnp.where(is_last, branch_weight * predicted, 0.0)
    latent_term = jnp.where(is_last & (branch_index == 0), latent, 0.0)
    velocity_own, latent_own = lax.psum((velocity_term, latent_term), ("segment", "cfg"))
    velocity_full, latent_full = (
        lax.all_gather(velocity_own, "seq", axis=1, tiled=True),
        lax.all_gather(latent_own, "seq", axis=1, tiled=True),
    )
    stepped = latent_full - velocity_full / SCHED_STEPS
    return (velocity_own, decode(stepped, w_conv, slab_rows))


ROWS = MICRO * TOK_DEV
SHIFTS = [(u, dy, dz) for u in range(3) for dy in (-1, 0, 1) for dz in (-1, 0, 1)]
QUARTERS = [
    (a, e, row, col) for a in range(2) for e in range(2) for row in range(2) for col in range(2)
]
MESH = pl.DeviceIdType.MESH


def cuts(*widths):
    edges = [sum(widths[:i]) for i in range(len(widths) + 1)]
    return [slice(a, b) for a, b in zip(edges[:-1], edges[1:])]


LOADS = cuts(512, 512, 512, 512, 512, 512)
PASSES = cuts(512, 512, 512, 512, 512, 512)
RETURNS = cuts(768, 512, 512, 512, 512, 256)
EARLY = 4
RELAYED = 1


def fused_kernel(
    seq_count,
    group_heads,
    lat_hbm,
    order_hbm,
    slab_hbm,
    step_hbm,
    cond_hbm,
    table_hbm,
    conv_hbm,
    emb_hbm,
    qkv_hbm,
    out_hbm,
    stale_hbm,
    fin_hbm,
    vel_ref,
    dec_ref,
    lat_ref,
    order_ref,
    slab_ref,
    step_index,
    cond_ref,
    table,
    conv,
    spread,
    taps,
    feature,
    emb,
    w_qkv,
    w_out,
    stale,
    fin,
    mod_ref,
    bias_ref,
    lat_all,
    staged,
    sums,
    folded,
    attended,
    parts,
    got_first,
    got_second,
    relay,
    owned,
    x_own,
    x_second,
    pred_all,
    load_sem,
    qkv_sem,
    lat_send,
    lat_recv,
    first_send,
    first_recv,
    pass_send,
    pass_recv,
    second_send,
    second_recv,
    relay_send,
    relay_recv,
    onward_send,
    pred_send,
    pred_recv,
):
    me = lax.axis_index("seq")
    segment = lax.axis_index("segment")
    branch = lax.axis_index("cfg")
    head_rows = 3 * HEAD_DIM
    tokens = seq_count * ROWS
    lanes = lat_ref.shape[-1]
    first = segment == 0
    second = segment == 1
    bf16, f32 = jnp.bfloat16, jnp.float32

    def peer(step):
        return lax.rem(me + step, seq_count)

    def block(index):
        return pl.ds(pl.multiple_of(index * ROWS, ROWS), ROWS)

    barrier = pltpu.get_barrier_semaphore()
    others = [
        (k, a, b) for k in range(seq_count) for a in range(2) for b in range(2) if k + a + b
    ]
    for k, a, b in others:
        where = {
            "seq": peer(k),
            "segment": lax.rem(segment + a, 2),
            "cfg": lax.rem(branch + b, 2),
        }
        pl.semaphore_signal(barrier, inc=1, device_id=where, device_id_type=MESH)

    def load(i, source, target):
        return pltpu.make_async_copy(source, target, load_sem.at[i])

    emb_load = load(0, emb_hbm, emb)
    table_load = load(1, table_hbm, table)
    conv_load = load(2, conv_hbm, conv)
    stale_load = load(3, stale_hbm, stale)
    out_load = load(4, out_hbm, w_out)
    fin_load = load(5, fin_hbm, fin)
    qkv_loads = [
        pltpu.make_async_copy(qkv_hbm.at[:, part], w_qkv.at[:, part], qkv_sem.at[c])
        for c, part in enumerate(LOADS)
    ]
    lat_load = load(6, lat_hbm, lat_ref)
    order_load = load(7, order_hbm, order_ref)
    slab_load = load(8, slab_hbm, slab_ref)
    step_load = load(9, step_hbm, step_index)
    cond_load = load(10, cond_hbm, cond_ref)
    lat_load.start()
    step_load.start()
    cond_load.start()
    table_load.start()
    emb_load.start()
    order_load.start()
    slab_load.start()
    for copy in qkv_loads:
        copy.start()
    conv_load.start()
    stale_load.start()
    out_load.start()
    fin_load.start()

    step_load.wait()
    cond_load.wait()
    table_load.wait()
    plan_row = lax.broadcasted_iota(jnp.int32, table.shape[1:], 0) == step_index[0]
    pieces = D // 128

    def plan(i):
        chosen = jnp.where(plan_row, table[i].astype(f32), 0.0)
        mod_ref[i : i + 1] = jnp.sum(chosen, axis=0, keepdims=True)
        for j in range(pieces):
            at = slice(j * 128, (j + 1) * 128)
            mod_ref[i : i + 1, at] += cond_ref[i * pieces + j : i * pieces + j + 1]

    plan(0)
    plan(1)
    staged[tokens:] = jnp.broadcast_to(mod_ref[0:1], (16, D)).astype(bf16)
    lat_load.wait()
    lat_all[me] = lat_ref[...]
    emb_load.wait()

    def project(c, part):
        for head in range(group_heads):
            rows = slice(head * head_rows, (head + 1) * head_rows)
            piece = lax.dot_general(
                staged[:, part],
                w_qkv[rows, part],
                (((1,), (1,)), ((), ())),
                preferred_element_type=f32,
            )
            if c == 0:
                sums[head] = piece
            else:
                sums[head] += piece

    def build_spread():
        conv_load.wait()
        spread[...] = jnp.zeros_like(spread)
        for n, (u, dy, dz) in enumerate(SHIFTS):
            for a, e, row_out, col_out in QUARTERS:
                v, w = 2 * dy + a - row_out + 1, 2 * dz + e - col_out + 1
                if 0 <= v < 3 and 0 <= w < 3:
                    at = n * lanes + (2 * a + e) * LAT_CH
                    to = (2 * row_out + col_out) * conv.shape[2]
                    spread[at : at + LAT_CH, to : to + conv.shape[2]] = conv[9 * u + 3 * v + w]

    def fold(c):
        part = LOADS[c]
        scaled = emb[:, part].astype(f32) * (1.0 + mod_ref[1:2, part])
        staged[0:tokens, part] = scaled.astype(bf16)
        qkv_loads[c].wait()
        project(c, part)

    @pl.when(first)
    def _():
        for c in range(EARLY):
            fold(c)

    pl.semaphore_wait(barrier, len(others))

    def remote(source, target, send, recv, where):
        return pltpu.make_async_remote_copy(
            src_ref=source,
            dst_ref=target,
            send_sem=send,
            recv_sem=recv,
            device_id=where,
            device_id_type=MESH,
        )

    def lat_copy(k, slot):
        return remote(
            lat_ref, lat_all.at[slot], lat_send.at[k], lat_recv.at[slot], {"seq": peer(k)}
        )

    def first_copy(k, c, sender):
        part = PASSES[c]
        return remote(
            parts.at[block(peer(k)), part],
            got_first.at[sender, :, part],
            first_send.at[k, c],
            first_recv.at[sender, c],
            {"seq": peer(k), "segment": 1, "cfg": 1 - branch},
        )

    def pass_copy(k, c, sender):
        return remote(
            owned.at[:, PASSES[c]],
            x_second.at[block(sender), PASSES[c]],
            pass_send.at[k, c],
            pass_recv.at[sender, c],
            {"seq": peer(k), "cfg": 1 - branch},
        )

    def second_copy(k, c, sender):
        part = RETURNS[c]
        return remote(
            parts.at[block(peer(k)), part],
            got_second.at[sender, :, part],
            second_send.at[k, c],
            second_recv.at[sender, c],
            {"seq": peer(k), "cfg": 1 - branch},
        )

    def relay_copy(k, c):
        rows = block(peer(k))
        return remote(
            parts.at[rows, RETURNS[c]],
            relay.at[rows, RETURNS[c]],
            relay_send.at[k, c],
            relay_recv.at[k, c],
            {"segment": 1 - segment, "cfg": 1 - branch},
        )

    def onward_copy(k, c):
        part = RETURNS[c]
        return remote(
            relay.at[block(peer(k)), part],
            got_second.at[me, :, part],
            onward_send.at[k, c],
            second_recv.at[me, c],
            {"seq": peer(k), "segment": 1},
        )

    def pred_copy(index, k, a, b, slot, sender_branch):
        return remote(
            pred_all.at[slot, sender_branch],
            pred_all.at[slot, sender_branch],
            pred_send.at[index],
            pred_recv.at[slot, sender_branch],
            {"seq": peer(k), "segment": 1 - a, "cfg": lax.rem(branch + b, 2)},
        )

    for k in range(1, seq_count):
        lat_copy(k, me).start()
    plan(2)
    order_load.wait()
    slab_load.wait()
    stale_load.wait()
    row = lax.broadcasted_iota(jnp.int32, bias_ref.shape, 0)
    column = lax.broadcasted_iota(jnp.int32, bias_ref.shape, 1)
    query_patch = (row >> 3) & 1
    fresh = column < tokens
    key_patch = jnp.where(
        fresh, (column >> 3) & 1, jnp.where(column < tokens + tokens // MICRO, 0, 1)
    )
    early = query_patch == order_ref[0]
    same = query_patch == key_patch
    bias_fresh = jnp.where(same, 0.0, jnp.where(early, -1e30, 0.0))
    bias_stale = jnp.where(same, -1e30, jnp.where(early, 0.0, -1e30))
    bias_ref[...] = jnp.where(fresh, bias_fresh, bias_stale)

    def attend(projected):
        scores = []
        for head in range(group_heads):
            key_lanes = slice(head * HEAD_DIM, (head + 1) * HEAD_DIM)
            keys = jnp.concatenate(
                [projected[head][:, HEAD_DIM : 2 * HEAD_DIM], stale[:, key_lanes]], 0
            )
            scores.append(
                lax.dot_general(
                    projected[head][:, :HEAD_DIM],
                    keys,
                    (((1,), (1,)), ((), ())),
                    preferred_element_type=f32,
                )
            )
        scores = jnp.stack(scores) * HEAD_DIM ** (-0.5) + bias_ref[...][None]
        weights = jnp.exp(scores - jnp.max(scores, axis=-1, keepdims=True))
        probs = (weights / jnp.sum(weights, axis=-1, keepdims=True)).astype(bf16)
        for head in range(group_heads):
            key_lanes = slice(head * HEAD_DIM, (head + 1) * HEAD_DIM)
            value_lanes = slice(
                (group_heads + head) * HEAD_DIM, (group_heads + head + 1) * HEAD_DIM
            )
            values = jnp.concatenate(
                [projected[head][:, 2 * HEAD_DIM :], stale[:, value_lanes]], 0
            )
            attended[:, key_lanes] = jnp.dot(
                probs[head], values, preferred_element_type=f32
            ).astype(bf16)

    def mix(part):
        mixed = jnp.dot(attended[...], w_out[:, part], preferred_element_type=f32)
        parts[:, part] = (mixed * mod_ref[2:3, part]).astype(bf16)

    @pl.when(first)
    def _():
        for c in range(EARLY, len(LOADS)):
            fold(c)
        for head in range(group_heads):
            whole = sums[head, 0:lanes]
            upper = whole.astype(bf16)
            folded[head, 0:lanes] = upper
            folded[head, lanes : 2 * lanes] = (whole - upper.astype(f32)).astype(bf16)
        for k in range(1, seq_count):
            lat_copy(k, peer(k)).wait_recv()
        once = lat_all[...].reshape(tokens, lanes).astype(bf16)
        square = jnp.zeros((tokens, 1), f32)
        for part in LOADS:
            wide = jnp.dot(once, emb[:, part], preferred_element_type=f32)
            wide = wide.astype(bf16).astype(f32)
            square = square + jnp.sum(wide * wide, axis=-1, keepdims=True)
        inverse = lax.rsqrt(square / D + norm_eps)
        twice = jnp.concatenate([once, once], 1)
        projected = []
        for head in range(group_heads):
            product = jnp.dot(twice, folded[head], preferred_element_type=f32)
            product = product * inverse + sums[head, tokens : tokens + 1]
            projected.append(product.astype(bf16))
        attend(projected)
        out_load.wait()
        for c, part in enumerate(PASSES):
            mix(part)
            for k in range(seq_count):
                first_copy(k, c, me).start()
        fin_load.wait()
        build_spread()
        for c in range(len(PASSES)):
            for k in range(seq_count):
                first_copy(k, c, me).wait_send()
        for c in range(RELAYED):
            for k in range(1, seq_count):
                relay_copy(k, c).wait_recv()
                onward_copy(k, c).start()
        for k in range(seq_count):
            for b in range(2):
                slot, sender_branch = peer(k), lax.rem(branch + b, 2)
                pred_copy(0, 0, 0, 0, slot, sender_branch).wait_recv()
        for c in range(RELAYED):
            for k in range(1, seq_count):
                onward_copy(k, c).wait_send()

    @pl.when(second)
    def _():
        own_latent = lat_ref[...].reshape(ROWS, lanes).astype(bf16)
        for part in LOADS:
            x_own[:, part] = jnp.dot(
                own_latent, emb[:, part], preferred_element_type=f32
            ).astype(bf16)
        for copy in qkv_loads:
            copy.wait()
        build_spread()
        for k in range(1, seq_count):
            lat_copy(k, peer(k)).wait_recv()
        fin_load.wait()
        out_load.wait()
        for c, part in enumerate(PASSES):
            total = x_own[:, part].astype(f32)
            for s in range(seq_count):
                first_copy(0, c, s).wait_recv()
                total = total + got_first[s, :, part].astype(f32)
            owned[:, part] = total.astype(bf16)
            for k in (2, 1, 3, 0):
                pass_copy(k, c, me).start()
        square = jnp.zeros((tokens, 1), f32)
        for c, part in enumerate(PASSES):
            for k in range(seq_count):
                pass_copy(k, c, peer(k)).wait_recv()
            wide = x_second[:, part].astype(f32)
            square = square + jnp.sum(wide * wide, axis=-1, keepdims=True)
            staged[0:tokens, part] = (wide * (1.0 + mod_ref[1:2, part])).astype(bf16)
            project(c, part)
        inverse = lax.rsqrt(square / D + norm_eps)
        projected = [
            (sums[head, 0:tokens] * inverse + sums[head, tokens : tokens + 1]).astype(bf16)
            for head in range(group_heads)
        ]
        attend(projected)
        for c, part in enumerate(RETURNS):
            mix(part)
            for k in (2, 1, 3, 0):
                (relay_copy(k, c) if k and c < RELAYED else second_copy(k, c, me)).start()
        predicted = jnp.zeros((ROWS, lanes), f32)
        square = jnp.zeros((ROWS, 1), f32)
        for c in [*range(RELAYED, len(RETURNS)), *range(RELAYED)]:
            part = RETURNS[c]
            total = owned[:, part].astype(f32)
            for k in range(seq_count):
                second_copy(k, c, peer(k)).wait_recv()
                total = total + got_second[peer(k), :, part].astype(f32)
            rounded = total.astype(bf16)
            wide = rounded.astype(f32)
            square = square + jnp.sum(wide * wide, axis=-1, keepdims=True)
            predicted = predicted + lax.dot_general(
                rounded, fin[:, part], (((1,), (1,)), ((), ())), preferred_element_type=f32
            )
        predicted = predicted * lax.rsqrt(square / D + norm_eps)
        pred_all[me, 1 - branch] = jnp.concatenate([predicted[:TOK_DEV], predicted[TOK_DEV:]], 1)
        targets = sorted(others, key=lambda t: (t[0] == 0, t[1] == 0, t[0] != 2))
        for index, (k, a, b) in enumerate(targets):
            pred_copy(index, k, a, b, me, 1 - branch).start()
        for c in range(len(PASSES)):
            for k in range(seq_count):
                pass_copy(k, c, me).wait_send()
        for c in range(len(RETURNS)):
            for k in range(seq_count):
                (relay_copy(k, c) if k and c < RELAYED else second_copy(k, c, me)).wait_send()
        for k in range(seq_count):
            for b in range(2):
                if k + b:
                    slot, sender_branch = peer(k), lax.rem(1 - branch + b, 2)
                    pred_copy(0, 0, 0, 0, slot, sender_branch).wait_recv()
        for index, (k, a, b) in enumerate(targets):
            pred_copy(index, k, a, b, me, 1 - branch).wait_send()

    def guided(slot):
        return (1.0 - guide_scale) * pred_all[slot, 0] + guide_scale * pred_all[slot, 1]

    velocity = guided(me)
    for p in range(MICRO):
        vel_ref[p] = velocity[:, p * lanes : (p + 1) * lanes]
    steps = [guided(s) / SCHED_STEPS for s in range(seq_count)]
    image = [
        lat_all[s, p] - steps[s][:, p * lanes : (p + 1) * lanes]
        for p in range(MICRO)
        for s in range(seq_count)
    ]
    image = jnp.concatenate(image, 0)
    image = image.astype(bf16).astype(f32)
    rows_deep = tokens // (FRAMES * (LAT_W // 2))
    frame = tokens // FRAMES
    place = lax.broadcasted_iota(jnp.int32, image.shape, 0)
    across = place & (LAT_W // 2 - 1)
    down = (place >> 2) & (rows_deep - 1)
    moved = {}
    for dy in (-1, 0, 1):
        for dz in (-1, 0, 1):
            by = dy * (LAT_W // 2) + dz
            shifted = pltpu.roll(image, (-by) % tokens, 0) if by else image
            if dz == 1:
                shifted = jnp.where(across < LAT_W // 2 - 1, shifted, 0.0)
            if dz == -1:
                shifted = jnp.where(across > 0, shifted, 0.0)
            if dy == 1:
                shifted = jnp.where(down < rows_deep - 1, shifted, 0.0)
            if dy == -1:
                shifted = jnp.where(down > 0, shifted, 0.0)
            moved[dy, dz] = shifted

    def tap(n):
        if n == len(SHIFTS):
            return jnp.zeros_like(image)
        u, dy, dz = SHIFTS[n]
        order = [max(f + u - 2, 0) for f in range(FRAMES)]
        return jnp.concatenate(
            [moved[dy, dz][f * frame : (f + 1) * frame] for f in order], 0
        )

    for pair in range((len(SHIFTS) + 1) // 2):
        both = jnp.concatenate([tap(2 * pair), tap(2 * pair + 1)], 1)
        taps[:, pair * 2 * lanes : (pair + 1) * 2 * lanes] = both.astype(bf16)
    channels = conv.shape[2]
    features = jnp.dot(taps[...], spread[...], preferred_element_type=f32)
    for a in range(2):
        for e in range(2):
            at = (2 * a + e) * channels
            feature[a, pl.ds(e, tokens, stride=2), :] = features[:, at : at + channels]
    start = jnp.int32(0)
    count = jnp.int32(0)
    for s in range(seq_count):
        start = start + jnp.where(s < me, slab_ref[s], 0)
        count = count + jnp.where(s == me, slab_ref[s], 0)
    for k in range(dec_ref.shape[2]):
        keep = [
            jnp.where((start + k == y) & (k < count), 1.0, 0.0) for y in range(2 * rows_deep)
        ]
        for f in range(FRAMES):
            total = jnp.zeros((LAT_W, channels), f32)
            for y in range(2 * rows_deep):
                at = (f * rows_deep + y // 2) * LAT_W
                total = total + keep[y] * feature[y % 2, at : at + LAT_W]
            dec_ref[0, f, k] = total.astype(bf16)

    for k in range(1, seq_count):
        lat_copy(k, me).wait_send()


def handed_over(velocity_in, decoded_in, velocity_out, decoded_out):
    velocity_out[...] = velocity_in[...]
    decoded_out[...] = decoded_in[...]


def shards_fused(
    latent,
    w_embed,
    w_qkv,
    w_out,
    mod_table,
    cond_mod,
    stale_kv,
    w_final,
    w_conv,
    patch_order,
    timestep,
    slab_rows,
):
    seq_count = lax.axis_size("seq")
    group_heads = HEADS // seq_count
    tokens = seq_count * ROWS
    lanes = latent.shape[-1]
    spreads = (len(SHIFTS) + 1) * lanes
    slab_most = 2 * 2 * tokens // (FRAMES * (LAT_W // 2)) // seq_count
    channels = w_conv.shape[2]
    bf16, f32, dma = jnp.bfloat16, jnp.float32, pltpu.SemaphoreType.DMA
    here = pl.BlockSpec(memory_space=pltpu.VMEM)
    away = pl.BlockSpec(memory_space=pl.ANY)
    velocity, decoded = pl.pallas_call(
        functools.partial(fused_kernel, seq_count, group_heads),
        out_shape=(
            jax.ShapeDtypeStruct(latent.shape, f32),
            jax.ShapeDtypeStruct((1, FRAMES, slab_most, LAT_W, channels), bf16),
        ),
        in_specs=[away] * 12,
        out_specs=(here, here),
        scratch_shapes=[
            pltpu.VMEM(latent.shape, f32),
            pltpu.SMEM(patch_order.shape, jnp.int32),
            pltpu.SMEM(slab_rows.shape, jnp.int32),
            pltpu.SMEM(timestep.shape, jnp.int32),
            pltpu.VMEM((3 * D // 128, 128), f32),
            pltpu.VMEM((3, SCHED_STEPS, D), bf16),
            pltpu.VMEM(w_conv.shape, bf16),
            pltpu.VMEM((spreads, 4 * channels), bf16),
            pltpu.VMEM((tokens, spreads), bf16),
            pltpu.VMEM((2, 2 * tokens, channels), f32),
            pltpu.VMEM((lanes, D), bf16),
            pltpu.VMEM((3 * group_heads * HEAD_DIM, D), bf16),
            pltpu.VMEM((group_heads * HEAD_DIM, D), bf16),
            pltpu.VMEM((tokens, 2 * group_heads * HEAD_DIM), bf16),
            pltpu.VMEM((lanes, D), bf16),
            pltpu.VMEM((8, D), f32),
            pltpu.VMEM((tokens, 2 * tokens), f32),
            pltpu.VMEM((seq_count,) + latent.shape, f32),
            pltpu.VMEM((tokens + 16, D), bf16),
            pltpu.VMEM((group_heads, tokens + 16, 3 * HEAD_DIM), f32),
            pltpu.VMEM((group_heads, 2 * lanes, 3 * HEAD_DIM), bf16),
            pltpu.VMEM((tokens, group_heads * HEAD_DIM), bf16),
            pltpu.VMEM((tokens, D), bf16),
            pltpu.VMEM((seq_count, ROWS, D), bf16),
            pltpu.VMEM((seq_count, ROWS, D), bf16),
            pltpu.VMEM((tokens, RETURNS[RELAYED].start), bf16),
            pltpu.VMEM((ROWS, D), bf16),
            pltpu.VMEM((ROWS, D), bf16),
            pltpu.VMEM((tokens, D), bf16),
            pltpu.VMEM((seq_count, 2, TOK_DEV, 2 * lanes), f32),
            dma((11,)),
            dma((len(LOADS),)),
            dma((seq_count,)),
            dma((seq_count,)),
            dma((seq_count, len(PASSES))),
            dma((seq_count, len(PASSES))),
            dma((seq_count, len(PASSES))),
            dma((seq_count, len(PASSES))),
            dma((seq_count, len(RETURNS))),
            dma((seq_count, len(RETURNS))),
            dma((seq_count, RELAYED)),
            dma((seq_count, RELAYED)),
            dma((seq_count, RELAYED)),
            dma((4 * seq_count - 1,)),
            dma((seq_count, 2)),
        ],
        compiler_params=pltpu.CompilerParams(
            collective_id=0, has_side_effects=True, vmem_limit_bytes=60 * 2**20
        ),
        name="denoise",
    )(
        latent,
        patch_order,
        slab_rows,
        timestep,
        cond_mod.reshape(3 * D // 128, 128),
        jnp.transpose(mod_table, (1, 0, 2)),
        w_conv,
        w_embed,
        w_qkv[0],
        w_out[0],
        stale_kv.reshape(tokens, 2 * group_heads * HEAD_DIM),
        w_final.T,
    )
    return pl.pallas_call(
        handed_over,
        out_shape=(
            jax.ShapeDtypeStruct(velocity.shape, f32),
            jax.ShapeDtypeStruct(decoded.shape, bf16),
        ),
        in_specs=[here, here],
        out_specs=(here, here),
        name="results",
    )(velocity, decoded)


def solution(mesh):
    in_specs = (
        P(None, ("groups", "seq"), None),
        P(),
        P("segment", "seq", None),
        P("segment", "seq", None),
        P(),
        P("cfg", ("groups", "segment"), None, None),
        P("segment", "cfg", "seq", None, "groups", None),
        P(),
        P(None, None, ("segment", "cfg")),
        P("groups"),
        P("groups"),
        P("groups"),
    )
    out_specs = (
        P(None, ("groups", "seq"), None),
        P(("groups", "seq"), None, None, None, ("segment", "cfg")),
    )
    small = mesh.shape["seq"] == 4 and mesh.shape["segment"] == 2 and mesh.shape["cfg"] == 2
    shards = shards_fused if small else shards_general
    return jax.shard_map(shards, mesh=mesh, in_specs=in_specs, out_specs=out_specs, check_vma=False)
```

```python
import functools

import jax
import jax.numpy as jnp
from jax import lax
from jax.experimental import pallas as pl
from jax.experimental.pallas import tpu as pltpu
from jax.sharding import PartitionSpec as P

HEADS = 24
HEAD_DIM = 128
D = 3072
LAT_CH = 16
SCHED_STEPS = 50
MICRO = 2
TOK_DEV = 8
FRAMES = 4
LAT_W = 8


guide_scale = 5.0
norm_eps = 1e-06


def swapped(value, axis, bit):
    return lax.ppermute(value, axis, [(i, i ^ 1 << bit) for i in range(lax.axis_size(axis))])


def passed_along(value, axis, by):
    size = lax.axis_size(axis)
    pairs = [(i, i + by) for i in range(size) if 0 <= i + by < size]
    return lax.ppermute(value, axis, pairs)


def rms_scaled(values):
    wide = values.astype(jnp.float32)
    return wide * lax.rsqrt(jnp.mean(wide * wide, axis=-1, keepdims=True) + norm_eps)


def cycle_join(piece, seq_index, cycle_bits):
    joined = piece
    for bit_number in range(cycle_bits):
        partner = swapped(joined, "seq", bit_number)
        upper_half = (seq_index // 2**bit_number % 2).astype(jnp.int32)
        part_rows = joined.shape[0]
        combined = jnp.zeros((2 * part_rows,) + joined.shape[1:], joined.dtype)
        combined = lax.dynamic_update_slice_in_dim(combined, joined, upper_half * part_rows, 0)
        joined = lax.dynamic_update_slice_in_dim(combined, partner, (1 - upper_half) * part_rows, 0)
    return joined


def decode(stepped, w_conv, slab_rows):
    seq_count = lax.axis_size("seq")
    seq_index = lax.axis_index("seq")
    token_rows = MICRO * seq_count * TOK_DEV // (FRAMES * (LAT_W // 2))
    image_rows = 2 * token_rows
    slab_most = 2 * image_rows // seq_count
    image = stepped.reshape(FRAMES, token_rows, LAT_W // 2, 2, 2, LAT_CH)
    image = (
        jnp.transpose(image, (0, 1, 3, 2, 4, 5))
        .reshape(FRAMES, image_rows, LAT_W, LAT_CH)
        .astype(jnp.bfloat16)
    )
    padded = jnp.concatenate([image[:1], image[:1], image], 0)
    padded = jnp.pad(padded, ((0, 0), (1, 1 + slab_most), (1, 1), (0, 0)))
    positions = jnp.arange(seq_count)
    slab_count = jnp.sum(jnp.where(positions == seq_index, slab_rows, 0))
    slab_start = jnp.sum(jnp.where(positions < seq_index, slab_rows, 0))
    window = lax.dynamic_slice_in_dim(padded, slab_start, slab_most + 2, 1)
    pieces = []
    for frame_shift in range(3):
        for row_shift in range(3):
            for col_shift in range(3):
                pieces.append(
                    window[
                        frame_shift : frame_shift + FRAMES,
                        row_shift : row_shift + slab_most,
                        col_shift : col_shift + LAT_W,
                    ]
                )
    columns = jnp.concatenate(pieces, -1).reshape(FRAMES * slab_most * LAT_W, 27 * LAT_CH)
    kernel = w_conv.reshape(27 * LAT_CH, w_conv.shape[2])
    features = jnp.dot(columns, kernel, preferred_element_type=jnp.float32).astype(jnp.bfloat16)
    features = features.reshape(FRAMES, slab_most, LAT_W, w_conv.shape[2])
    row_valid = jnp.arange(slab_most)[None, :, None, None] < slab_count
    decoded = jnp.where(row_valid, features, jnp.zeros_like(features))
    return decoded[None]


def shards_general(
    latent,
    w_embed,
    w_qkv,
    w_out,
    mod_table,
    cond_mod,
    stale_kv,
    w_final,
    w_conv,
    patch_order,
    timestep,
    slab_rows,
):
    seq_count = lax.axis_size("seq")
    segment_count = lax.axis_size("segment")
    seq_index = lax.axis_index("seq")
    segment_index = lax.axis_index("segment")
    branch_index = lax.axis_index("cfg")
    group_count = min(seq_count, 8)
    cycle_size = seq_count // group_count
    cycle_bits = cycle_size.bit_length() - 1
    group_heads = HEADS // group_count
    sub_rows = TOK_DEV // cycle_size
    share_rows = seq_count * sub_rows
    kv_lanes = 2 * group_heads * HEAD_DIM
    table_row = lax.dynamic_index_in_dim(mod_table, timestep[0], 0, keepdims=False).astype(
        jnp.float32
    )
    modulation = table_row + cond_mod[0, 0]
    shift_row = modulation[0]
    scale_row = modulation[1]
    gate_row = modulation[2]
    joined_weights = (
        cycle_join(w_qkv[0], seq_index, cycle_bits),
        cycle_join(w_out[0], seq_index, cycle_bits),
    )
    stale_joined = cycle_join(stale_kv[0, 0], seq_index, cycle_bits)
    cache = jnp.transpose(stale_joined, (1, 0, 2, 3)).reshape(
        MICRO, cycle_size * share_rows, kv_lanes
    )
    received = jnp.zeros((TOK_DEV, D), jnp.bfloat16)
    finished = jnp.zeros((MICRO, TOK_DEV, D), jnp.bfloat16)
    slot_ids = jnp.arange(MICRO)
    tick_count = MICRO + segment_count - 1
    for tick_index in range(tick_count):
        qkv_rows, out_rows = joined_weights
        micro_index = tick_index - segment_index
        active = (micro_index >= 0) & (micro_index < MICRO)
        clipped = jnp.clip(micro_index, 0, MICRO - 1)
        patch_id = jnp.sum(jnp.where(slot_ids == clipped, patch_order, 0))
        own_latent = lax.dynamic_index_in_dim(latent, patch_id, 0, keepdims=False).astype(
            jnp.bfloat16
        )
        embedded = jnp.dot(own_latent, w_embed, preferred_element_type=jnp.float32).astype(
            jnp.bfloat16
        )
        layer_input = jnp.where(segment_index == 0, embedded, received)
        normed = (rms_scaled(layer_input) * (1.0 + scale_row) + shift_row).astype(jnp.bfloat16)
        outgoing = jnp.broadcast_to(
            normed.reshape(1, cycle_size, sub_rows, D), (group_count, cycle_size, sub_rows, D)
        )
        shared = lax.all_to_all(
            outgoing.reshape(share_rows, D), "seq", split_axis=0, concat_axis=0, tiled=True
        )
        projected = lax.dot_general(
            shared, qkv_rows, (((1,), (1,)), ((), ())), preferred_element_type=jnp.float32
        )
        projected = projected.astype(jnp.bfloat16).reshape(share_rows, group_heads, 3, HEAD_DIM)
        queries = projected[:, :, 0]
        fresh_local = jnp.transpose(projected[:, :, 1:], (0, 2, 1, 3)).reshape(
            1, share_rows, kv_lanes
        )
        fresh = cycle_join(fresh_local, seq_index, cycle_bits).reshape(
            cycle_size * share_rows, kv_lanes
        )
        previous = lax.dynamic_index_in_dim(cache, patch_id, 0, keepdims=False)
        cache = lax.dynamic_update_index_in_dim(
            cache, jnp.where(active, fresh, previous), patch_id, 0
        )
        keyvals = cache.reshape(MICRO * cycle_size * share_rows, 2, group_heads, HEAD_DIM)
        scores = jnp.einsum(
            "shd,khd->hsk", queries, keyvals[:, 0], preferred_element_type=jnp.float32
        ) * HEAD_DIM ** (-0.5)
        probs = jax.nn.softmax(scores, axis=-1).astype(jnp.bfloat16)
        attended = jnp.einsum(
            "hsk,khd->shd", probs, keyvals[:, 1], preferred_element_type=jnp.float32
        ).astype(jnp.bfloat16)
        partial_out = jnp.dot(
            attended.reshape(share_rows, group_heads * HEAD_DIM),
            out_rows,
            preferred_element_type=jnp.float32,
        )
        returned = lax.all_to_all(
            partial_out.astype(jnp.bfloat16), "seq", split_axis=0, concat_axis=0, tiled=True
        ).astype(partial_out.dtype)
        mixed = jnp.sum(returned.reshape(group_count, cycle_size, sub_rows, D), axis=0).reshape(
            TOK_DEV, D
        )
        layer_output = (layer_input.astype(jnp.float32) + gate_row * mixed).astype(jnp.bfloat16)
        keep_final = active & (segment_index == segment_count - 1)
        earlier = lax.dynamic_index_in_dim(finished, patch_id, 0, keepdims=False)
        finished = lax.dynamic_update_index_in_dim(
            finished, jnp.where(keep_final, layer_output, earlier), patch_id, 0
        )
        if tick_index + 1 < tick_count:
            received = passed_along(layer_output, "segment", 1)
    final_normed = rms_scaled(finished).astype(jnp.bfloat16)
    predicted = jnp.einsum("mtd,dc->mtc", final_normed, w_final, preferred_element_type=jnp.float32)
    is_last = segment_index == segment_count - 1
    branch_weight = jnp.where(branch_index == 0, 1.0 - guide_scale, guide_scale)
    velocity_term = jnp.where(is_last, branch_weight * predicted, 0.0)
    latent_term = jnp.where(is_last & (branch_index == 0), latent, 0.0)
    velocity_own, latent_own = lax.psum((velocity_term, latent_term), ("segment", "cfg"))
    velocity_full, latent_full = (
        lax.all_gather(velocity_own, "seq", axis=1, tiled=True),
        lax.all_gather(latent_own, "seq", axis=1, tiled=True),
    )
    stepped = latent_full - velocity_full / SCHED_STEPS
    return (velocity_own, decode(stepped, w_conv, slab_rows))


ROWS = MICRO * TOK_DEV
SHIFTS = [(u, dy, dz) for u in range(3) for dy in (-1, 0, 1) for dz in (-1, 0, 1)]
QUARTERS = [
    (a, e, row, col) for a in range(2) for e in range(2) for row in range(2) for col in range(2)
]
MESH = pl.DeviceIdType.MESH


def cuts(*widths):
    edges = [sum(widths[:i]) for i in range(len(widths) + 1)]
    return [slice(a, b) for a, b in zip(edges[:-1], edges[1:])]


LOADS = cuts(512, 512, 512, 512, 512, 512)
PASSES = cuts(512, 512, 512, 512, 512, 512)
RETURNS = cuts(768, 512, 512, 512, 512, 256)
EARLY = 4
RELAYED = 1


def fused_kernel(
    seq_count,
    group_heads,
    lat_hbm,
    order_hbm,
    slab_hbm,
    step_hbm,
    cond_hbm,
    table_hbm,
    conv_hbm,
    emb_hbm,
    qkv_hbm,
    out_hbm,
    stale_hbm,
    fin_hbm,
    vel_ref,
    dec_ref,
    lat_ref,
    order_ref,
    slab_ref,
    step_index,
    cond_ref,
    table,
    conv,
    spread,
    taps,
    feature,
    emb,
    w_qkv,
    w_out,
    stale,
    fin,
    mod_ref,
    bias_ref,
    lat_all,
    staged,
    sums,
    folded,
    attended,
    parts,
    got_first,
    got_second,
    relay,
    owned,
    x_own,
    x_second,
    pred_all,
    load_sem,
    qkv_sem,
    lat_send,
    lat_recv,
    first_send,
    first_recv,
    pass_send,
    pass_recv,
    second_send,
    second_recv,
    relay_send,
    relay_recv,
    onward_send,
    pred_send,
    pred_recv,
):
    me = lax.axis_index("seq")
    segment = lax.axis_index("segment")
    branch = lax.axis_index("cfg")
    head_rows = 3 * HEAD_DIM
    tokens = seq_count * ROWS
    lanes = lat_ref.shape[-1]
    first = segment == 0
    second = segment == 1
    bf16, f32 = jnp.bfloat16, jnp.float32

    def peer(step):
        return lax.rem(me + step, seq_count)

    def block(index):
        return pl.ds(pl.multiple_of(index * ROWS, ROWS), ROWS)

    barrier = pltpu.get_barrier_semaphore()
    others = [
        (k, a, b) for k in range(seq_count) for a in range(2) for b in range(2) if k + a + b
    ]
    for k, a, b in sorted(others, key=lambda t: (t[0] == 0, t[0] != 2, t[1] == 0)):
        where = {
            "seq": peer(k),
            "segment": lax.rem(segment + a, 2),
            "cfg": lax.rem(branch + b, 2),
        }
        pl.semaphore_signal(barrier, inc=1, device_id=where, device_id_type=MESH)

    def load(i, source, target):
        return pltpu.make_async_copy(source, target, load_sem.at[i])

    emb_load = load(0, emb_hbm, emb)
    table_load = load(1, table_hbm, table)
    conv_load = load(2, conv_hbm, conv)
    stale_load = load(3, stale_hbm, stale)
    out_load = load(4, out_hbm, w_out)
    fin_load = load(5, fin_hbm, fin)
    qkv_loads = [
        pltpu.make_async_copy(qkv_hbm.at[:, part], w_qkv.at[:, part], qkv_sem.at[c])
        for c, part in enumerate(LOADS)
    ]
    lat_load = load(6, lat_hbm, lat_ref)
    order_load = load(7, order_hbm, order_ref)
    slab_load = load(8, slab_hbm, slab_ref)
    step_load = load(9, step_hbm, step_index)
    cond_load = load(10, cond_hbm, cond_ref)
    lat_load.start()
    step_load.start()
    cond_load.start()
    table_load.start()
    emb_load.start()
    order_load.start()
    slab_load.start()
    for copy in qkv_loads:
        copy.start()
    conv_load.start()
    stale_load.start()
    out_load.start()
    fin_load.start()

    step_load.wait()
    cond_load.wait()
    table_load.wait()
    plan_row = lax.broadcasted_iota(jnp.int32, table.shape[1:], 0) == step_index[0]
    pieces = D // 128

    def plan(i):
        chosen = jnp.where(plan_row, table[i].astype(f32), 0.0)
        mod_ref[i : i + 1] = jnp.sum(chosen, axis=0, keepdims=True)
        for j in range(pieces):
            at = slice(j * 128, (j + 1) * 128)
            mod_ref[i : i + 1, at] += cond_ref[i * pieces + j : i * pieces + j + 1]

    plan(0)
    plan(1)
    staged[tokens:] = jnp.broadcast_to(mod_ref[0:1], (16, D)).astype(bf16)
    lat_load.wait()
    lat_all[me] = lat_ref[...]
    emb_load.wait()

    def project(c, part):
        for head in range(group_heads):
            rows = slice(head * head_rows, (head + 1) * head_rows)
            piece = lax.dot_general(
                staged[:, part],
                w_qkv[rows, part],
                (((1,), (1,)), ((), ())),
                preferred_element_type=f32,
            )
            if c == 0:
                sums[head] = piece
            else:
                sums[head] += piece

    def build_spread():
        conv_load.wait()
        spread[...] = jnp.zeros_like(spread)
        for n, (u, dy, dz) in enumerate(SHIFTS):
            for a, e, row_out, col_out in QUARTERS:
                v, w = 2 * dy + a - row_out + 1, 2 * dz + e - col_out + 1
                if 0 <= v < 3 and 0 <= w < 3:
                    at = n * lanes + (2 * a + e) * LAT_CH
                    to = (2 * row_out + col_out) * conv.shape[2]
                    spread[at : at + LAT_CH, to : to + conv.shape[2]] = conv[9 * u + 3 * v + w]

    def fold(c):
        part = LOADS[c]
        scaled = emb[:, part].astype(f32) * (1.0 + mod_ref[1:2, part])
        staged[0:tokens, part] = scaled.astype(bf16)
        qkv_loads[c].wait()
        project(c, part)

    @pl.when(first)
    def _():
        for c in range(EARLY):
            fold(c)

    pl.semaphore_wait(barrier, len(others))

    def remote(source, target, send, recv, where):
        return pltpu.make_async_remote_copy(
            src_ref=source,
            dst_ref=target,
            send_sem=send,
            recv_sem=recv,
            device_id=where,
            device_id_type=MESH,
        )

    def lat_copy(k, slot):
        return remote(
            lat_ref, lat_all.at[slot], lat_send.at[k], lat_recv.at[slot], {"seq": peer(k)}
        )

    def first_copy(k, c, sender):
        part = PASSES[c]
        return remote(
            parts.at[block(peer(k)), part],
            got_first.at[sender, :, part],
            first_send.at[k, c],
            first_recv.at[sender, c],
            {"seq": peer(k), "segment": 1, "cfg": 1 - branch},
        )

    def pass_copy(k, c, sender):
        return remote(
            owned.at[:, PASSES[c]],
            x_second.at[block(sender), PASSES[c]],
            pass_send.at[k, c],
            pass_recv.at[sender, c],
            {"seq": peer(k), "cfg": 1 - branch},
        )

    def second_copy(k, c, sender):
        part = RETURNS[c]
        return remote(
            parts.at[block(peer(k)), part],
            got_second.at[sender, :, part],
            second_send.at[k, c],
            second_recv.at[sender, c],
            {"seq": peer(k), "cfg": 1 - branch},
        )

    def relay_copy(k, c):
        rows = block(peer(k))
        return remote(
            parts.at[rows, RETURNS[c]],
            relay.at[rows, RETURNS[c]],
            relay_send.at[k, c],
            relay_recv.at[k, c],
            {"segment": 1 - segment, "cfg": 1 - branch},
        )

    def onward_copy(k, c):
        part = RETURNS[c]
        return remote(
            relay.at[block(peer(k)), part],
            got_second.at[me, :, part],
            onward_send.at[k, c],
            second_recv.at[me, c],
            {"seq": peer(k), "segment": 1},
        )

    def pred_copy(index, k, a, b, slot, sender_branch):
        return remote(
            pred_all.at[slot, sender_branch],
            pred_all.at[slot, sender_branch],
            pred_send.at[index],
            pred_recv.at[slot, sender_branch],
            {"seq": peer(k), "segment": 1 - a, "cfg": lax.rem(branch + b, 2)},
        )

    for k in range(1, seq_count):
        lat_copy(k, me).start()
    plan(2)
    order_load.wait()
    slab_load.wait()
    stale_load.wait()
    row = lax.broadcasted_iota(jnp.int32, bias_ref.shape, 0)
    column = lax.broadcasted_iota(jnp.int32, bias_ref.shape, 1)
    query_patch = (row >> 3) & 1
    fresh = column < tokens
    key_patch = jnp.where(
        fresh, (column >> 3) & 1, jnp.where(column < tokens + tokens // MICRO, 0, 1)
    )
    early = query_patch == order_ref[0]
    same = query_patch == key_patch
    bias_fresh = jnp.where(same, 0.0, jnp.where(early, -1e30, 0.0))
    bias_stale = jnp.where(same, -1e30, jnp.where(early, 0.0, -1e30))
    bias_ref[...] = jnp.where(fresh, bias_fresh, bias_stale)

    def attend(projected):
        scores = []
        for head in range(group_heads):
            key_lanes = slice(head * HEAD_DIM, (head + 1) * HEAD_DIM)
            keys = jnp.concatenate(
                [projected[head][:, HEAD_DIM : 2 * HEAD_DIM], stale[:, key_lanes]], 0
            )
            scores.append(
                lax.dot_general(
                    projected[head][:, :HEAD_DIM],
                    keys,
                    (((1,), (1,)), ((), ())),
                    preferred_element_type=f32,
                )
            )
        scores = jnp.stack(scores) * HEAD_DIM ** (-0.5) + bias_ref[...][None]
        weights = jnp.exp(scores - jnp.max(scores, axis=-1, keepdims=True))
        probs = (weights / jnp.sum(weights, axis=-1, keepdims=True)).astype(bf16)
        for head in range(group_heads):
            key_lanes = slice(head * HEAD_DIM, (head + 1) * HEAD_DIM)
            value_lanes = slice(
                (group_heads + head) * HEAD_DIM, (group_heads + head + 1) * HEAD_DIM
            )
            values = jnp.concatenate(
                [projected[head][:, 2 * HEAD_DIM :], stale[:, value_lanes]], 0
            )
            attended[:, key_lanes] = jnp.dot(
                probs[head], values, preferred_element_type=f32
            ).astype(bf16)

    def mix(part):
        mixed = jnp.dot(attended[...], w_out[:, part], preferred_element_type=f32)
        parts[:, part] = (mixed * mod_ref[2:3, part]).astype(bf16)

    @pl.when(first)
    def _():
        for c in range(EARLY, len(LOADS)):
            fold(c)
        for head in range(group_heads):
            whole = sums[head, 0:lanes]
            upper = whole.astype(bf16)
            folded[head, 0:lanes] = upper
            folded[head, lanes : 2 * lanes] = (whole - upper.astype(f32)).astype(bf16)
        for k in range(1, seq_count):
            lat_copy(k, peer(k)).wait_recv()
        once = lat_all[...].reshape(tokens, lanes).astype(bf16)
        square = jnp.zeros((tokens, 1), f32)
        for part in LOADS:
            wide = jnp.dot(once, emb[:, part], preferred_element_type=f32)
            wide = wide.astype(bf16).astype(f32)
            square = square + jnp.sum(wide * wide, axis=-1, keepdims=True)
        inverse = lax.rsqrt(square / D + norm_eps)
        twice = jnp.concatenate([once, once], 1)
        projected = []
        for head in range(group_heads):
            product = jnp.dot(twice, folded[head], preferred_element_type=f32)
            product = product * inverse + sums[head, tokens : tokens + 1]
            projected.append(product.astype(bf16))
        attend(projected)
        out_load.wait()
        for c, part in enumerate(PASSES):
            mix(part)
            for k in range(seq_count):
                first_copy(k, c, me).start()
        fin_load.wait()
        build_spread()
        for c in range(len(PASSES)):
            for k in range(seq_count):
                first_copy(k, c, me).wait_send()
        for c in range(RELAYED):
            for k in range(1, seq_count):
                relay_copy(k, c).wait_recv()
                onward_copy(k, c).start()
        for k in range(seq_count):
            for b in range(2):
                slot, sender_branch = peer(k), lax.rem(branch + b, 2)
                pred_copy(0, 0, 0, 0, slot, sender_branch).wait_recv()
        for c in range(RELAYED):
            for k in range(1, seq_count):
                onward_copy(k, c).wait_send()

    @pl.when(second)
    def _():
        own_latent = lat_ref[...].reshape(ROWS, lanes).astype(bf16)
        for part in LOADS:
            x_own[:, part] = jnp.dot(
                own_latent, emb[:, part], preferred_element_type=f32
            ).astype(bf16)
        for copy in qkv_loads:
            copy.wait()
        build_spread()
        for k in range(1, seq_count):
            lat_copy(k, peer(k)).wait_recv()
        fin_load.wait()
        out_load.wait()
        for c, part in enumerate(PASSES):
            total = x_own[:, part].astype(f32)
            for s in range(seq_count):
                first_copy(0, c, s).wait_recv()
                total = total + got_first[s, :, part].astype(f32)
            owned[:, part] = total.astype(bf16)
            for k in (2, 1, 3, 0):
                pass_copy(k, c, me).start()
        square = jnp.zeros((tokens, 1), f32)
        for c, part in enumerate(PASSES):
            for k in range(seq_count):
                pass_copy(k, c, peer(k)).wait_recv()
            wide = x_second[:, part].astype(f32)
            square = square + jnp.sum(wide * wide, axis=-1, keepdims=True)
            staged[0:tokens, part] = (wide * (1.0 + mod_ref[1:2, part])).astype(bf16)
            project(c, part)
        inverse = lax.rsqrt(square / D + norm_eps)
        projected = [
            (sums[head, 0:tokens] * inverse + sums[head, tokens : tokens + 1]).astype(bf16)
            for head in range(group_heads)
        ]
        attend(projected)
        for c, part in enumerate(RETURNS):
            mix(part)
            for k in (2, 1, 3, 0):
                (relay_copy(k, c) if k and c < RELAYED else second_copy(k, c, me)).start()
        predicted = jnp.zeros((ROWS, lanes), f32)
        square = jnp.zeros((ROWS, 1), f32)
        for c in [*range(RELAYED, len(RETURNS)), *range(RELAYED)]:
            part = RETURNS[c]
            total = owned[:, part].astype(f32)
            for k in range(seq_count):
                second_copy(k, c, peer(k)).wait_recv()
                total = total + got_second[peer(k), :, part].astype(f32)
            rounded = total.astype(bf16)
            wide = rounded.astype(f32)
            square = square + jnp.sum(wide * wide, axis=-1, keepdims=True)
            predicted = predicted + lax.dot_general(
                rounded, fin[:, part], (((1,), (1,)), ((), ())), preferred_element_type=f32
            )
        predicted = predicted * lax.rsqrt(square / D + norm_eps)
        pred_all[me, 1 - branch] = jnp.concatenate([predicted[:TOK_DEV], predicted[TOK_DEV:]], 1)
        targets = sorted(others, key=lambda t: (t[0] == 0, t[1] == 0, t[0] != 2))
        for index, (k, a, b) in enumerate(targets):
            pred_copy(index, k, a, b, me, 1 - branch).start()
        for c in range(len(PASSES)):
            for k in range(seq_count):
                pass_copy(k, c, me).wait_send()
        for c in range(len(RETURNS)):
            for k in range(seq_count):
                (relay_copy(k, c) if k and c < RELAYED else second_copy(k, c, me)).wait_send()
        for k in range(seq_count):
            for b in range(2):
                if k + b:
                    slot, sender_branch = peer(k), lax.rem(1 - branch + b, 2)
                    pred_copy(0, 0, 0, 0, slot, sender_branch).wait_recv()
        for index, (k, a, b) in enumerate(targets):
            pred_copy(index, k, a, b, me, 1 - branch).wait_send()

    def guided(slot):
        return (1.0 - guide_scale) * pred_all[slot, 0] + guide_scale * pred_all[slot, 1]

    velocity = guided(me)
    for p in range(MICRO):
        vel_ref[p] = velocity[:, p * lanes : (p + 1) * lanes]
    steps = [guided(s) / SCHED_STEPS for s in range(seq_count)]
    image = [
        lat_all[s, p] - steps[s][:, p * lanes : (p + 1) * lanes]
        for p in range(MICRO)
        for s in range(seq_count)
    ]
    image = jnp.concatenate(image, 0)
    image = image.astype(bf16).astype(f32)
    rows_deep = tokens // (FRAMES * (LAT_W // 2))
    frame = tokens // FRAMES
    place = lax.broadcasted_iota(jnp.int32, image.shape, 0)
    across = place & (LAT_W // 2 - 1)
    down = (place >> 2) & (rows_deep - 1)
    moved = {}
    for dy in (-1, 0, 1):
        for dz in (-1, 0, 1):
            by = dy * (LAT_W // 2) + dz
            shifted = pltpu.roll(image, (-by) % tokens, 0) if by else image
            if dz == 1:
                shifted = jnp.where(across < LAT_W // 2 - 1, shifted, 0.0)
            if dz == -1:
                shifted = jnp.where(across > 0, shifted, 0.0)
            if dy == 1:
                shifted = jnp.where(down < rows_deep - 1, shifted, 0.0)
            if dy == -1:
                shifted = jnp.where(down > 0, shifted, 0.0)
            moved[dy, dz] = shifted

    def tap(n):
        if n == len(SHIFTS):
            return jnp.zeros_like(image)
        u, dy, dz = SHIFTS[n]
        order = [max(f + u - 2, 0) for f in range(FRAMES)]
        return jnp.concatenate(
            [moved[dy, dz][f * frame : (f + 1) * frame] for f in order], 0
        )

    for pair in range((len(SHIFTS) + 1) // 2):
        both = jnp.concatenate([tap(2 * pair), tap(2 * pair + 1)], 1)
        taps[:, pair * 2 * lanes : (pair + 1) * 2 * lanes] = both.astype(bf16)
    channels = conv.shape[2]
    features = jnp.dot(taps[...], spread[...], preferred_element_type=f32)
    for a in range(2):
        for e in range(2):
            at = (2 * a + e) * channels
            feature[a, pl.ds(e, tokens, stride=2), :] = features[:, at : at + channels]
    start = jnp.int32(0)
    count = jnp.int32(0)
    for s in range(seq_count):
        start = start + jnp.where(s < me, slab_ref[s], 0)
        count = count + jnp.where(s == me, slab_ref[s], 0)
    for k in range(dec_ref.shape[2]):
        keep = [
            jnp.where((start + k == y) & (k < count), 1.0, 0.0) for y in range(2 * rows_deep)
        ]
        for f in range(FRAMES):
            total = jnp.zeros((LAT_W, channels), f32)
            for y in range(2 * rows_deep):
                at = (f * rows_deep + y // 2) * LAT_W
                total = total + keep[y] * feature[y % 2, at : at + LAT_W]
            dec_ref[0, f, k] = total.astype(bf16)

    for k in range(1, seq_count):
        lat_copy(k, me).wait_send()


def handed_over(velocity_in, decoded_in, velocity_out, decoded_out):
    velocity_out[...] = velocity_in[...]
    decoded_out[...] = decoded_in[...]


def shards_fused(
    latent,
    w_embed,
    w_qkv,
    w_out,
    mod_table,
    cond_mod,
    stale_kv,
    w_final,
    w_conv,
    patch_order,
    timestep,
    slab_rows,
):
    seq_count = lax.axis_size("seq")
    group_heads = HEADS // seq_count
    tokens = seq_count * ROWS
    lanes = latent.shape[-1]
    spreads = (len(SHIFTS) + 1) * lanes
    slab_most = 2 * 2 * tokens // (FRAMES * (LAT_W // 2)) // seq_count
    channels = w_conv.shape[2]
    bf16, f32, dma = jnp.bfloat16, jnp.float32, pltpu.SemaphoreType.DMA
    here = pl.BlockSpec(memory_space=pltpu.VMEM)
    away = pl.BlockSpec(memory_space=pl.ANY)
    velocity, decoded = pl.pallas_call(
        functools.partial(fused_kernel, seq_count, group_heads),
        out_shape=(
            jax.ShapeDtypeStruct(latent.shape, f32),
            jax.ShapeDtypeStruct((1, FRAMES, slab_most, LAT_W, channels), bf16),
        ),
        in_specs=[away] * 12,
        out_specs=(here, here),
        scratch_shapes=[
            pltpu.VMEM(latent.shape, f32),
            pltpu.SMEM(patch_order.shape, jnp.int32),
            pltpu.SMEM(slab_rows.shape, jnp.int32),
            pltpu.SMEM(timestep.shape, jnp.int32),
            pltpu.VMEM((3 * D // 128, 128), f32),
            pltpu.VMEM((3, SCHED_STEPS, D), bf16),
            pltpu.VMEM(w_conv.shape, bf16),
            pltpu.VMEM((spreads, 4 * channels), bf16),
            pltpu.VMEM((tokens, spreads), bf16),
            pltpu.VMEM((2, 2 * tokens, channels), f32),
            pltpu.VMEM((lanes, D), bf16),
            pltpu.VMEM((3 * group_heads * HEAD_DIM, D), bf16),
            pltpu.VMEM((group_heads * HEAD_DIM, D), bf16),
            pltpu.VMEM((tokens, 2 * group_heads * HEAD_DIM), bf16),
            pltpu.VMEM((lanes, D), bf16),
            pltpu.VMEM((8, D), f32),
            pltpu.VMEM((tokens, 2 * tokens), f32),
            pltpu.VMEM((seq_count,) + latent.shape, f32),
            pltpu.VMEM((tokens + 16, D), bf16),
            pltpu.VMEM((group_heads, tokens + 16, 3 * HEAD_DIM), f32),
            pltpu.VMEM((group_heads, 2 * lanes, 3 * HEAD_DIM), bf16),
            pltpu.VMEM((tokens, group_heads * HEAD_DIM), bf16),
            pltpu.VMEM((tokens, D), bf16),
            pltpu.VMEM((seq_count, ROWS, D), bf16),
            pltpu.VMEM((seq_count, ROWS, D), bf16),
            pltpu.VMEM((tokens, RETURNS[RELAYED].start), bf16),
            pltpu.VMEM((ROWS, D), bf16),
            pltpu.VMEM((ROWS, D), bf16),
            pltpu.VMEM((tokens, D), bf16),
            pltpu.VMEM((seq_count, 2, TOK_DEV, 2 * lanes), f32),
            dma((11,)),
            dma((len(LOADS),)),
            dma((seq_count,)),
            dma((seq_count,)),
            dma((seq_count, len(PASSES))),
            dma((seq_count, len(PASSES))),
            dma((seq_count, len(PASSES))),
            dma((seq_count, len(PASSES))),
            dma((seq_count, len(RETURNS))),
            dma((seq_count, len(RETURNS))),
            dma((seq_count, RELAYED)),
            dma((seq_count, RELAYED)),
            dma((seq_count, RELAYED)),
            dma((4 * seq_count - 1,)),
            dma((seq_count, 2)),
        ],
        compiler_params=pltpu.CompilerParams(
            collective_id=0, has_side_effects=True, vmem_limit_bytes=60 * 2**20
        ),
        name="denoise",
    )(
        latent,
        patch_order,
        slab_rows,
        timestep,
        cond_mod.reshape(3 * D // 128, 128),
        jnp.transpose(mod_table, (1, 0, 2)),
        w_conv,
        w_embed,
        w_qkv[0],
        w_out[0],
        stale_kv.reshape(tokens, 2 * group_heads * HEAD_DIM),
        w_final.T,
    )
    return pl.pallas_call(
        handed_over,
        out_shape=(
            jax.ShapeDtypeStruct(velocity.shape, f32),
            jax.ShapeDtypeStruct(decoded.shape, bf16),
        ),
        in_specs=[here, here],
        out_specs=(here, here),
        name="results",
    )(velocity, decoded)


def solution(mesh):
    in_specs = (
        P(None, ("groups", "seq"), None),
        P(),
        P("segment", "seq", None),
        P("segment", "seq", None),
        P(),
        P("cfg", ("groups", "segment"), None, None),
        P("segment", "cfg", "seq", None, "groups", None),
        P(),
        P(None, None, ("segment", "cfg")),
        P("groups"),
        P("groups"),
        P("groups"),
    )
    out_specs = (
        P(None, ("groups", "seq"), None),
        P(("groups", "seq"), None, None, None, ("segment", "cfg")),
    )
    small = mesh.shape["seq"] == 4 and mesh.shape["segment"] == 2 and mesh.shape["cfg"] == 2
    shards = shards_fused if small else shards_general
    return jax.shard_map(shards, mesh=mesh, in_specs=in_specs, out_specs=out_specs, check_vma=False)
```
